32 devices in a mesh: dp: 4 (over y, core), row: 4 (over z), col: 2 (over x).
Axes of the slice: x: 2, y: 2, z: 4, core: 2. Of those that a mesh axis runs over, the one named last changes fastest.
Arguments:
- tokens: bfloat16 [768, 4096], P('row', ('dp', 'col')), may hold values from -6 to 6
- segment_ids: int32 [16, 256], P(('dp', 'row')), may hold values from 0 to 7, never falling along the last dimension, each value on 1 to 96 neighbouring positions
- query_weight: bfloat16 [768, 768], P('row', 'col'), may hold values from -0.21875 to 0.21875
- key_weight: bfloat16 [768, 768], P('row', 'col'), may hold values from -0.21875 to 0.21875
- value_weight: bfloat16 [768, 768], P('row', 'col'), may hold values from -0.21875 to 0.21875
- query_bias: float32 [768], P('col'), may hold values from -3 to 3
- value_bias: float32 [768], P('col'), may hold values from -3 to 3
- out_weight: bfloat16 [768, 768], P('col', 'row'), may hold values from -0.875 to 0.875
- out_bias: float32 [768], P('row'), may hold values from -3 to 3
- attn_gain: float32 [768], P('row'), may hold values from 0.5 to 1.5
- attn_shift: float32 [768], P('row'), may hold values from -3 to 3
- up_weight: bfloat16 [768, 3072], P('row', 'col'), may hold values from -0.21875 to 0.21875
- up_bias: float32 [3072], P('col'), may hold values from -3 to 3
- down_weight: bfloat16 [3072, 768], P('col', 'row'), may hold values from -0.109375 to 0.109375
- down_bias: float32 [768], P('row'), may hold values from -3 to 3
- ffn_gain: float32 [768], P('row'), may hold values from 0.5 to 1.5
- ffn_shift: float32 [768], P('row'), may hold values from -3 to 3
- cotangent: bfloat16 [768, 4096], P('row', ('dp', 'col')), may hold values from -6 to 6
Outputs:
- output: bfloat16 [768, 4096], P('row', ('dp', 'col'))
- tokens_grad: float32 [768, 4096], P('row', ('dp', 'col'))
- query_weight_grad: float32 [768, 768], P('row', 'col')
- key_weight_grad: float32 [768, 768], P('row', 'col')
- value_weight_grad: float32 [768, 768], P('row', 'col')
- query_bias_grad: float32 [768], P('col')
- value_bias_grad: float32 [768], P('col')
- out_weight_grad: float32 [768, 768], P('col', 'row')
- out_bias_grad: float32 [768], P('row')
- attn_gain_grad: float32 [768], P('row')
- attn_shift_grad: float32 [768], P('row')
- up_weight_grad: float32 [768, 3072], P('row', 'col')
- up_bias_grad: float32 [3072], P('col')
- down_weight_grad: float32 [3072, 768], P('col', 'row')
- down_bias_grad: float32 [768], P('row')
- ffn_gain_grad: float32 [768], P('row')
- ffn_shift_grad: float32 [768], P('row')
The draws below stay inside these ranges and needn't reach their ends.
Inputs may be any that keep to these rules, and one draw needn't show every extreme that they name: `segment_ids`: in each row segment numbers never fall and start at 0; each document has 1 to 96 tokens, and one has exactly that many.
All inputs are finite; a program needn't handle non-finite values.
Results may differ from the reference program's by a relative error of at most 0.012.
Values may be sent and summed in bfloat16 or wider, within the bound.
A program may use at most 128 MiB of HBM per device.

```python
import functools
import math
import jax
import jax.numpy as jnp
import numpy as np
from jax import lax

D = 768
HEADS = 12
HEAD = 64
FF = 3072
DOCS = 8
SEQ = 256
NSEQ = 16
TOKENS = 4096


def block_scale(stream_key, extent, shards, low, top_value):
    factor_of, own = 1.0, jax.random.fold_in(stream_key, 6)
    for axis_at, blocks in shards:
        draws = jnp.exp(jax.random.uniform(jax.random.fold_in(own, axis_at), (blocks,), jnp.float32, low / len(shards), top_value / len(shards)))
        factor_of = factor_of * jnp.repeat(draws, extent[axis_at] // blocks).reshape([-1 if axis == axis_at else 1 for axis in range(len(extent))])
    return factor_of


def profile(amount, total, reach, lean):
    portions = [(1 << 20) // math.isqrt(grade ** lean) + 1 for grade in range(2, amount + 1)]
    surplus, holding = total - reach - (amount - 1), [1] * (amount - 1)
    while surplus > 0:
        free = [i for i in range(amount - 1) if holding[i] < reach]
        whole, remaining = sum([portions[i] for i in free]), surplus
        for i in free:
            extra = min(reach - holding[i], max(1, remaining * portions[i] // whole), surplus)
            holding[i] = holding[i] + extra
            surplus = surplus - extra
    return np.array([reach] + holding)


def ragged_sizes(stream_key, count, total, most, lean):
    if count == 2:
        one = jax.random.randint(stream_key, (), max(1, total - most), min(most, total - 1) + 1)
        return jnp.stack([one, total - one])
    sizes = jnp.asarray(profile(count, total, most, lean), jnp.int32)
    twos = (count - 1) // 2
    source_of, sink = sizes[1:1 + 2 * twos:2], sizes[2:2 + 2 * twos:2]
    room = jnp.minimum(source_of - 1, most - sink)
    passed = jax.random.randint(jax.random.fold_in(stream_key, 1), (twos,), 0, 1 << 20) % (room + 1)
    sizes = sizes.at[1:1 + 2 * twos:2].set(source_of - passed).at[2:2 + 2 * twos:2].set(sink + passed)
    return sizes[jax.random.permutation(jax.random.fold_in(stream_key, 2), count)]


def noise(key, dims, scale, reach, pieces=(), kind=jnp.bfloat16):
    factor_of = block_scale(key, dims, pieces, -0.22, 0.18) if pieces else 1.0
    drawn = jax.random.normal(key, dims, jnp.float32) * scale * factor_of
    return jnp.minimum(jnp.maximum(drawn, -reach), reach).astype(kind)


def setup_inputs(seed: int = 0) -> dict:
    streams_of = jax.random.split(jax.random.key(seed), 19)
    tokens = noise(streams_of[0], (D, TOKENS), 1.0, 6.0, ((0, 4), (1, 8)))
    segment_ids = jax.vmap(lambda own: jnp.searchsorted(jnp.cumsum(ragged_sizes(own, DOCS, SEQ, SEQ * 3 // 8, 2)), jnp.arange(SEQ), side="right"))(jax.random.split(streams_of[1], NSEQ)).reshape((NSEQ, SEQ)).astype(jnp.int32)
    query_weight = noise(streams_of[2], (D, D), D ** -0.5, 0.21875, ((0, 4), (1, 2)))
    key_weight = noise(streams_of[3], (D, D), D ** -0.5, 0.21875, ((0, 4), (1, 2)))
    value_weight = noise(streams_of[4], (D, D), D ** -0.5, 0.21875, ((0, 4), (1, 2)))
    query_bias = noise(streams_of[5], (D,), 0.5, 3.0, ((0, 2),), jnp.float32)
    value_bias = noise(streams_of[6], (D,), 0.5, 3.0, ((0, 2),), jnp.float32)
    out_weight = noise(streams_of[7], (D, D), (D // 16) ** -0.5, 0.875, ((0, 2), (1, 4)))
    out_bias = noise(streams_of[8], (D,), 0.5, 3.0, ((0, 4),), jnp.float32)
    attn_gain = jnp.clip(1.0 + 0.1 * jax.random.normal(streams_of[9], (D,), jnp.float32), 0.5, 1.5)
    attn_shift = noise(streams_of[10], (D,), 0.5, 3.0, ((0, 4),), jnp.float32)
    up_weight = noise(streams_of[11], (D, FF), D ** -0.5, 0.21875, ((0, 4), (1, 2)))
    up_bias = noise(streams_of[12], (FF,), 0.5, 3.0, ((0, 2),), jnp.float32)
    down_weight = noise(streams_of[13], (FF, D), FF ** -0.5, 0.109375, ((0, 2), (1, 4)))
    down_bias = noise(streams_of[14], (D,), 0.5, 3.0, ((0, 4),), jnp.float32)
    ffn_gain = jnp.clip(1.0 + 0.1 * jax.random.normal(streams_of[15], (D,), jnp.float32), 0.5, 1.5)
    ffn_shift = noise(streams_of[16], (D,), 0.5, 3.0, ((0, 4),), jnp.float32)
    cotangent = noise(streams_of[17], (D, TOKENS), 1.0, 6.0, ((0, 4), (1, 8)))
    return dict(tokens=tokens, segment_ids=segment_ids, query_weight=query_weight, key_weight=key_weight, value_weight=value_weight, query_bias=query_bias, value_bias=value_bias, out_weight=out_weight, out_bias=out_bias, attn_gain=attn_gain, attn_shift=attn_shift, up_weight=up_weight, up_bias=up_bias, down_weight=down_weight, down_bias=down_bias, ffn_gain=ffn_gain, ffn_shift=ffn_shift, cotangent=cotangent)


@jax.custom_vjp
def low(v):
    return lax.optimization_barrier(v.astype(jnp.bfloat16)).astype(jnp.float32)

@jax.custom_vjp
def low_back(v):
    return v

def low_keep(v):
    return (low(v), None)

def low_pass(kept, grad):
    return (grad,)

def back_keep(v):
    return (v, None)

def back_low(kept, grad):
    return (low(grad),)
low.defvjp(low_keep, low_pass)
low_back.defvjp(back_keep, back_low)
EPS = 1e-05

def matmul(left, right):
    return jnp.dot(left, right, precision=lax.Precision.HIGHEST)

def layer_norm(values, gain, shift):
    centre = lax.optimization_barrier(jnp.mean(values, -1, keepdims=True))
    deviate = values - centre
    spread = lax.optimization_barrier(jnp.mean(deviate * deviate, -1, keepdims=True))
    return deviate * lax.rsqrt(spread + EPS) * gain + shift

def gelu_tanh(values):
    return jax.nn.gelu(values, approximate=True)

def attention(queries, key_vectors, values, segment_ids):
    block_rows = min(512, SEQ)
    score_scale = 1.0 / math.sqrt(HEAD)

    def one_sequence(sequence_item):
        seq_queries, seq_keys, seq_values, seq_ids = sequence_item
        key_heads = seq_keys.reshape(SEQ, HEADS, HEAD)
        value_heads = seq_values.reshape(SEQ, HEADS, HEAD)

        def one_block(block_item):
            block_queries, block_ids = block_item
            scores = jnp.einsum('qhd,khd->hqk', block_queries.reshape(block_rows, HEADS, HEAD), key_heads, precision=lax.Precision.HIGHEST) * score_scale
            scores = low_back(scores)
            same_doc = block_ids[:, None] == seq_ids[None, :]
            attn_probs = low(jax.nn.softmax(jnp.where(same_doc[None], scores, -1000000000.0), axis=-1))
            result = jnp.einsum('hqk,khd->qhd', attn_probs, value_heads, precision=lax.Precision.HIGHEST)
            return result.reshape(block_rows, D)
        outputs = lax.map(jax.checkpoint(one_block), (seq_queries.reshape(SEQ // block_rows, block_rows, D), seq_ids.reshape(SEQ // block_rows, block_rows)))
        return outputs.reshape(SEQ, D)
    stacked = lax.map(one_sequence, (queries.reshape(NSEQ, SEQ, D), key_vectors.reshape(NSEQ, SEQ, D), values.reshape(NSEQ, SEQ, D), segment_ids))
    return stacked.reshape(NSEQ * SEQ, D)

def layer(tokens, query_weight, key_weight, value_weight, query_bias, value_bias, out_weight, out_bias, attn_gain, attn_shift, up_weight, up_bias, down_weight, down_bias, ffn_gain, ffn_shift, segment_ids):
    queries = low_back(low(matmul(tokens, query_weight) + query_bias))
    key_vectors = low_back(low(matmul(tokens, key_weight)))
    values = low_back(low(matmul(tokens, value_weight) + value_bias))
    attended = low_back(low(attention(queries, key_vectors, values, segment_ids)))
    projected = low_back(matmul(attended, out_weight) + out_bias)
    hidden = layer_norm(tokens + projected, attn_gain, attn_shift)
    pre_act = low_back(matmul(low(hidden), up_weight) + up_bias)
    activated = low(gelu_tanh(pre_act))
    down_out = low_back(matmul(activated, down_weight) + down_bias)
    return layer_norm(hidden + down_out, ffn_gain, ffn_shift)

def reference(tokens, segment_ids, query_weight, key_weight, value_weight, query_bias, value_bias, out_weight, out_bias, attn_gain, attn_shift, up_weight, up_bias, down_weight, down_bias, ffn_gain, ffn_shift, cotangent):
    primals = (tokens.T.astype(jnp.float32), query_weight.astype(jnp.float32), key_weight.astype(jnp.float32), value_weight.astype(jnp.float32), query_bias.astype(jnp.float32), value_bias.astype(jnp.float32), out_weight.astype(jnp.float32), out_bias.astype(jnp.float32), attn_gain.astype(jnp.float32), attn_shift.astype(jnp.float32), up_weight.astype(jnp.float32), up_bias.astype(jnp.float32), down_weight.astype(jnp.float32), down_bias.astype(jnp.float32), ffn_gain.astype(jnp.float32), ffn_shift.astype(jnp.float32))
    forward = functools.partial(layer, segment_ids=segment_ids)
    output, pull = jax.vjp(forward, *primals)
    grads = pull(cotangent.T.astype(jnp.float32))
    return (output.T.astype(jnp.bfloat16), grads[0].T, grads[1], grads[2], grads[3], grads[4], grads[5], grads[6], grads[7], grads[8], grads[9], grads[10], grads[11], grads[12], grads[13], grads[14], grads[15])
```

```python
import math

import jax
import jax.numpy as jnp
from jax import lax
from jax.experimental import pallas as pl
from jax.experimental.pallas import tpu as pltpu
from jax.sharding import PartitionSpec as P

HEADS = 12
HEAD = 64


EPS = 1e-05


def gather_over_col(values):
    return lax.all_gather(values, "col", axis=0, tiled=True)


def gather_over_row(values):
    return lax.all_gather(values, "row", axis=0, tiled=True)


def contract(left, weight, flipped):
    if flipped:
        return lax.dot_general(
            left, weight, (((1,), (1,)), ((), ())), preferred_element_type=jnp.float32
        )
    return jnp.dot(left, weight, preferred_element_type=jnp.float32)


def product_rows(gathered, weight, flipped):
    return contract(gathered, weight, flipped)


def heads_in(values):
    return lax.all_to_all(values, "col", split_axis=0, concat_axis=1, tiled=True)


def heads_out(values):
    return lax.all_to_all(values, "col", split_axis=1, concat_axis=0, tiled=True)


def sum_over_row(gathered, block, flipped):
    return lax.psum_scatter(
        product_rows(gathered, block, flipped), "row", scatter_dimension=0, tiled=True
    )


def sum_over_col(gathered, block, flipped):
    return lax.psum_scatter(
        product_rows(gathered, block, flipped), "col", scatter_dimension=0, tiled=True
    )


def row_totals(values):
    return lax.psum(values, "row")


def layer_norm(resid, gain, shift):
    feature_count = resid.shape[1] * lax.axis_size("row")
    centre = row_totals((jnp.sum(resid, 1, keepdims=True),))[0] / feature_count
    deviate = resid - centre
    spread = row_totals((jnp.sum(deviate * deviate, 1, keepdims=True),))[0] / feature_count
    scaling = lax.rsqrt(spread + EPS)
    normed = deviate * scaling
    return (normed * gain + shift, normed, scaling)


def norm_backward(upstream, normed, scaling, gain):
    feature_count = upstream.shape[1] * lax.axis_size("row")
    scaled_grad = upstream * gain
    first_sum, second_sum = row_totals(
        (jnp.sum(scaled_grad, 1, keepdims=True), jnp.sum(scaled_grad * normed, 1, keepdims=True))
    )
    return scaling * (
        scaled_grad - first_sum / feature_count - normed * (second_sum / feature_count)
    )


def gelu_tanh(values):
    return jax.nn.gelu(values, approximate=True)


def column_sums(values):
    return jnp.sum(values, 0, dtype=jnp.float32)


def head_scores(query_split, key_split, same_doc):
    scores = jnp.einsum("qhd,khd->hqk", query_split, key_split, preferred_element_type=jnp.float32)
    scores = scores * (1.0 / math.sqrt(HEAD))
    return jnp.where(same_doc[None], scores, -1000000000.0)


def body(
    tokens,
    segment_ids,
    query_weight,
    key_weight,
    value_weight,
    query_bias,
    value_bias,
    out_weight,
    out_bias,
    attn_gain,
    attn_shift,
    up_weight,
    up_bias,
    down_weight,
    down_bias,
    ffn_gain,
    ffn_shift,
    cotangent,
):
    token_major = tokens.T
    head_cols = query_weight.shape[1]
    score_scale = 1.0 / math.sqrt(HEAD)
    joined_weight = jnp.concatenate([query_weight, key_weight, value_weight], 1)
    token_rows = gather_over_col(token_major)
    joined = sum_over_row(token_rows, joined_weight, False)
    query_block = (joined[:, :head_cols] + query_bias).astype(jnp.bfloat16)
    key_block = joined[:, head_cols : 2 * head_cols].astype(jnp.bfloat16)
    value_block = (joined[:, 2 * head_cols :] + value_bias).astype(jnp.bfloat16)
    query_heads = heads_in(query_block)
    key_heads, value_heads = (
        lax.all_gather(key_block, "col", axis=1, tiled=True),
        lax.all_gather(value_block, "col", axis=1, tiled=True),
    )
    query_count = query_heads.shape[0]
    key_count = key_heads.shape[0]
    sequence_ids = segment_ids[0]
    query_ids = lax.dynamic_slice_in_dim(
        sequence_ids, lax.axis_index("col") * query_count, query_count, 0
    )
    same_doc = query_ids[:, None] == sequence_ids[None, :]
    query_split = query_heads.reshape(query_count, HEADS, HEAD)
    key_split = key_heads.reshape(key_count, HEADS, HEAD)
    value_split = value_heads.reshape(key_count, HEADS, HEAD)
    scores = head_scores(query_split, key_split, same_doc)
    highest = jnp.max(scores, -1, keepdims=True)
    exponent = jnp.exp(scores - highest)
    totals = jnp.sum(exponent, -1, keepdims=True)
    log_totals = highest + jnp.log(totals)
    attn_probs = (exponent / totals).astype(jnp.bfloat16)
    attended = jnp.einsum(
        "hqk,khd->qhd", attn_probs, value_split, preferred_element_type=jnp.float32
    )
    attended = attended.reshape(query_count, -1).astype(jnp.bfloat16)
    attended_block = heads_out(attended)
    attended_rows = gather_over_row(attended_block)
    projected = sum_over_col(attended_rows, out_weight, False) + out_bias
    hidden, hidden_normed, hidden_scaling = layer_norm(
        token_major.astype(jnp.float32) + projected, attn_gain, attn_shift
    )
    hidden_low = hidden.astype(jnp.bfloat16)
    hidden_rows = gather_over_col(hidden_low)
    pre_act = sum_over_row(hidden_rows, up_weight, False) + up_bias
    activated, gelu_pull = jax.vjp(gelu_tanh, pre_act)
    act_block = activated.astype(jnp.bfloat16)
    act_rows = gather_over_row(act_block)
    down_out = sum_over_col(act_rows, down_weight, False) + down_bias
    output, out_normed, out_scaling = layer_norm(hidden + down_out, ffn_gain, ffn_shift)
    upstream = cotangent.T.astype(jnp.float32)
    ffn_gain_grad = jnp.sum(upstream * out_normed, 0)
    ffn_shift_grad = jnp.sum(upstream, 0)
    resid_grad = norm_backward(upstream, out_normed, out_scaling, ffn_gain)
    down_grad_rows = gather_over_col(resid_grad.astype(jnp.bfloat16))
    down_weight_grad = jnp.einsum(
        "tf,td->fd", act_rows, down_grad_rows, preferred_element_type=jnp.float32
    )
    down_bias_grad = column_sums(down_grad_rows)
    act_grad = sum_over_row(down_grad_rows, down_weight, True)
    pre_grad = gelu_pull(act_grad)[0].astype(jnp.bfloat16)
    pre_grad_rows = gather_over_row(pre_grad)
    up_weight_grad = jnp.einsum(
        "td,tf->df", hidden_rows, pre_grad_rows, preferred_element_type=jnp.float32
    )
    up_bias_grad = column_sums(pre_grad_rows)
    hidden_grad = sum_over_col(pre_grad_rows, up_weight, True) + resid_grad
    attn_gain_grad = jnp.sum(hidden_grad * hidden_normed, 0)
    attn_shift_grad = jnp.sum(hidden_grad, 0)
    first_grad = norm_backward(hidden_grad, hidden_normed, hidden_scaling, attn_gain)
    proj_grad_rows = gather_over_col(first_grad.astype(jnp.bfloat16))
    out_weight_grad = jnp.einsum(
        "tc,td->cd", attended_rows, proj_grad_rows, preferred_element_type=jnp.float32
    )
    out_bias_grad = column_sums(proj_grad_rows)
    attended_grad = heads_in(sum_over_row(proj_grad_rows, out_weight, True).astype(jnp.bfloat16))
    scores = head_scores(query_split, key_split, same_doc)
    attn_exact = jnp.exp(scores - log_totals)
    grad_split = attended_grad.reshape(query_count, HEADS, HEAD)
    prob_grad = jnp.einsum(
        "qhd,khd->hqk", grad_split, value_split, preferred_element_type=jnp.float32
    )
    score_grad = attn_exact * (prob_grad - jnp.sum(prob_grad * attn_exact, -1, keepdims=True))
    score_grad = score_grad.astype(jnp.bfloat16)
    query_grad = (
        jnp.einsum("hqk,khd->qhd", score_grad, key_split, preferred_element_type=jnp.float32)
        * score_scale
    )
    query_grad = query_grad.reshape(query_count, -1).astype(jnp.bfloat16)
    key_grad = (
        jnp.einsum("hqk,qhd->khd", score_grad, query_split, preferred_element_type=jnp.float32)
        * score_scale
    )
    key_grad = key_grad.reshape(key_count, -1)
    value_grad = jnp.einsum(
        "hqk,qhd->khd",
        attn_exact.astype(jnp.bfloat16),
        grad_split,
        preferred_element_type=jnp.float32,
    ).reshape(key_count, -1)
    key_sum, value_sum = (
        lax.psum_scatter(
            key_grad.astype(jnp.bfloat16), "col", scatter_dimension=1, tiled=True
        ).astype(jnp.float32),
        lax.psum_scatter(
            value_grad.astype(jnp.bfloat16), "col", scatter_dimension=1, tiled=True
        ).astype(jnp.float32),
    )
    joined_grad = jnp.concatenate(
        [heads_out(query_grad), key_sum.astype(jnp.bfloat16), value_sum.astype(jnp.bfloat16)], 1
    )
    joined_rows = gather_over_row(joined_grad)
    joined_weight_grad = jnp.einsum(
        "td,tf->df", token_rows, joined_rows, preferred_element_type=jnp.float32
    )
    query_bias_grad = column_sums(joined_rows[:, :head_cols])
    value_bias_grad = column_sums(joined_rows[:, 2 * head_cols :])
    tokens_grad = sum_over_col(joined_rows, joined_weight, True) + first_grad
    summed = lax.psum(
        (
            joined_weight_grad,
            query_bias_grad,
            value_bias_grad,
            out_weight_grad,
            out_bias_grad,
            up_weight_grad,
            up_bias_grad,
            down_weight_grad,
            down_bias_grad,
        ),
        "dp",
    )
    norm_sums = lax.psum(
        (attn_gain_grad, attn_shift_grad, ffn_gain_grad, ffn_shift_grad), ("dp", "col")
    )
    return (
        output.T.astype(jnp.bfloat16),
        tokens_grad.T,
        summed[0][:, :head_cols],
        summed[0][:, head_cols : 2 * head_cols],
        summed[0][:, 2 * head_cols :],
        summed[1],
        summed[2],
        summed[3],
        summed[4],
        norm_sums[0],
        norm_sums[1],
        summed[5],
        summed[6],
        summed[7],
        summed[8],
        norm_sums[2],
        norm_sums[3],
    )


MESH_ID = pl.DeviceIdType.MESH
BF = jnp.bfloat16
F32 = jnp.float32
GRID = {"dp": 4, "row": 4, "col": 2}
SEQ = 256
WIDE = 768
HALF = 128
ROWS = 192
CHUNK = 384
CHUNKS = 12
SEMS = 256


def small_grid(mesh):
    return dict(mesh.shape) == GRID


def mm(a, b):
    return jnp.dot(a, b, preferred_element_type=F32)


def mm_nt(a, b):
    return lax.dot_general(a, b, (((1,), (1,)), ((), ())), preferred_element_type=F32)


def loop(count, step):
    def wrapped(i, carry):
        step(i)
        return carry

    lax.fori_loop(0, count, wrapped, 0)


def row_mean(values):
    return jnp.sum(values, axis=1, keepdims=True) * (1.0 / WIDE)


def fold(values):
    return jnp.sum(values.reshape(values.shape[0] // 8, 8, values.shape[1]), axis=0)


def layer_kernel(
    ids,
    tok,
    cot,
    qw,
    kw,
    vw,
    ow,
    uw,
    dw,
    qb,
    vb,
    ub,
    own_vec,
    fin_out,
    res_out,
    tg_out,
    vec_out,
    W,
    G,
    R1,
    R2,
    RD,
    RU,
    fin,
    xin,
    cin,
    xs,
    xr,
    vg,
    vec,
    VA,
    VB,
    VC,
    VD,
    VZ,
    xf,
    cf,
    neq,
    q,
    k,
    v,
    qT,
    kT,
    P,
    at,
    hid,
    n1,
    s1,
    hb,
    hT,
    act,
    dact,
    outf,
    r2g,
    dg,
    dgT,
    pg,
    fg,
    fgT,
    pgT,
    prg,
    dA,
    dAT,
    dT,
    tgp,
    tgr,
    osend,
    obuf,
    tsend,
    tbuf,
    send,
    recv,
):
    dp = lax.axis_index("dp")
    z = lax.axis_index("row")
    x = lax.axis_index("col")
    core = lax.rem(dp, 2)
    y = lax.div(dp, 2)
    mate = dp + 1 - 2 * core
    far = lax.rem(dp + 2, 4)
    matefar = lax.rem(mate + 2, 4)
    other = 1 - x
    counts = {"s": 0, "r": 0}
    pending = []

    def new(kind, n=1):
        base = counts[kind]
        counts[kind] = base + n
        assert counts[kind] <= SEMS
        return base

    def push(src, dst, ssem, rsem, **where):
        return pltpu.make_async_remote_copy(
            src_ref=src,
            dst_ref=dst,
            send_sem=send.at[ssem],
            recv_sem=recv.at[rsem],
            device_id=where,
            device_id_type=MESH_ID,
        )

    def start(pred, make):
        if pred is None:
            make().start()
        else:

            @pl.when(pred)
            def _():
                make().start()

        pending.append((pred, make))

    def arrived(dst, rsem, **where):
        push(dst, dst, 0, rsem, **where).wait_recv()

    def rows(b):
        return pl.ds(pl.multiple_of(b * ROWS, ROWS), ROWS)

    bar = pltpu.get_barrier_semaphore()
    for j in range(4):
        for h in range(2):

            @pl.when((z != j) | (x != h))
            def _(j=j, h=h):
                pl.semaphore_signal(bar, inc=1, device_id={"row": j, "col": h}, device_id_type=MESH_ID)

    pl.semaphore_signal(bar, inc=1, device_id={"dp": mate}, device_id_type=MESH_ID)
    pl.semaphore_signal(bar, inc=1, device_id={"dp": far}, device_id_type=MESH_ID)

    lsem = new("s", CHUNKS)
    mine = rows(z)

    def local_parts():
        parts = []
        for j, ref in enumerate((qw, kw, vw, ow)):
            parts.append((ref, W.at[j, mine]))
        for i in range(4):
            parts.append((uw.at[:, i * CHUNK : (i + 1) * CHUNK], W.at[4 + i, mine]))
        for i in range(4):
            parts.append((dw.at[:, i * CHUNK : (i + 1) * CHUNK], W.at[8 + i, mine]))
        return [pltpu.make_async_copy(a, b, send.at[lsem + n]) for n, (a, b) in enumerate(parts)]

    locals_ = local_parts()
    for c in locals_:
        c.start()
    vg[z] = own_vec[...]
    seg = jnp.broadcast_to(ids[...].astype(F32), (SEQ, SEQ))
    neq[...] = jnp.abs(seg - seg.T)
    pl.semaphore_wait(bar, 9)

    def spread(ref, landing):
        ssem, rsem = new("s", 4), new("r", 4)
        for s in range(2):
            for h in range(2):
                jj = 2 * x + s
                self_ = (jj == z) & (h == x)
                src = ref.at[:, s * SEQ + h * HALF : s * SEQ + (h + 1) * HALF]
                dst = landing.at[h, mine]
                start(
                    jnp.logical_not(self_),
                    lambda src=src, dst=dst, n=2 * s + h, jj=jj, h=h: push(
                        src, dst, ssem + n, rsem + z, row=jj, col=h
                    ),
                )

                @pl.when(self_)
                def _(src=src, dst=dst):
                    pltpu.make_async_copy(src, dst, recv.at[rsem + z]).start()

        def collect():
            home = lax.div(z, 2) == x
            for b in range(4):
                local = home & (z == b)
                dst = landing.at[x, rows(b)]

                @pl.when(local)
                def _(dst=dst, b=b):
                    pltpu.make_async_copy(ref.at[:, 0:HALF], dst, recv.at[rsem + b]).wait()

                @pl.when(jnp.logical_not(local))
                def _(dst=dst, b=b):
                    arrived(dst, rsem + b, col=other)

        return collect

    def swap(landing):
        ssem, rsem = new("s"), new("r")
        start(None, lambda: push(landing.at[x], landing.at[x], ssem, rsem, col=other))

        def collect():
            arrived(landing.at[other], rsem, col=other)

        return collect

    def share_vec():
        ssem, rsem = new("s", 3), new("r", 4)
        for o in range(1, 4):
            to = lax.rem(z + o, 4)
            start(None, lambda o=o, to=to: push(own_vec, vg.at[z], ssem + o - 1, rsem + z, row=to))

        def collect():
            for o in range(1, 4):
                b = lax.rem(z + o, 4)
                arrived(vg.at[b], rsem + b, row=b)
            vec[...] = vg[0] + vg[1] + vg[2] + vg[3]

        return collect

    def gather(g):
        zs, ys, cs = new("s", 6), new("s", 4), new("s", 8)
        zr, yr, cr = new("r", 4), new("r", 4), new("r", 8)
        own, ychunk = 4 * g + dp, 4 * g + far

        def block(chunk, b):
            return W.at[chunk, rows(b)]

        def up(d, b, pred):
            start(pred, lambda: push(block(own, b), block(own, b), zs + d, zr + b, row=z + 1))

        def down(d, b, pred):
            start(pred, lambda: push(block(own, b), block(own, b), zs + 3 + d, zr + b, row=z - 1))

        def first():
            up(0, z, z < 3)
            down(0, z, z > 0)

        def hop(d):
            for below in (True, False):
                b = z - d if below else z + d
                here = z >= d if below else z + d <= 3

                @pl.when(here)
                def _(b=b):
                    arrived(block(own, b), zr + b, row=b)

                if d < 3:
                    if below:
                        up(d, b, here & (z < 3))
                    else:
                        down(d, b, here & (z > 0))
                start(here, lambda b=b: push(block(own, b), block(own, b), ys + b, yr + b, dp=far))
                start(here, lambda b=b: push(block(own, b), block(own, b), cs + b, cr + b, dp=mate))

        def across():
            for b in range(4):
                there = z != b

                @pl.when(there)
                def _(b=b):
                    arrived(block(ychunk, b), yr + b, dp=far)

                start(
                    there,
                    lambda b=b: push(block(ychunk, b), block(ychunk, b), cs + 4 + b, cr + 4 + b, dp=mate),
                )

        def finish():
            for b in range(4):

                @pl.when(z != b)
                def _(b=b):
                    arrived(block(4 * g + mate, b), cr + b, dp=mate)
                    arrived(block(4 * g + matefar, b), cr + 4 + b, dp=mate)

        return first, hop, across, finish

    def exchange(n):
        ssem, rsem = new("s", 3), new("r", 3)

        def put(c, value):
            xs[n, c] = value.astype(BF)
            start(None, lambda: push(xs.at[n, c], xr.at[n, c], ssem + c, rsem + c, col=other))

        def collect():
            for c in range(3):
                arrived(xr.at[n, c], rsem + c, col=other)

        return put, collect

    def both(n, r):
        own = [xs[n, c, r, :].astype(F32) + xr[n, c, r, :].astype(F32) for c in range(3)]
        return jnp.concatenate(own, axis=1)

    def reduce(g):
        s1_, s2_, sd, su, sy, sc = new("s", 2), new("s"), new("s", 3), new("s", 3), new("s"), new("s", 2)
        r1, r2, rd, ru, ry, rc = new("r", 2), new("r"), new("r", 3), new("r", 3), new("r"), new("r", 2)
        own, ychunk = 4 * g + dp, 4 * g + far
        sf = new("s", 2)

        def to_core():
            for j in range(2):
                src = G.at[4 * g + 2 * j + 1 - core]
                start(None, lambda src=src, j=j: push(src, R1.at[g, j], s1_ + j, r1 + j, dp=mate))

        def add(chunk, extra, base, count):
            def step(i):
                at_ = pl.ds(pl.multiple_of(base + i * 64, 64), 64)
                from_ = pl.ds(pl.multiple_of(i * 64, 64), 64)
                G[chunk, at_, :] = (G[chunk, at_, :].astype(F32) + extra[from_, :].astype(F32)).astype(BF)

            loop(count // 64, step)

        def to_y():
            for j in (1 - y, y):
                chunk = 4 * g + 2 * j + core
                arrived(R1.at[g, j], r1 + j, dp=mate)
                add(chunk, R1.at[g, j], 0, WIDE)
                if j is not y:
                    start(None, lambda: push(G.at[ychunk], R2.at[g], s2_, r2, dp=far))

        def piece(b):
            return G.at[own, rows(b)]

        def send_down(b, pred):
            start(pred, lambda: push(piece(b), RD.at[g, b], sd + b, rd + b, row=z - 1))

        def send_up(b, pred):
            start(pred, lambda: push(piece(b), RU.at[g, b - 1], su + b - 1, ru + b - 1, row=z + 1))

        def take_down(b):
            arrived(RD.at[g, b], rd + b, row=z + 1)
            add(own, RD.at[g, b], b * ROWS, ROWS)

        def take_up(b):
            arrived(RU.at[g, b - 1], ru + b - 1, row=z - 1)
            add(own, RU.at[g, b - 1], b * ROWS, ROWS)

        def chain0():
            arrived(R2.at[g], r2, dp=far)
            add(own, R2.at[g], 0, WIDE)
            for b in (0, 1, 2):
                send_down(b, z == 3)
            for b in (3, 2, 1):
                send_up(b, z == 0)

        def chain1():
            for b in (0, 1):

                @pl.when(z == 2)
                def _(b=b):
                    take_down(b)

                send_down(b, z == 2)
            for b in (3, 2):

                @pl.when(z == 1)
                def _(b=b):
                    take_up(b)

                send_up(b, z == 1)

        def chain2():
            @pl.when(z == 1)
            def _():
                take_down(0)

            send_down(0, z == 1)

            @pl.when(z == 2)
            def _():
                take_up(3)

            send_up(3, z == 2)

        def settle():
            @pl.when(z < 3)
            def _():
                take_down(z)

            @pl.when(z > 0)
            def _():
                take_up(z)

            fin[own] = G[own, mine, :]
            start(None, lambda: push(fin.at[own], fin.at[own], sy, ry, dp=far))
            start(None, lambda: push(fin.at[own], fin.at[own], sc, rc, dp=mate))

        def across():
            arrived(fin.at[ychunk], ry, dp=far)
            start(None, lambda: push(fin.at[ychunk], fin.at[ychunk], sc + 1, rc + 1, dp=mate))

        def finish():
            arrived(fin.at[4 * g + mate], rc, dp=mate)
            arrived(fin.at[4 * g + matefar], rc + 1, dp=mate)

        return to_core, to_y, chain0, chain1, chain2, settle, across, finish

    def deliver(sent, landed, out):
        ssem, rsem = new("s", 4), new("r", 4)
        slot = 2 * lax.rem(z, 2) + x
        home = lax.div(z, 2) == x
        for b in range(4):
            self_ = home & (z == b)
            start(
                jnp.logical_not(self_),
                lambda b=b: push(
                    sent.at[rows(b)], landed.at[slot], ssem + b, rsem + slot, row=b, col=lax.div(z, 2)
                ),
            )

            @pl.when(self_)
            def _(b=b):
                pltpu.make_async_copy(sent.at[rows(b)], landed.at[slot], recv.at[rsem + slot]).start()

        def collect():
            osem = new("s", 4)
            copies = []
            for n in range(4):
                s, h = n // 2, n % 2
                local = (2 * x + s == z) & (h == x)

                @pl.when(local)
                def _(n=n):
                    pltpu.make_async_copy(sent.at[rows(z)], landed.at[n], recv.at[rsem + n]).wait()

                @pl.when(jnp.logical_not(local))
                def _(n=n):
                    arrived(landed.at[n], rsem + n, col=other)

                copies.append(
                    pltpu.make_async_copy(
                        landed.at[n], out.at[:, n * HALF : (n + 1) * HALF], send.at[osem + n]
                    )
                )
                copies[-1].start()
            return copies

        return collect

    tok_in = spread(tok, xin)
    vec_in = share_vec()
    gathers = [gather(g) for g in range(3)]
    for c in locals_:
        c.wait()
    for g in range(3):
        gathers[g][0]()
    cot_in = spread(cot, cin)
    tok_in()
    tok_swap = swap(xin)
    gathers[0][1](1)
    gathers[0][1](2)
    gathers[0][1](3)
    tok_swap()
    vec_in()
    for h in range(2):
        xf[h * HALF : (h + 1) * HALF, :] = xin[h].astype(F32).T
    gathers[0][2]()
    gathers[1][1](1)
    gathers[1][1](2)
    gathers[1][1](3)
    gathers[0][3]()

    xb = xf[...].astype(BF)
    for j, (dst, bias) in enumerate(((q, qb), (k, None), (v, vb))):
        r = mm(xb, W[j])
        if bias is not None:
            r = r + bias[...]
        for p in range(3):
            dst[p] = r[:, p * HALF : (p + 1) * HALF].astype(BF)

    lane = lax.broadcasted_iota(jnp.int32, (SEQ, HALF), 1) < HEAD
    scale = 1.0 / math.sqrt(HEAD)

    def only(values, hh):
        keep = lane if hh == 0 else jnp.logical_not(lane)
        return jnp.where(keep, values.astype(F32), 0.0).astype(BF)

    def attend(p):
        qv, kv, vv = q[p], k[p], v[p]
        outs = []
        for hh in range(2):
            s = mm_nt(only(qv, hh), kv) * scale
            s = jnp.where(neq[...] == 0.0, s, -1000000000.0)
            e = jnp.exp(s - jnp.max(s, axis=1, keepdims=True))
            pr = e / jnp.sum(e, axis=1, keepdims=True)
            P[2 * p + hh] = pr
            outs.append(mm(pr.astype(BF), vv))
        at[p] = jnp.where(lane, outs[0], outs[1]).astype(BF)

    loop(3, attend)
    gathers[2][1](1)

    put0, get0 = exchange(0)
    att = jnp.concatenate([at[0], at[1], at[2]], axis=1)
    for c in range(3):
        put0(c, mm_nt(att, W[3, c * SEQ : (c + 1) * SEQ, :]))
    for p in range(3):
        qT[p] = q[p].astype(F32).T.astype(BF)
        kT[p] = k[p].astype(F32).T.astype(BF)
    gathers[2][1](2)
    gathers[2][1](3)
    gathers[1][2]()
    cot_in()
    cot_swap = swap(cin)
    get0()

    def norm1(i):
        r = pl.ds(pl.multiple_of(i * 32, 32), 32)
        resid = xf[r, :] + (both(0, r) + vec[0:1, :])
        d = resid - row_mean(resid)
        s = lax.rsqrt(row_mean(d * d) + EPS)
        n = d * s
        h = n * vec[1:2, :] + vec[2:3, :]
        n1[r, :] = n
        s1[r, :] = jnp.broadcast_to(s, (32, HALF))
        hid[r, :] = h
        hb[r, :] = h.astype(BF)

    loop(8, norm1)
    gathers[1][3]()

    hv = hb[...]
    c0 = math.sqrt(2.0 / math.pi)

    def up_step(i):
        u = mm(hv, W[4 + i]) + ub[i]
        u2 = u * u
        t = jnp.tanh(c0 * (u + 0.044715 * (u2 * u)))
        half = 0.5 * (1.0 + t)
        act[i] = (u * half).astype(BF)
        dact[i] = half + (0.5 * u) * (1.0 - t * t) * (c0 * (1.0 + (3 * 0.044715) * u2))

    loop(4, up_step)
    gathers[2][2]()
    hT[...] = hid[...].T.astype(BF)
    cot_swap()
    for h in range(2):
        cf[h * HALF : (h + 1) * HALF, :] = cin[h].astype(F32).T
    gathers[2][3]()
    put1, get1 = exchange(1)
    for c in range(3):
        acc = mm_nt(act[0], W[8, c * SEQ : (c + 1) * SEQ, :])
        for i in range(1, 4):
            acc = acc + mm_nt(act[i], W[8 + i, c * SEQ : (c + 1) * SEQ, :])
        put1(c, acc)
    get1()

    VA[...] = jnp.zeros_like(VA)

    def norm2(i, carry):
        gain_sum, shift_sum, bias_sum = carry
        r = pl.ds(pl.multiple_of(i * 32, 32), 32)
        resid = hid[r, :] + (both(1, r) + vec[3:4, :])
        d = resid - row_mean(resid)
        s = lax.rsqrt(row_mean(d * d) + EPS)
        n = d * s
        outf[r, :] = n * vec[4:5, :] + vec[5:6, :]
        up = cf[r, :]
        e = up * vec[4:5, :]
        grad = s * (e - row_mean(e) - n * row_mean(e * n))
        low = grad.astype(BF)
        r2g[r, :] = grad
        dg[r, :] = low
        return gain_sum + fold(up * n), shift_sum + fold(up), bias_sum + fold(low.astype(F32))

    zero = jnp.zeros((8, WIDE), F32)
    sums = lax.fori_loop(0, 8, norm2, (zero, zero, zero))

    def total(values):
        return jnp.sum(values, axis=0, keepdims=True)

    VA[7:8, :] = total(sums[0])
    VA[8:9, :] = total(sums[1])
    VA[6:7, :] = total(sums[2])
    dgT[...] = r2g[...].T.astype(BF)
    reduces = [reduce(g) for g in range(3)]

    def outer(dst, left, right):
        def step(b):
            r = pl.ds(pl.multiple_of(b * SEQ, SEQ), SEQ)
            G[dst, r, :] = mm(left[r, :], right).astype(BF)

        loop(3, step)

    loop(4, lambda i: outer(8 + i, dgT, act[i]))
    reduces[2][0]()

    ones = jnp.ones((8, SEQ), BF)
    dgv = dg[...]

    def pre_step(i):
        low = (mm(dgv, W[8 + i]) * dact[i]).astype(BF)
        prg[i] = low

    loop(4, pre_step)
    put2, get2 = exchange(2)
    for c in range(3):
        acc = mm_nt(prg[0], W[4, c * SEQ : (c + 1) * SEQ, :])
        for i in range(1, 4):
            acc = acc + mm_nt(prg[i], W[4 + i, c * SEQ : (c + 1) * SEQ, :])
        put2(c, acc)
    for i in range(4):
        VA[1 + i // 2 : 2 + i // 2, (i % 2) * CHUNK : (i % 2 + 1) * CHUNK] = mm(ones, prg[i])[0:1, :]
    loop(4, lambda i: outer(4 + i, hT, prg[i]))
    reduces[1][0]()
    reduces[2][1]()

    mine_tokens = pl.ds(pl.multiple_of(x * HALF, HALF), HALF)
    osend[...] = outf[mine_tokens, :].T.astype(BF)
    out_in = deliver(osend, obuf, res_out)
    reduces[2][2]()
    reduces[1][1]()
    get2()

    def norm1_back(i, carry):
        gain_sum, shift_sum, bias_sum = carry
        r = pl.ds(pl.multiple_of(i * 32, 32), 32)
        up = r2g[r, :] + both(2, r)
        n = n1[r, :]
        s = s1[r, :][:, 0:1]
        e = up * vec[1:2, :]
        grad = s * (e - row_mean(e) - n * row_mean(e * n))
        low = grad.astype(BF)
        fg[r, :] = grad
        pg[r, :] = low
        return gain_sum + fold(up * n), shift_sum + fold(up), bias_sum + fold(low.astype(F32))

    sums = lax.fori_loop(0, 8, norm1_back, (zero, zero, zero))
    VA[4:5, :] = total(sums[0])
    VA[5:6, :] = total(sums[1])
    VA[3:4, :] = total(sums[2])
    for h in range(2):
        t = fg[h * HALF : (h + 1) * HALF, :].T
        fgT[h] = t
        pgT[:, h * HALF : (h + 1) * HALF] = t.astype(BF)

    reduces[2][3]()
    reduces[1][2]()
    r = mm(pg[...], W[3])
    for p in range(3):
        part = r[:, p * HALF : (p + 1) * HALF].astype(BF)
        dA[p] = part
        dAT[p] = part.astype(F32).T.astype(BF)
    outer(3, pgT, att)

    top = lax.broadcasted_iota(jnp.int32, (HALF, SEQ), 0) < HEAD

    def attend_back(p):
        dAv, vv = dA[p], v[p]
        dq, dk, dv = [], [], []
        for hh in range(2):
            pr = P[2 * p + hh]
            pgrad = mm_nt(only(dAv, hh), vv)
            ds = (pr * (pgrad - jnp.sum(pgrad * pr, axis=1, keepdims=True))).astype(BF)
            dq.append(mm_nt(kT[p], ds))
            dk.append(mm(qT[p], ds))
            dv.append(mm(dAT[p], pr.astype(BF)))
        dT[0, p] = (jnp.where(top, dq[0], dq[1]) * scale).astype(BF)
        dT[1, p] = (jnp.where(top, dk[0], dk[1]) * scale).astype(BF)
        dT[2, p] = jnp.where(top, dv[0], dv[1]).astype(BF)

    loop(3, attend_back)
    reduces[2][4]()
    reduces[1][3]()

    for j in range(3):
        t = dT[j].reshape(CHUNK, SEQ)
        if j != 1:
            at_ = 0 if j == 0 else CHUNK
            VA[0:1, at_ : at_ + CHUNK] = mm_nt(ones, t)[0:1, :]

        def step(b, t=t, j=j):
            r = pl.ds(pl.multiple_of(b * SEQ, SEQ), SEQ)
            left = jnp.concatenate([xin[0, r, :], xin[1, r, :]], axis=1)
            G[j, r, :] = mm_nt(left, t).astype(BF)

        loop(3, step)
    reduces[0][0]()
    vs, vr = new("s", 5), new("r", 6)
    start(None, lambda: push(VA, VB, vs, vr, dp=mate))

    def back_step(b):
        r = pl.ds(pl.multiple_of(b * SEQ, SEQ), SEQ)
        acc = mm(W[0, r, :], dT[0].reshape(CHUNK, SEQ))
        acc = acc + mm(W[1, r, :], dT[1].reshape(CHUNK, SEQ))
        acc = acc + mm(W[2, r, :], dT[2].reshape(CHUNK, SEQ))
        tgp[0, r, :] = acc[:, :HALF].astype(BF)
        tgp[1, r, :] = acc[:, HALF:].astype(BF)

    loop(3, back_step)
    ts, tr = new("s"), new("r")
    start(None, lambda: push(tgp.at[other], tgr, ts, tr, col=other))
    reduces[0][1]()
    reduces[2][5]()
    reduces[1][4]()
    arrived(VB, vr, dp=mate)
    VD[...] = VA[...] + VB[...]
    start(None, lambda: push(VD, VC, vs + 1, vr + 1, dp=far))
    reduces[0][2]()
    arrived(tgr, tr, col=other)
    tsend[...] = (tgp[x].astype(F32) + tgr[...].astype(F32) + fgT[x]).astype(BF)
    tg_in = deliver(tsend, tbuf, tg_out)
    reduces[1][5]()
    reduces[0][3]()
    reduces[2][6]()
    reduces[0][4]()
    reduces[1][6]()
    arrived(VC, vr + 1, dp=far)
    VZ[z] = VD[...] + VC[...]
    for o in range(1, 4):
        to = lax.rem(z + o, 4)
        start(None, lambda o=o, to=to: push(VZ.at[z], VZ.at[z], vs + 1 + o, vr + 2 + z, row=to))
    reduces[0][5]()
    reduces[2][7]()
    reduces[1][7]()
    copies = []
    fsem = new("s", 3)

    def flush(g):
        c = pltpu.make_async_copy(
            fin.at[4 * g : 4 * g + 4], fin_out.at[4 * g : 4 * g + 4], send.at[fsem + g]
        )
        c.start()
        copies.append(c)

    flush(2)
    flush(1)
    for o in range(1, 4):
        b = lax.rem(z + o, 4)
        arrived(VZ.at[b], vr + 2 + b, row=b)
    vec_out[...] = VZ[0] + VZ[1] + VZ[2] + VZ[3]
    copies += out_in()
    copies += tg_in()
    reduces[0][6]()
    reduces[0][7]()
    flush(0)
    for pred, make in pending:
        if pred is None:
            make().wait_send()
        else:

            @pl.when(pred)
            def _(make=make):
                make().wait_send()

    for c in copies:
        c.wait()


def fused_body(
    tokens,
    segment_ids,
    query_weight,
    key_weight,
    value_weight,
    query_bias,
    value_bias,
    out_weight,
    out_bias,
    attn_gain,
    attn_shift,
    up_weight,
    up_bias,
    down_weight,
    down_bias,
    ffn_gain,
    ffn_shift,
    cotangent,
):
    z = lax.axis_index("row")
    vectors = jnp.stack([out_bias, attn_gain, attn_shift, down_bias, ffn_gain, ffn_shift])
    vectors = jnp.pad(vectors, ((0, 2), (0, 0)))
    placed = jnp.concatenate(
        [jnp.where(z == b, vectors, 0.0) for b in range(4)], axis=1
    )
    hbm = pl.BlockSpec(memory_space=pl.ANY)
    vmem = pl.BlockSpec(memory_space=pltpu.VMEM)
    grads, out, tgrad, sums = pl.pallas_call(
        layer_kernel,
        out_shape=(
            jax.ShapeDtypeStruct((CHUNKS, ROWS, CHUNK), BF),
            jax.ShapeDtypeStruct((ROWS, 2 * SEQ), BF),
            jax.ShapeDtypeStruct((ROWS, 2 * SEQ), BF),
            jax.ShapeDtypeStruct((16, WIDE), F32),
        ),
        in_specs=[vmem] + [hbm] * 8 + [vmem] * 4,
        out_specs=(hbm, hbm, hbm, vmem),
        scratch_shapes=[
            pltpu.VMEM((CHUNKS, WIDE, CHUNK), BF),
            pltpu.VMEM((CHUNKS, WIDE, CHUNK), BF),
            pltpu.VMEM((3, 2, WIDE, CHUNK), BF),
            pltpu.VMEM((3, WIDE, CHUNK), BF),
            pltpu.VMEM((3, 3, ROWS, CHUNK), BF),
            pltpu.VMEM((3, 3, ROWS, CHUNK), BF),
            pltpu.VMEM((CHUNKS, ROWS, CHUNK), BF),
            pltpu.VMEM((2, WIDE, HALF), BF),
            pltpu.VMEM((2, WIDE, HALF), BF),
            pltpu.VMEM((3, 3, SEQ, SEQ), BF),
            pltpu.VMEM((3, 3, SEQ, SEQ), BF),
            pltpu.VMEM((4, 8, WIDE), F32),
            pltpu.VMEM((8, WIDE), F32),
            pltpu.VMEM((16, WIDE), F32),
            pltpu.VMEM((16, WIDE), F32),
            pltpu.VMEM((16, WIDE), F32),
            pltpu.VMEM((16, WIDE), F32),
            pltpu.VMEM((4, 16, WIDE), F32),
            pltpu.VMEM((SEQ, WIDE), F32),
            pltpu.VMEM((SEQ, WIDE), F32),
            pltpu.VMEM((SEQ, SEQ), F32),
            pltpu.VMEM((3, SEQ, HALF), BF),
            pltpu.VMEM((3, SEQ, HALF), BF),
            pltpu.VMEM((3, SEQ, HALF), BF),
            pltpu.VMEM((3, HALF, SEQ), BF),
            pltpu.VMEM((3, HALF, SEQ), BF),
            pltpu.VMEM((6, SEQ, SEQ), F32),
            pltpu.VMEM((3, SEQ, HALF), BF),
            pltpu.VMEM((SEQ, WIDE), F32),
            pltpu.VMEM((SEQ, WIDE), F32),
            pltpu.VMEM((SEQ, HALF), F32),
            pltpu.VMEM((SEQ, WIDE), BF),
            pltpu.VMEM((WIDE, SEQ), BF),
            pltpu.VMEM((4, SEQ, CHUNK), BF),
            pltpu.VMEM((4, SEQ, CHUNK), F32),
            pltpu.VMEM((SEQ, WIDE), F32),
            pltpu.VMEM((SEQ, WIDE), F32),
            pltpu.VMEM((SEQ, WIDE), BF),
            pltpu.VMEM((WIDE, SEQ), BF),
            pltpu.VMEM((SEQ, WIDE), BF),
            pltpu.VMEM((SEQ, WIDE), F32),
            pltpu.VMEM((2, WIDE, HALF), F32),
            pltpu.VMEM((WIDE, SEQ), BF),
            pltpu.VMEM((4, SEQ, CHUNK), BF),
            pltpu.VMEM((3, SEQ, HALF), BF),
            pltpu.VMEM((3, HALF, SEQ), BF),
            pltpu.VMEM((3, 3, HALF, SEQ), BF),
            pltpu.VMEM((2, WIDE, HALF), BF),
            pltpu.VMEM((WIDE, HALF), BF),
            pltpu.VMEM((WIDE, HALF), BF),
            pltpu.VMEM((4, ROWS, HALF), BF),
            pltpu.VMEM((WIDE, HALF), BF),
            pltpu.VMEM((4, ROWS, HALF), BF),
            pltpu.SemaphoreType.DMA((SEMS,)),
            pltpu.SemaphoreType.DMA((SEMS,)),
        ],
        compiler_params=pltpu.CompilerParams(
            collective_id=0, has_side_effects=True, vmem_limit_bytes=63 * 1024 * 1024
        ),
    )(
        segment_ids,
        tokens,
        cotangent,
        query_weight,
        key_weight,
        value_weight,
        out_weight.T,
        up_weight,
        down_weight.T,
        query_bias.reshape(1, CHUNK),
        value_bias.reshape(1, CHUNK),
        up_bias.reshape(4, 1, CHUNK),
        placed,
    )
    wide = grads.astype(F32)
    up_grad = wide[4:8].transpose(1, 0, 2).reshape(ROWS, 4 * CHUNK)
    down_grad = wide[8:12].transpose(0, 2, 1).reshape(4 * CHUNK, ROWS)
    slices = lax.dynamic_slice_in_dim(sums, z * ROWS, ROWS, 1)
    return (
        out,
        tgrad.astype(F32),
        wide[0],
        wide[1],
        wide[2],
        sums[0, :CHUNK],
        sums[0, CHUNK:],
        wide[3].T,
        slices[3],
        slices[4],
        slices[5],
        up_grad,
        sums[1:3].reshape(4 * CHUNK),
        down_grad,
        slices[6],
        slices[7],
        slices[8],
    )


def solution(mesh):
    placed = (
        P("row", ("dp", "col")),
        P(("dp", "row"), None),
        P("row", "col"),
        P("row", "col"),
        P("row", "col"),
        P("col"),
        P("col"),
        P("col", "row"),
        P("row"),
        P("row"),
        P("row"),
        P("row", "col"),
        P("col"),
        P("col", "row"),
        P("row"),
        P("row"),
        P("row"),
        P("row", ("dp", "col")),
    )
    return jax.shard_map(
        fused_body if small_grid(mesh) else body,
        mesh=mesh,
        in_specs=placed,
        out_specs=(
            P("row", ("dp", "col")),
            P("row", ("dp", "col")),
            P("row", "col"),
            P("row", "col"),
            P("row", "col"),
            P("col"),
            P("col"),
            P("col", "row"),
            P("row"),
            P("row"),
            P("row"),
            P("row", "col"),
            P("col"),
            P("col", "row"),
            P("row"),
            P("row"),
            P("row"),
        ),
        check_vma=False,
    )
```

```python
import math

import jax
import jax.numpy as jnp
from jax import lax
from jax.experimental import pallas as pl
from jax.experimental.pallas import tpu as pltpu
from jax.sharding import PartitionSpec as P

HEADS = 12
HEAD = 64


EPS = 1e-05


def gather_over_col(values):
    return lax.all_gather(values, "col", axis=0, tiled=True)


def gather_over_row(values):
    return lax.all_gather(values, "row", axis=0, tiled=True)


def contract(left, weight, flipped):
    if flipped:
        return lax.dot_general(
            left, weight, (((1,), (1,)), ((), ())), preferred_element_type=jnp.float32
        )
    return jnp.dot(left, weight, preferred_element_type=jnp.float32)


def product_rows(gathered, weight, flipped):
    return contract(gathered, weight, flipped)


def heads_in(values):
    return lax.all_to_all(values, "col", split_axis=0, concat_axis=1, tiled=True)


def heads_out(values):
    return lax.all_to_all(values, "col", split_axis=1, concat_axis=0, tiled=True)


def sum_over_row(gathered, block, flipped):
    return lax.psum_scatter(
        product_rows(gathered, block, flipped), "row", scatter_dimension=0, tiled=True
    )


def sum_over_col(gathered, block, flipped):
    return lax.psum_scatter(
        product_rows(gathered, block, flipped), "col", scatter_dimension=0, tiled=True
    )


def row_totals(values):
    return lax.psum(values, "row")


def layer_norm(resid, gain, shift):
    feature_count = resid.shape[1] * lax.axis_size("row")
    centre = row_totals((jnp.sum(resid, 1, keepdims=True),))[0] / feature_count
    deviate = resid - centre
    spread = row_totals((jnp.sum(deviate * deviate, 1, keepdims=True),))[0] / feature_count
    scaling = lax.rsqrt(spread + EPS)
    normed = deviate * scaling
    return (normed * gain + shift, normed, scaling)


def norm_backward(upstream, normed, scaling, gain):
    feature_count = upstream.shape[1] * lax.axis_size("row")
    scaled_grad = upstream * gain
    first_sum, second_sum = row_totals(
        (jnp.sum(scaled_grad, 1, keepdims=True), jnp.sum(scaled_grad * normed, 1, keepdims=True))
    )
    return scaling * (
        scaled_grad - first_sum / feature_count - normed * (second_sum / feature_count)
    )


def gelu_tanh(values):
    return jax.nn.gelu(values, approximate=True)


def column_sums(values):
    return jnp.sum(values, 0, dtype=jnp.float32)


def head_scores(query_split, key_split, same_doc):
    scores = jnp.einsum("qhd,khd->hqk", query_split, key_split, preferred_element_type=jnp.float32)
    scores = scores * (1.0 / math.sqrt(HEAD))
    return jnp.where(same_doc[None], scores, -1000000000.0)


def body(
    tokens,
    segment_ids,
    query_weight,
    key_weight,
    value_weight,
    query_bias,
    value_bias,
    out_weight,
    out_bias,
    attn_gain,
    attn_shift,
    up_weight,
    up_bias,
    down_weight,
    down_bias,
    ffn_gain,
    ffn_shift,
    cotangent,
):
    token_major = tokens.T
    head_cols = query_weight.shape[1]
    score_scale = 1.0 / math.sqrt(HEAD)
    joined_weight = jnp.concatenate([query_weight, key_weight, value_weight], 1)
    token_rows = gather_over_col(token_major)
    joined = sum_over_row(token_rows, joined_weight, False)
    query_block = (joined[:, :head_cols] + query_bias).astype(jnp.bfloat16)
    key_block = joined[:, head_cols : 2 * head_cols].astype(jnp.bfloat16)
    value_block = (joined[:, 2 * head_cols :] + value_bias).astype(jnp.bfloat16)
    query_heads = heads_in(query_block)
    key_heads, value_heads = (
        lax.all_gather(key_block, "col", axis=1, tiled=True),
        lax.all_gather(value_block, "col", axis=1, tiled=True),
    )
    query_count = query_heads.shape[0]
    key_count = key_heads.shape[0]
    sequence_ids = segment_ids[0]
    query_ids = lax.dynamic_slice_in_dim(
        sequence_ids, lax.axis_index("col") * query_count, query_count, 0
    )
    same_doc = query_ids[:, None] == sequence_ids[None, :]
    query_split = query_heads.reshape(query_count, HEADS, HEAD)
    key_split = key_heads.reshape(key_count, HEADS, HEAD)
    value_split = value_heads.reshape(key_count, HEADS, HEAD)
    scores = head_scores(query_split, key_split, same_doc)
    highest = jnp.max(scores, -1, keepdims=True)
    exponent = jnp.exp(scores - highest)
    totals = jnp.sum(exponent, -1, keepdims=True)
    log_totals = highest + jnp.log(totals)
    attn_probs = (exponent / totals).astype(jnp.bfloat16)
    attended = jnp.einsum(
        "hqk,khd->qhd", attn_probs, value_split, preferred_element_type=jnp.float32
    )
    attended = attended.reshape(query_count, -1).astype(jnp.bfloat16)
    attended_block = heads_out(attended)
    attended_rows = gather_over_row(attended_block)
    projected = sum_over_col(attended_rows, out_weight, False) + out_bias
    hidden, hidden_normed, hidden_scaling = layer_norm(
        token_major.astype(jnp.float32) + projected, attn_gain, attn_shift
    )
    hidden_low = hidden.astype(jnp.bfloat16)
    hidden_rows = gather_over_col(hidden_low)
    pre_act = sum_over_row(hidden_rows, up_weight, False) + up_bias
    activated, gelu_pull = jax.vjp(gelu_tanh, pre_act)
    act_block = activated.astype(jnp.bfloat16)
    act_rows = gather_over_row(act_block)
    down_out = sum_over_col(act_rows, down_weight, False) + down_bias
    output, out_normed, out_scaling = layer_norm(hidden + down_out, ffn_gain, ffn_shift)
    upstream = cotangent.T.astype(jnp.float32)
    ffn_gain_grad = jnp.sum(upstream * out_normed, 0)
    ffn_shift_grad = jnp.sum(upstream, 0)
    resid_grad = norm_backward(upstream, out_normed, out_scaling, ffn_gain)
    down_grad_rows = gather_over_col(resid_grad.astype(jnp.bfloat16))
    down_weight_grad = jnp.einsum(
        "tf,td->fd", act_rows, down_grad_rows, preferred_element_type=jnp.float32
    )
    down_bias_grad = column_sums(down_grad_rows)
    act_grad = sum_over_row(down_grad_rows, down_weight, True)
    pre_grad = gelu_pull(act_grad)[0].astype(jnp.bfloat16)
    pre_grad_rows = gather_over_row(pre_grad)
    up_weight_grad = jnp.einsum(
        "td,tf->df", hidden_rows, pre_grad_rows, preferred_element_type=jnp.float32
    )
    up_bias_grad = column_sums(pre_grad_rows)
    hidden_grad = sum_over_col(pre_grad_rows, up_weight, True) + resid_grad
    attn_gain_grad = jnp.sum(hidden_grad * hidden_normed, 0)
    attn_shift_grad = jnp.sum(hidden_grad, 0)
    first_grad = norm_backward(hidden_grad, hidden_normed, hidden_scaling, attn_gain)
    proj_grad_rows = gather_over_col(first_grad.astype(jnp.bfloat16))
    out_weight_grad = jnp.einsum(
        "tc,td->cd", attended_rows, proj_grad_rows, preferred_element_type=jnp.float32
    )
    out_bias_grad = column_sums(proj_grad_rows)
    attended_grad = heads_in(sum_over_row(proj_grad_rows, out_weight, True).astype(jnp.bfloat16))
    scores = head_scores(query_split, key_split, same_doc)
    attn_exact = jnp.exp(scores - log_totals)
    grad_split = attended_grad.reshape(query_count, HEADS, HEAD)
    prob_grad = jnp.einsum(
        "qhd,khd->hqk", grad_split, value_split, preferred_element_type=jnp.float32
    )
    score_grad = attn_exact * (prob_grad - jnp.sum(prob_grad * attn_exact, -1, keepdims=True))
    score_grad = score_grad.astype(jnp.bfloat16)
    query_grad = (
        jnp.einsum("hqk,khd->qhd", score_grad, key_split, preferred_element_type=jnp.float32)
        * score_scale
    )
    query_grad = query_grad.reshape(query_count, -1).astype(jnp.bfloat16)
    key_grad = (
        jnp.einsum("hqk,qhd->khd", score_grad, query_split, preferred_element_type=jnp.float32)
        * score_scale
    )
    key_grad = key_grad.reshape(key_count, -1)
    value_grad = jnp.einsum(
        "hqk,qhd->khd",
        attn_exact.astype(jnp.bfloat16),
        grad_split,
        preferred_element_type=jnp.float32,
    ).reshape(key_count, -1)
    key_sum, value_sum = (
        lax.psum_scatter(
            key_grad.astype(jnp.bfloat16), "col", scatter_dimension=1, tiled=True
        ).astype(jnp.float32),
        lax.psum_scatter(
            value_grad.astype(jnp.bfloat16), "col", scatter_dimension=1, tiled=True
        ).astype(jnp.float32),
    )
    joined_grad = jnp.concatenate(
        [heads_out(query_grad), key_sum.astype(jnp.bfloat16), value_sum.astype(jnp.bfloat16)], 1
    )
    joined_rows = gather_over_row(joined_grad)
    joined_weight_grad = jnp.einsum(
        "td,tf->df", token_rows, joined_rows, preferred_element_type=jnp.float32
    )
    query_bias_grad = column_sums(joined_rows[:, :head_cols])
    value_bias_grad = column_sums(joined_rows[:, 2 * head_cols :])
    tokens_grad = sum_over_col(joined_rows, joined_weight, True) + first_grad
    summed = lax.psum(
        (
            joined_weight_grad,
            query_bias_grad,
            value_bias_grad,
            out_weight_grad,
            out_bias_grad,
            up_weight_grad,
            up_bias_grad,
            down_weight_grad,
            down_bias_grad,
        ),
        "dp",
    )
    norm_sums = lax.psum(
        (attn_gain_grad, attn_shift_grad, ffn_gain_grad, ffn_shift_grad), ("dp", "col")
    )
    return (
        output.T.astype(jnp.bfloat16),
        tokens_grad.T,
        summed[0][:, :head_cols],
        summed[0][:, head_cols : 2 * head_cols],
        summed[0][:, 2 * head_cols :],
        summed[1],
        summed[2],
        summed[3],
        summed[4],
        norm_sums[0],
        norm_sums[1],
        summed[5],
        summed[6],
        summed[7],
        summed[8],
        norm_sums[2],
        norm_sums[3],
    )


MESH_ID = pl.DeviceIdType.MESH
BF = jnp.bfloat16
F32 = jnp.float32
GRID = {"dp": 4, "row": 4, "col": 2}
SEQ = 256
WIDE = 768
HALF = 128
ROWS = 192
CHUNK = 384
CHUNKS = 12
SEMS = 256
ORDER = (0, 3, 1, 2)


def small_grid(mesh):
    return dict(mesh.shape) == GRID


def mm(a, b):
    return jnp.dot(a, b, preferred_element_type=F32)


def mm_nt(a, b):
    return lax.dot_general(a, b, (((1,), (1,)), ((), ())), preferred_element_type=F32)


def loop(count, step):
    def wrapped(i, carry):
        step(i)
        return carry

    lax.fori_loop(0, count, wrapped, 0)


def row_mean(values):
    return jnp.sum(values, axis=1, keepdims=True) * (1.0 / WIDE)


def fold(values):
    return jnp.sum(values.reshape(values.shape[0] // 8, 8, values.shape[1]), axis=0)


def layer_kernel(
    ids,
    tok,
    cot,
    qw,
    kw,
    vw,
    ow,
    uw,
    dw,
    qb,
    vb,
    ub,
    own_vec,
    fin_out,
    res_out,
    tg_out,
    vec_out,
    W,
    G,
    R1,
    R2,
    RZ,
    fin,
    xin,
    cin,
    xs,
    xr,
    vg,
    vec,
    VA,
    VB,
    VC,
    VD,
    VZ,
    xf,
    cf,
    neq,
    q,
    k,
    v,
    qT,
    kT,
    P,
    at,
    hid,
    n1,
    s1,
    hb,
    hT,
    act,
    dact,
    outf,
    r2g,
    dg,
    dgT,
    pg,
    fg,
    fgT,
    pgT,
    prg,
    dA,
    dAT,
    dT,
    tgp,
    tgr,
    osend,
    obuf,
    tsend,
    tbuf,
    send,
    recv,
):
    dp = lax.axis_index("dp")
    z = lax.axis_index("row")
    x = lax.axis_index("col")
    core = lax.rem(dp, 2)
    y = lax.div(dp, 2)
    mate = dp + 1 - 2 * core
    far = lax.rem(dp + 2, 4)
    matefar = lax.rem(mate + 2, 4)
    other = 1 - x
    counts = {"s": 0, "r": 0}
    pending = []

    def new(kind, n=1):
        base = counts[kind]
        counts[kind] = base + n
        assert counts[kind] <= SEMS
        return base

    def push(src, dst, ssem, rsem, **where):
        return pltpu.make_async_remote_copy(
            src_ref=src,
            dst_ref=dst,
            send_sem=send.at[ssem],
            recv_sem=recv.at[rsem],
            device_id=where,
            device_id_type=MESH_ID,
        )

    def start(pred, make):
        if pred is None:
            make().start()
        else:

            @pl.when(pred)
            def _():
                make().start()

        pending.append((pred, make))

    def arrived(dst, rsem, **where):
        push(dst, dst, 0, rsem, **where).wait_recv()

    def rows(b):
        return pl.ds(pl.multiple_of(b * ROWS, ROWS), ROWS)

    bar = pltpu.get_barrier_semaphore()
    for j in range(4):
        for h in range(2):

            @pl.when((z != j) | (x != h))
            def _(j=j, h=h):
                pl.semaphore_signal(bar, inc=1, device_id={"row": j, "col": h}, device_id_type=MESH_ID)

    pl.semaphore_signal(bar, inc=1, device_id={"dp": mate}, device_id_type=MESH_ID)
    pl.semaphore_signal(bar, inc=1, device_id={"dp": far}, device_id_type=MESH_ID)

    lsem = new("s", CHUNKS)
    mine = rows(z)

    def local_parts():
        parts = []
        for j, ref in enumerate((qw, kw, vw, ow)):
            parts.append((ref, W.at[j, mine]))
        for i in range(4):
            parts.append((uw.at[:, i * CHUNK : (i + 1) * CHUNK], W.at[4 + i, mine]))
        for i in range(4):
            parts.append((dw.at[:, i * CHUNK : (i + 1) * CHUNK], W.at[8 + i, mine]))
        return [pltpu.make_async_copy(a, b, send.at[lsem + n]) for n, (a, b) in enumerate(parts)]

    locals_ = local_parts()
    for c in locals_:
        c.start()
    vg[z] = own_vec[...]
    seg = jnp.broadcast_to(ids[...].astype(F32), (SEQ, SEQ))
    neq[...] = jnp.abs(seg - seg.T)
    pl.semaphore_wait(bar, 9)

    def spread(ref, landing):
        ssem, rsem = new("s", 4), new("r", 4)
        for s in range(2):
            for h in range(2):
                jj = 2 * x + s
                self_ = (jj == z) & (h == x)
                src = ref.at[:, s * SEQ + h * HALF : s * SEQ + (h + 1) * HALF]
                dst = landing.at[h, mine]
                start(
                    jnp.logical_not(self_),
                    lambda src=src, dst=dst, n=2 * s + h, jj=jj, h=h: push(
                        src, dst, ssem + n, rsem + z, row=jj, col=h
                    ),
                )

                @pl.when(self_)
                def _(src=src, dst=dst):
                    pltpu.make_async_copy(src, dst, recv.at[rsem + z]).start()

        def collect():
            home = lax.div(z, 2) == x
            for b in range(4):
                local = home & (z == b)
                dst = landing.at[x, rows(b)]

                @pl.when(local)
                def _(dst=dst, b=b):
                    pltpu.make_async_copy(ref.at[:, 0:HALF], dst, recv.at[rsem + b]).wait()

                @pl.when(jnp.logical_not(local))
                def _(dst=dst, b=b):
                    arrived(dst, rsem + b, col=other)

        return collect

    def swap(landing):
        ssem, rsem = new("s"), new("r")
        start(None, lambda: push(landing.at[x], landing.at[x], ssem, rsem, col=other))

        def collect():
            arrived(landing.at[other], rsem, col=other)

        return collect

    def share_vec():
        ssem, rsem = new("s", 3), new("r", 4)
        for o in range(1, 4):
            to = lax.rem(z + o, 4)
            start(None, lambda o=o, to=to: push(own_vec, vg.at[z], ssem + o - 1, rsem + z, row=to))

        def collect():
            for o in range(1, 4):
                b = lax.rem(z + o, 4)
                arrived(vg.at[b], rsem + b, row=b)
            vec[...] = vg[0] + vg[1] + vg[2] + vg[3]

        return collect

    def gather(g):
        zs, ys, cs = new("s", 5), new("s", 4), new("s", 8)
        zr, yr, cr = new("r", 4), new("r", 4), new("r", 8)
        own, ychunk = 4 * g + dp, 4 * g + far

        def block(chunk, b):
            return W.at[chunk, rows(b)]

        def along(n, b, to, pred):
            start(pred, lambda: push(block(own, b), block(own, b), zs + n, zr + b, row=to))

        def first():
            along(0, z, z + 1, (z < 3) if g == 0 else (z < 2))
            along(1, z, z - 1, (z > 0) if g == 0 else (z > 1))
            along(2, z, z + 2, z < 2)
            along(3, z, z - 2, z > 1)

        def late():
            along(0, z, z + 1, z == 2)
            along(1, z, z - 1, z == 1)

        def take(b, pred):
            @pl.when(pred)
            def _():
                arrived(block(own, b), zr + b, row=b)

            start(pred, lambda: push(block(own, b), block(own, b), ys + b, yr + b, dp=far))
            start(pred, lambda: push(block(own, b), block(own, b), cs + b, cr + b, dp=mate))

        def hop1():
            for b in range(4):
                take(b, (z == b - 1) | (z == b + 1))

        def hop2():
            for b, at_ in ((0, 2), (3, 1)):

                @pl.when(z == at_)
                def _(b=b):
                    arrived(block(own, b), zr + b, row=b)

                along(4, b, 3 - b, z == at_)
                start(z == at_, lambda b=b: push(block(own, b), block(own, b), ys + b, yr + b, dp=far))
                start(z == at_, lambda b=b: push(block(own, b), block(own, b), cs + b, cr + b, dp=mate))
            if g < 2:
                gathers[g + 1][1]()
            take(2, z == 0)
            take(1, z == 3)

        def hop3():
            take(3, z == 0)
            take(0, z == 3)

        def across():
            for b in range(4):
                there = z != b

                @pl.when(there)
                def _(b=b):
                    arrived(block(ychunk, b), yr + b, dp=far)

                start(
                    there,
                    lambda b=b: push(block(ychunk, b), block(ychunk, b), cs + 4 + b, cr + 4 + b, dp=mate),
                )

        def finish():
            for b in range(4):

                @pl.when(z != b)
                def _(b=b):
                    arrived(block(4 * g + mate, b), cr + b, dp=mate)
                    arrived(block(4 * g + matefar, b), cr + 4 + b, dp=mate)

        return first, late, hop1, hop2, hop3, across, finish

    def exchange(n):
        ssem, rsem = new("s", 3), new("r", 3)

        def put(c, value):
            xs[n, c] = value.astype(BF)
            start(None, lambda: push(xs.at[n, c], xr.at[n, c], ssem + c, rsem + c, col=other))

        def collect():
            for c in range(3):
                arrived(xr.at[n, c], rsem + c, col=other)

        return put, collect

    def both(n, r):
        own = [xs[n, c, r, :].astype(F32) + xr[n, c, r, :].astype(F32) for c in range(3)]
        return jnp.concatenate(own, axis=1)

    def reduce(g):
        s1_, s2_, sz, sy, sc = new("s", 2), new("s", 4), new("s", 4), new("s"), new("s", 2)
        r1, r2, rz, ry, rc = new("r", 2), new("r", 4), new("r", 4), new("r"), new("r", 2)
        own, ychunk = 4 * g + dp, 4 * g + far

        def to_core():
            for j in range(2):
                src = G.at[4 * g + 2 * j + 1 - core]
                start(None, lambda src=src, j=j: push(src, R1.at[g, j], s1_ + j, r1 + j, dp=mate))

        def add(chunk, extra, base, count):
            def step(i):
                at_ = pl.ds(pl.multiple_of(base + i * 64, 64), 64)
                G[chunk, at_, :] = (G[chunk, at_, :].astype(F32) + extra[at_, :].astype(F32)).astype(BF)

            loop(count // 64, step)

        def piece(ref, b):
            return ref.at[pl.ds(b * ROWS, ROWS)]

        def to_y():
            arrived(R1.at[g, 1 - y], r1 + 1 - y, dp=mate)
            for b in ORDER:
                add(ychunk, R1.at[g, 1 - y], b * ROWS, ROWS)
                start(
                    None,
                    lambda b=b: push(piece(G.at[ychunk], b), piece(R2.at[g], b), s2_ + b, r2 + b, dp=far),
                )
            arrived(R1.at[g, y], r1 + y, dp=mate)
            add(own, R1.at[g, y], 0, WIDE)

        def take(b):
            arrived(piece(R2.at[g], b), r2 + b, dp=far)
            add(own, R2.at[g], b * ROWS, ROWS)
            start(z != b, lambda: push(piece(G.at[own], b), RZ.at[g, z], sz + b, rz + z, row=b))

        def settle():
            for o in range(1, 4):
                b = lax.rem(z + o, 4)
                arrived(RZ.at[g, b], rz + b, row=b)
            RZ[g, z] = G[own, mine, :]

            def step(i):
                at_ = pl.ds(pl.multiple_of(i * 32, 32), 32)
                part = [RZ[g, b, at_, :].astype(F32) for b in range(4)]
                fin[own, at_, :] = ((part[0] + part[1]) + (part[2] + part[3])).astype(BF)

            loop(ROWS // 32, step)
            start(None, lambda: push(fin.at[own], fin.at[own], sy, ry, dp=far))
            start(None, lambda: push(fin.at[own], fin.at[own], sc, rc, dp=mate))

        def across():
            arrived(fin.at[ychunk], ry, dp=far)
            start(None, lambda: push(fin.at[ychunk], fin.at[ychunk], sc + 1, rc + 1, dp=mate))

        def finish():
            arrived(fin.at[4 * g + mate], rc, dp=mate)
            arrived(fin.at[4 * g + matefar], rc + 1, dp=mate)

        return to_core, to_y, take, settle, across, finish

    def deliver(sent, landed, out):
        ssem, rsem = new("s", 4), new("r", 4)
        slot = 2 * lax.rem(z, 2) + x
        home = lax.div(z, 2) == x
        for b in range(4):
            self_ = home & (z == b)
            start(
                jnp.logical_not(self_),
                lambda b=b: push(
                    sent.at[rows(b)], landed.at[slot], ssem + b, rsem + slot, row=b, col=lax.div(z, 2)
                ),
            )

            @pl.when(self_)
            def _(b=b):
                pltpu.make_async_copy(sent.at[rows(b)], landed.at[slot], recv.at[rsem + slot]).start()

        def collect():
            osem = new("s", 4)
            copies = []
            for n in range(4):
                s, h = n // 2, n % 2
                local = (2 * x + s == z) & (h == x)

                @pl.when(local)
                def _(n=n):
                    pltpu.make_async_copy(sent.at[rows(z)], landed.at[n], recv.at[rsem + n]).wait()

                @pl.when(jnp.logical_not(local))
                def _(n=n):
                    arrived(landed.at[n], rsem + n, col=other)

                copies.append(
                    pltpu.make_async_copy(
                        landed.at[n], out.at[:, n * HALF : (n + 1) * HALF], send.at[osem + n]
                    )
                )
                copies[-1].start()
            return copies

        return collect

    tok_in = spread(tok, xin)
    vec_in = share_vec()
    gathers = [gather(g) for g in range(3)]
    for c in locals_:
        c.wait()
    for g in range(3):
        gathers[g][0]()
    cot_in = spread(cot, cin)
    gathers[0][2]()
    tok_in()
    tok_swap = swap(xin)
    gathers[0][3]()
    gathers[0][4]()
    vec_in()
    tok_swap()
    for h in range(2):
        xf[h * HALF : (h + 1) * HALF, :] = xin[h].astype(F32).T
    gathers[0][5]()
    gathers[0][6]()

    xb = xf[...].astype(BF)
    for j, (dst, bias) in enumerate(((q, qb), (k, None), (v, vb))):
        r = mm(xb, W[j])
        if bias is not None:
            r = r + bias[...]
        for p in range(3):
            dst[p] = r[:, p * HALF : (p + 1) * HALF].astype(BF)

    lane = lax.broadcasted_iota(jnp.int32, (SEQ, HALF), 1) < HEAD
    scale = 1.0 / math.sqrt(HEAD)

    def only(values, hh):
        keep = lane if hh == 0 else jnp.logical_not(lane)
        return jnp.where(keep, values.astype(F32), 0.0).astype(BF)

    def attend(p):
        qv, kv, vv = q[p], k[p], v[p]
        outs = []
        for hh in range(2):
            s = mm_nt(only(qv, hh), kv) * scale
            s = jnp.where(neq[...] == 0.0, s, -1000000000.0)
            e = jnp.exp(s - jnp.max(s, axis=1, keepdims=True))
            pr = e / jnp.sum(e, axis=1, keepdims=True)
            P[2 * p + hh] = pr
            outs.append(mm(pr.astype(BF), vv))
        at[p] = jnp.where(lane, outs[0], outs[1]).astype(BF)

    gathers[1][2]()
    loop(3, attend)
    gathers[1][3]()

    put0, get0 = exchange(0)
    att = jnp.concatenate([at[0], at[1], at[2]], axis=1)
    for c in range(3):
        put0(c, mm_nt(att, W[3, c * SEQ : (c + 1) * SEQ, :]))
    gathers[1][4]()
    for p in range(3):
        qT[p] = q[p].astype(F32).T.astype(BF)
        kT[p] = k[p].astype(F32).T.astype(BF)
    gathers[1][5]()
    gathers[2][2]()
    gathers[2][3]()
    get0()

    def norm1(i):
        r = pl.ds(pl.multiple_of(i * 32, 32), 32)
        resid = xf[r, :] + (both(0, r) + vec[0:1, :])
        d = resid - row_mean(resid)
        s = lax.rsqrt(row_mean(d * d) + EPS)
        n = d * s
        h = n * vec[1:2, :] + vec[2:3, :]
        n1[r, :] = n
        s1[r, :] = jnp.broadcast_to(s, (32, HALF))
        hid[r, :] = h
        hb[r, :] = h.astype(BF)

    loop(8, norm1)
    gathers[1][6]()

    hv = hb[...]
    c0 = math.sqrt(2.0 / math.pi)

    def up_step(i):
        u = mm(hv, W[4 + i]) + ub[i]
        u2 = u * u
        t = jnp.tanh(c0 * (u + 0.044715 * (u2 * u)))
        half = 0.5 * (1.0 + t)
        act[i] = (u * half).astype(BF)
        dact[i] = half + (0.5 * u) * (1.0 - t * t) * (c0 * (1.0 + (3 * 0.044715) * u2))

    loop(4, up_step)
    gathers[2][4]()
    cot_in()
    cot_swap = swap(cin)
    gathers[2][5]()
    hT[...] = hid[...].T.astype(BF)
    gathers[2][6]()
    put1, get1 = exchange(1)
    for c in range(3):
        acc = mm_nt(act[0], W[8, c * SEQ : (c + 1) * SEQ, :])
        for i in range(1, 4):
            acc = acc + mm_nt(act[i], W[8 + i, c * SEQ : (c + 1) * SEQ, :])
        put1(c, acc)
    cot_swap()
    for h in range(2):
        cf[h * HALF : (h + 1) * HALF, :] = cin[h].astype(F32).T
    get1()

    VA[...] = jnp.zeros_like(VA)

    def norm2(i, carry):
        gain_sum, shift_sum, bias_sum = carry
        r = pl.ds(pl.multiple_of(i * 32, 32), 32)
        resid = hid[r, :] + (both(1, r) + vec[3:4, :])
        d = resid - row_mean(resid)
        s = lax.rsqrt(row_mean(d * d) + EPS)
        n = d * s
        outf[r, :] = n * vec[4:5, :] + vec[5:6, :]
        up = cf[r, :]
        e = up * vec[4:5, :]
        grad = s * (e - row_mean(e) - n * row_mean(e * n))
        low = grad.astype(BF)
        r2g[r, :] = grad
        dg[r, :] = low
        return gain_sum + fold(up * n), shift_sum + fold(up), bias_sum + fold(low.astype(F32))

    zero = jnp.zeros((8, WIDE), F32)
    sums = lax.fori_loop(0, 8, norm2, (zero, zero, zero))

    def total(values):
        return jnp.sum(values, axis=0, keepdims=True)

    VA[7:8, :] = total(sums[0])
    VA[8:9, :] = total(sums[1])
    VA[6:7, :] = total(sums[2])
    dgT[...] = r2g[...].T.astype(BF)
    reduces = [reduce(g) for g in range(3)]

    def outer(dst, left, right):
        def step(b):
            r = pl.ds(pl.multiple_of(b * SEQ, SEQ), SEQ)
            G[dst, r, :] = mm(left[r, :], right).astype(BF)

        loop(3, step)

    loop(4, lambda i: outer(8 + i, dgT, act[i]))
    reduces[2][0]()

    ones = jnp.ones((8, SEQ), BF)
    dgv = dg[...]

    def pre_step(i):
        low = (mm(dgv, W[8 + i]) * dact[i]).astype(BF)
        prg[i] = low

    loop(4, pre_step)
    reduces[2][1]()
    put2, get2 = exchange(2)
    for c in range(3):
        acc = mm_nt(prg[0], W[4, c * SEQ : (c + 1) * SEQ, :])
        for i in range(1, 4):
            acc = acc + mm_nt(prg[i], W[4 + i, c * SEQ : (c + 1) * SEQ, :])
        put2(c, acc)
    for i in range(4):
        VA[1 + i // 2 : 2 + i // 2, (i % 2) * CHUNK : (i % 2 + 1) * CHUNK] = mm(ones, prg[i])[0:1, :]
    loop(4, lambda i: outer(4 + i, hT, prg[i]))
    reduces[1][0]()
    reduces[2][2](ORDER[0])

    mine_tokens = pl.ds(pl.multiple_of(x * HALF, HALF), HALF)
    osend[...] = outf[mine_tokens, :].T.astype(BF)
    out_in = deliver(osend, obuf, res_out)
    reduces[2][2](ORDER[1])
    reduces[1][1]()
    get2()

    def norm1_back(i, carry):
        gain_sum, shift_sum, bias_sum = carry
        r = pl.ds(pl.multiple_of(i * 32, 32), 32)
        up = r2g[r, :] + both(2, r)
        n = n1[r, :]
        s = s1[r, :][:, 0:1]
        e = up * vec[1:2, :]
        grad = s * (e - row_mean(e) - n * row_mean(e * n))
        low = grad.astype(BF)
        fg[r, :] = grad
        pg[r, :] = low
        return gain_sum + fold(up * n), shift_sum + fold(up), bias_sum + fold(low.astype(F32))

    sums = lax.fori_loop(0, 8, norm1_back, (zero, zero, zero))
    VA[4:5, :] = total(sums[0])
    VA[5:6, :] = total(sums[1])
    VA[3:4, :] = total(sums[2])
    for h in range(2):
        t = fg[h * HALF : (h + 1) * HALF, :].T
        fgT[h] = t
        pgT[:, h * HALF : (h + 1) * HALF] = t.astype(BF)

    reduces[2][2](ORDER[2])
    reduces[2][2](ORDER[3])
    r = mm(pg[...], W[3])
    for p in range(3):
        part = r[:, p * HALF : (p + 1) * HALF].astype(BF)
        dA[p] = part
        dAT[p] = part.astype(F32).T.astype(BF)
    outer(3, pgT, att)

    top = lax.broadcasted_iota(jnp.int32, (HALF, SEQ), 0) < HEAD

    def attend_back(p):
        dAv, vv = dA[p], v[p]
        dq, dk, dv = [], [], []
        for hh in range(2):
            pr = P[2 * p + hh]
            pgrad = mm_nt(only(dAv, hh), vv)
            ds = (pr * (pgrad - jnp.sum(pgrad * pr, axis=1, keepdims=True))).astype(BF)
            dq.append(mm_nt(kT[p], ds))
            dk.append(mm(qT[p], ds))
            dv.append(mm(dAT[p], pr.astype(BF)))
        dT[0, p] = (jnp.where(top, dq[0], dq[1]) * scale).astype(BF)
        dT[1, p] = (jnp.where(top, dk[0], dk[1]) * scale).astype(BF)
        dT[2, p] = jnp.where(top, dv[0], dv[1]).astype(BF)

    loop(3, attend_back)
    reduces[1][2](ORDER[0])

    for j in range(3):
        t = dT[j].reshape(CHUNK, SEQ)
        if j != 1:
            at_ = 0 if j == 0 else CHUNK
            VA[0:1, at_ : at_ + CHUNK] = mm_nt(ones, t)[0:1, :]

        def step(b, t=t, j=j):
            r = pl.ds(pl.multiple_of(b * SEQ, SEQ), SEQ)
            left = jnp.concatenate([xin[0, r, :], xin[1, r, :]], axis=1)
            G[j, r, :] = mm_nt(left, t).astype(BF)

        loop(3, step)
    reduces[0][0]()
    vs, vr = new("s", 5), new("r", 6)
    start(None, lambda: push(VA, VB, vs, vr, dp=mate))

    def back_step(b):
        r = pl.ds(pl.multiple_of(b * SEQ, SEQ), SEQ)
        acc = mm(W[0, r, :], dT[0].reshape(CHUNK, SEQ))
        acc = acc + mm(W[1, r, :], dT[1].reshape(CHUNK, SEQ))
        acc = acc + mm(W[2, r, :], dT[2].reshape(CHUNK, SEQ))
        tgp[0, r, :] = acc[:, :HALF].astype(BF)
        tgp[1, r, :] = acc[:, HALF:].astype(BF)

    loop(3, back_step)
    ts, tr = new("s"), new("r")
    start(None, lambda: push(tgp.at[other], tgr, ts, tr, col=other))
    arrived(VB, vr, dp=mate)
    VD[...] = VA[...] + VB[...]
    start(None, lambda: push(VD, VC, vs + 1, vr + 1, dp=far))
    reduces[2][3]()
    reduces[0][1]()
    reduces[1][2](ORDER[1])
    arrived(tgr, tr, col=other)
    tsend[...] = (tgp[x].astype(F32) + tgr[...].astype(F32) + fgT[x]).astype(BF)
    tg_in = deliver(tsend, tbuf, tg_out)
    reduces[1][2](ORDER[2])
    reduces[1][2](ORDER[3])
    arrived(VC, vr + 1, dp=far)
    VZ[z] = VD[...] + VC[...]
    for o in range(1, 4):
        to = lax.rem(z + o, 4)
        start(None, lambda o=o, to=to: push(VZ.at[z], VZ.at[z], vs + 1 + o, vr + 2 + z, row=to))
    reduces[2][4]()
    reduces[0][2](ORDER[0])
    reduces[1][3]()
    reduces[0][2](ORDER[1])
    reduces[0][2](ORDER[2])
    reduces[0][2](ORDER[3])
    reduces[2][5]()
    reduces[1][4]()
    reduces[0][3]()
    reduces[1][5]()
    copies = []
    fsem = new("s", 3)

    def flush(g):
        c = pltpu.make_async_copy(
            fin.at[4 * g : 4 * g + 4], fin_out.at[4 * g : 4 * g + 4], send.at[fsem + g]
        )
        c.start()
        copies.append(c)

    flush(2)
    flush(1)
    for o in range(1, 4):
        b = lax.rem(z + o, 4)
        arrived(VZ.at[b], vr + 2 + b, row=b)
    vec_out[...] = VZ[0] + VZ[1] + VZ[2] + VZ[3]
    copies += out_in()
    copies += tg_in()
    reduces[0][4]()
    reduces[0][5]()
    flush(0)
    for pred, make in pending:
        if pred is None:
            make().wait_send()
        else:

            @pl.when(pred)
            def _(make=make):
                make().wait_send()

    for c in copies:
        c.wait()


def fused_body(
    tokens,
    segment_ids,
    query_weight,
    key_weight,
    value_weight,
    query_bias,
    value_bias,
    out_weight,
    out_bias,
    attn_gain,
    attn_shift,
    up_weight,
    up_bias,
    down_weight,
    down_bias,
    ffn_gain,
    ffn_shift,
    cotangent,
):
    z = lax.axis_index("row")
    vectors = jnp.stack([out_bias, attn_gain, attn_shift, down_bias, ffn_gain, ffn_shift])
    vectors = jnp.pad(vectors, ((0, 2), (0, 0)))
    placed = jnp.concatenate(
        [jnp.where(z == b, vectors, 0.0) for b in range(4)], axis=1
    )
    hbm = pl.BlockSpec(memory_space=pl.ANY)
    vmem = pl.BlockSpec(memory_space=pltpu.VMEM)
    grads, out, tgrad, sums = pl.pallas_call(
        layer_kernel,
        out_shape=(
            jax.ShapeDtypeStruct((CHUNKS, ROWS, CHUNK), BF),
            jax.ShapeDtypeStruct((ROWS, 2 * SEQ), BF),
            jax.ShapeDtypeStruct((ROWS, 2 * SEQ), BF),
            jax.ShapeDtypeStruct((16, WIDE), F32),
        ),
        in_specs=[vmem] + [hbm] * 8 + [vmem] * 4,
        out_specs=(hbm, hbm, hbm, vmem),
        scratch_shapes=[
            pltpu.VMEM((CHUNKS, WIDE, CHUNK), BF),
            pltpu.VMEM((CHUNKS, WIDE, CHUNK), BF),
            pltpu.VMEM((3, 2, WIDE, CHUNK), BF),
            pltpu.VMEM((3, WIDE, CHUNK), BF),
            pltpu.VMEM((3, 4, ROWS, CHUNK), BF),
            pltpu.VMEM((CHUNKS, ROWS, CHUNK), BF),
            pltpu.VMEM((2, WIDE, HALF), BF),
            pltpu.VMEM((2, WIDE, HALF), BF),
            pltpu.VMEM((3, 3, SEQ, SEQ), BF),
            pltpu.VMEM((3, 3, SEQ, SEQ), BF),
            pltpu.VMEM((4, 8, WIDE), F32),
            pltpu.VMEM((8, WIDE), F32),
            pltpu.VMEM((16, WIDE), F32),
            pltpu.VMEM((16, WIDE), F32),
            pltpu.VMEM((16, WIDE), F32),
            pltpu.VMEM((16, WIDE), F32),
            pltpu.VMEM((4, 16, WIDE), F32),
            pltpu.VMEM((SEQ, WIDE), F32),
            pltpu.VMEM((SEQ, WIDE), F32),
            pltpu.VMEM((SEQ, SEQ), F32),
            pltpu.VMEM((3, SEQ, HALF), BF),
            pltpu.VMEM((3, SEQ, HALF), BF),
            pltpu.VMEM((3, SEQ, HALF), BF),
            pltpu.VMEM((3, HALF, SEQ), BF),
            pltpu.VMEM((3, HALF, SEQ), BF),
            pltpu.VMEM((6, SEQ, SEQ), F32),
            pltpu.VMEM((3, SEQ, HALF), BF),
            pltpu.VMEM((SEQ, WIDE), F32),
            pltpu.VMEM((SEQ, WIDE), F32),
            pltpu.VMEM((SEQ, HALF), F32),
            pltpu.VMEM((SEQ, WIDE), BF),
            pltpu.VMEM((WIDE, SEQ), BF),
            pltpu.VMEM((4, SEQ, CHUNK), BF),
            pltpu.VMEM((4, SEQ, CHUNK), F32),
            pltpu.VMEM((SEQ, WIDE), F32),
            pltpu.VMEM((SEQ, WIDE), F32),
            pltpu.VMEM((SEQ, WIDE), BF),
            pltpu.VMEM((WIDE, SEQ), BF),
            pltpu.VMEM((SEQ, WIDE), BF),
            pltpu.VMEM((SEQ, WIDE), F32),
            pltpu.VMEM((2, WIDE, HALF), F32),
            pltpu.VMEM((WIDE, SEQ), BF),
            pltpu.VMEM((4, SEQ, CHUNK), BF),
            pltpu.VMEM((3, SEQ, HALF), BF),
            pltpu.VMEM((3, HALF, SEQ), BF),
            pltpu.VMEM((3, 3, HALF, SEQ), BF),
            pltpu.VMEM((2, WIDE, HALF), BF),
            pltpu.VMEM((WIDE, HALF), BF),
            pltpu.VMEM((WIDE, HALF), BF),
            pltpu.VMEM((4, ROWS, HALF), BF),
            pltpu.VMEM((WIDE, HALF), BF),
            pltpu.VMEM((4, ROWS, HALF), BF),
            pltpu.SemaphoreType.DMA((SEMS,)),
            pltpu.SemaphoreType.DMA((SEMS,)),
        ],
        compiler_params=pltpu.CompilerParams(
            collective_id=0, has_side_effects=True, vmem_limit_bytes=63 * 1024 * 1024
        ),
    )(
        segment_ids,
        tokens,
        cotangent,
        query_weight,
        key_weight,
        value_weight,
        out_weight.T,
        up_weight,
        down_weight.T,
        query_bias.reshape(1, CHUNK),
        value_bias.reshape(1, CHUNK),
        up_bias.reshape(4, 1, CHUNK),
        placed,
    )
    wide = grads.astype(F32)
    up_grad = wide[4:8].transpose(1, 0, 2).reshape(ROWS, 4 * CHUNK)
    down_grad = wide[8:12].transpose(0, 2, 1).reshape(4 * CHUNK, ROWS)
    slices = lax.dynamic_slice_in_dim(sums, z * ROWS, ROWS, 1)
    return (
        out,
        tgrad.astype(F32),
        wide[0],
        wide[1],
        wide[2],
        sums[0, :CHUNK],
        sums[0, CHUNK:],
        wide[3].T,
        slices[3],
        slices[4],
        slices[5],
        up_grad,
        sums[1:3].reshape(4 * CHUNK),
        down_grad,
        slices[6],
        slices[7],
        slices[8],
    )


def solution(mesh):
    placed = (
        P("row", ("dp", "col")),
        P(("dp", "row"), None),
        P("row", "col"),
        P("row", "col"),
        P("row", "col"),
        P("col"),
        P("col"),
        P("col", "row"),
        P("row"),
        P("row"),
        P("row"),
        P("row", "col"),
        P("col"),
        P("col", "row"),
        P("row"),
        P("row"),
        P("row"),
        P("row", ("dp", "col")),
    )
    return jax.shard_map(
        fused_body if small_grid(mesh) else body,
        mesh=mesh,
        in_specs=placed,
        out_specs=(
            P("row", ("dp", "col")),
            P("row", ("dp", "col")),
            P("row", "col"),
            P("row", "col"),
            P("row", "col"),
            P("col"),
            P("col"),
            P("col", "row"),
            P("row"),
            P("row"),
            P("row"),
            P("row", "col"),
            P("col"),
            P("col", "row"),
            P("row"),
            P("row"),
            P("row"),
        ),
        check_vma=False,
    )
```

```python
import math

import jax
import jax.numpy as jnp
from jax import lax
from jax.experimental import pallas as pl
from jax.experimental.pallas import tpu as pltpu
from jax.sharding import PartitionSpec as P

HEADS = 12
HEAD = 64


EPS = 1e-05


def gather_over_col(values):
    return lax.all_gather(values, "col", axis=0, tiled=True)


def gather_over_row(values):
    return lax.all_gather(values, "row", axis=0, tiled=True)


def contract(left, weight, flipped):
    if flipped:
        return lax.dot_general(
            left, weight, (((1,), (1,)), ((), ())), preferred_element_type=jnp.float32
        )
    return jnp.dot(left, weight, preferred_element_type=jnp.float32)


def product_rows(gathered, weight, flipped):
    return contract(gathered, weight, flipped)


def heads_in(values):
    return lax.all_to_all(values, "col", split_axis=0, concat_axis=1, tiled=True)


def heads_out(values):
    return lax.all_to_all(values, "col", split_axis=1, concat_axis=0, tiled=True)


def sum_over_row(gathered, block, flipped):
    return lax.psum_scatter(
        product_rows(gathered, block, flipped), "row", scatter_dimension=0, tiled=True
    )


def sum_over_col(gathered, block, flipped):
    return lax.psum_scatter(
        product_rows(gathered, block, flipped), "col", scatter_dimension=0, tiled=True
    )


def row_totals(values):
    return lax.psum(values, "row")


def layer_norm(resid, gain, shift):
    feature_count = resid.shape[1] * lax.axis_size("row")
    centre = row_totals((jnp.sum(resid, 1, keepdims=True),))[0] / feature_count
    deviate = resid - centre
    spread = row_totals((jnp.sum(deviate * deviate, 1, keepdims=True),))[0] / feature_count
    scaling = lax.rsqrt(spread + EPS)
    normed = deviate * scaling
    return (normed * gain + shift, normed, scaling)


def norm_backward(upstream, normed, scaling, gain):
    feature_count = upstream.shape[1] * lax.axis_size("row")
    scaled_grad = upstream * gain
    first_sum, second_sum = row_totals(
        (jnp.sum(scaled_grad, 1, keepdims=True), jnp.sum(scaled_grad * normed, 1, keepdims=True))
    )
    return scaling * (
        scaled_grad - first_sum / feature_count - normed * (second_sum / feature_count)
    )


def gelu_tanh(values):
    return jax.nn.gelu(values, approximate=True)


def column_sums(values):
    return jnp.sum(values, 0, dtype=jnp.float32)


def head_scores(query_split, key_split, same_doc):
    scores = jnp.einsum("qhd,khd->hqk", query_split, key_split, preferred_element_type=jnp.float32)
    scores = scores * (1.0 / math.sqrt(HEAD))
    return jnp.where(same_doc[None], scores, -1000000000.0)


def body(
    tokens,
    segment_ids,
    query_weight,
    key_weight,
    value_weight,
    query_bias,
    value_bias,
    out_weight,
    out_bias,
    attn_gain,
    attn_shift,
    up_weight,
    up_bias,
    down_weight,
    down_bias,
    ffn_gain,
    ffn_shift,
    cotangent,
):
    token_major = tokens.T
    head_cols = query_weight.shape[1]
    score_scale = 1.0 / math.sqrt(HEAD)
    joined_weight = jnp.concatenate([query_weight, key_weight, value_weight], 1)
    token_rows = gather_over_col(token_major)
    joined = sum_over_row(token_rows, joined_weight, False)
    query_block = (joined[:, :head_cols] + query_bias).astype(jnp.bfloat16)
    key_block = joined[:, head_cols : 2 * head_cols].astype(jnp.bfloat16)
    value_block = (joined[:, 2 * head_cols :] + value_bias).astype(jnp.bfloat16)
    query_heads = heads_in(query_block)
    key_heads, value_heads = (
        lax.all_gather(key_block, "col", axis=1, tiled=True),
        lax.all_gather(value_block, "col", axis=1, tiled=True),
    )
    query_count = query_heads.shape[0]
    key_count = key_heads.shape[0]
    sequence_ids = segment_ids[0]
    query_ids = lax.dynamic_slice_in_dim(
        sequence_ids, lax.axis_index("col") * query_count, query_count, 0
    )
    same_doc = query_ids[:, None] == sequence_ids[None, :]
    query_split = query_heads.reshape(query_count, HEADS, HEAD)
    key_split = key_heads.reshape(key_count, HEADS, HEAD)
    value_split = value_heads.reshape(key_count, HEADS, HEAD)
    scores = head_scores(query_split, key_split, same_doc)
    highest = jnp.max(scores, -1, keepdims=True)
    exponent = jnp.exp(scores - highest)
    totals = jnp.sum(exponent, -1, keepdims=True)
    log_totals = highest + jnp.log(totals)
    attn_probs = (exponent / totals).astype(jnp.bfloat16)
    attended = jnp.einsum(
        "hqk,khd->qhd", attn_probs, value_split, preferred_element_type=jnp.float32
    )
    attended = attended.reshape(query_count, -1).astype(jnp.bfloat16)
    attended_block = heads_out(attended)
    attended_rows = gather_over_row(attended_block)
    projected = sum_over_col(attended_rows, out_weight, False) + out_bias
    hidden, hidden_normed, hidden_scaling = layer_norm(
        token_major.astype(jnp.float32) + projected, attn_gain, attn_shift
    )
    hidden_low = hidden.astype(jnp.bfloat16)
    hidden_rows = gather_over_col(hidden_low)
    pre_act = sum_over_row(hidden_rows, up_weight, False) + up_bias
    activated, gelu_pull = jax.vjp(gelu_tanh, pre_act)
    act_block = activated.astype(jnp.bfloat16)
    act_rows = gather_over_row(act_block)
    down_out = sum_over_col(act_rows, down_weight, False) + down_bias
    output, out_normed, out_scaling = layer_norm(hidden + down_out, ffn_gain, ffn_shift)
    upstream = cotangent.T.astype(jnp.float32)
    ffn_gain_grad = jnp.sum(upstream * out_normed, 0)
    ffn_shift_grad = jnp.sum(upstream, 0)
    resid_grad = norm_backward(upstream, out_normed, out_scaling, ffn_gain)
    down_grad_rows = gather_over_col(resid_grad.astype(jnp.bfloat16))
    down_weight_grad = jnp.einsum(
        "tf,td->fd", act_rows, down_grad_rows, preferred_element_type=jnp.float32
    )
    down_bias_grad = column_sums(down_grad_rows)
    act_grad = sum_over_row(down_grad_rows, down_weight, True)
    pre_grad = gelu_pull(act_grad)[0].astype(jnp.bfloat16)
    pre_grad_rows = gather_over_row(pre_grad)
    up_weight_grad = jnp.einsum(
        "td,tf->df", hidden_rows, pre_grad_rows, preferred_element_type=jnp.float32
    )
    up_bias_grad = column_sums(pre_grad_rows)
    hidden_grad = sum_over_col(pre_grad_rows, up_weight, True) + resid_grad
    attn_gain_grad = jnp.sum(hidden_grad * hidden_normed, 0)
    attn_shift_grad = jnp.sum(hidden_grad, 0)
    first_grad = norm_backward(hidden_grad, hidden_normed, hidden_scaling, attn_gain)
    proj_grad_rows = gather_over_col(first_grad.astype(jnp.bfloat16))
    out_weight_grad = jnp.einsum(
        "tc,td->cd", attended_rows, proj_grad_rows, preferred_element_type=jnp.float32
    )
    out_bias_grad = column_sums(proj_grad_rows)
    attended_grad = heads_in(sum_over_row(proj_grad_rows, out_weight, True).astype(jnp.bfloat16))
    scores = head_scores(query_split, key_split, same_doc)
    attn_exact = jnp.exp(scores - log_totals)
    grad_split = attended_grad.reshape(query_count, HEADS, HEAD)
    prob_grad = jnp.einsum(
        "qhd,khd->hqk", grad_split, value_split, preferred_element_type=jnp.float32
    )
    score_grad = attn_exact * (prob_grad - jnp.sum(prob_grad * attn_exact, -1, keepdims=True))
    score_grad = score_grad.astype(jnp.bfloat16)
    query_grad = (
        jnp.einsum("hqk,khd->qhd", score_grad, key_split, preferred_element_type=jnp.float32)
        * score_scale
    )
    query_grad = query_grad.reshape(query_count, -1).astype(jnp.bfloat16)
    key_grad = (
        jnp.einsum("hqk,qhd->khd", score_grad, query_split, preferred_element_type=jnp.float32)
        * score_scale
    )
    key_grad = key_grad.reshape(key_count, -1)
    value_grad = jnp.einsum(
        "hqk,qhd->khd",
        attn_exact.astype(jnp.bfloat16),
        grad_split,
        preferred_element_type=jnp.float32,
    ).reshape(key_count, -1)
    key_sum, value_sum = (
        lax.psum_scatter(
            key_grad.astype(jnp.bfloat16), "col", scatter_dimension=1, tiled=True
        ).astype(jnp.float32),
        lax.psum_scatter(
            value_grad.astype(jnp.bfloat16), "col", scatter_dimension=1, tiled=True
        ).astype(jnp.float32),
    )
    joined_grad = jnp.concatenate(
        [heads_out(query_grad), key_sum.astype(jnp.bfloat16), value_sum.astype(jnp.bfloat16)], 1
    )
    joined_rows = gather_over_row(joined_grad)
    joined_weight_grad = jnp.einsum(
        "td,tf->df", token_rows, joined_rows, preferred_element_type=jnp.float32
    )
    query_bias_grad = column_sums(joined_rows[:, :head_cols])
    value_bias_grad = column_sums(joined_rows[:, 2 * head_cols :])
    tokens_grad = sum_over_col(joined_rows, joined_weight, True) + first_grad
    summed = lax.psum(
        (
            joined_weight_grad,
            query_bias_grad,
            value_bias_grad,
            out_weight_grad,
            out_bias_grad,
            up_weight_grad,
            up_bias_grad,
            down_weight_grad,
            down_bias_grad,
        ),
        "dp",
    )
    norm_sums = lax.psum(
        (attn_gain_grad, attn_shift_grad, ffn_gain_grad, ffn_shift_grad), ("dp", "col")
    )
    return (
        output.T.astype(jnp.bfloat16),
        tokens_grad.T,
        summed[0][:, :head_cols],
        summed[0][:, head_cols : 2 * head_cols],
        summed[0][:, 2 * head_cols :],
        summed[1],
        summed[2],
        summed[3],
        summed[4],
        norm_sums[0],
        norm_sums[1],
        summed[5],
        summed[6],
        summed[7],
        summed[8],
        norm_sums[2],
        norm_sums[3],
    )


MESH_ID = pl.DeviceIdType.MESH
BF = jnp.bfloat16
F32 = jnp.float32
GRID = {"dp": 4, "row": 4, "col": 2}
SEQ = 256
WIDE = 768
HALF = 128
ROWS = 192
CHUNK = 384
CHUNKS = 12
SEMS = 256
ORDER = (0, 3, 1, 2)


def small_grid(mesh):
    return dict(mesh.shape) == GRID


def mm(a, b):
    return jnp.dot(a, b, preferred_element_type=F32)


def mm_nt(a, b):
    return lax.dot_general(a, b, (((1,), (1,)), ((), ())), preferred_element_type=F32)


def loop(count, step):
    def wrapped(i, carry):
        step(i)
        return carry

    lax.fori_loop(0, count, wrapped, 0)


def row_mean(values):
    return jnp.sum(values, axis=1, keepdims=True) * (1.0 / WIDE)


def fold(values):
    return jnp.sum(values.reshape(values.shape[0] // 8, 8, values.shape[1]), axis=0)


def layer_kernel(
    ids,
    tok,
    cot,
    qw,
    kw,
    vw,
    ow,
    uw,
    dw,
    qb,
    vb,
    ub,
    ob,
    ag,
    ash,
    db,
    fgn,
    fsh,
    q_out,
    k_out,
    v_out,
    o_out,
    u_out,
    d_out,
    res_out,
    tg_out,
    bias_out,
    norm_out,
    own_vec,
    upb,
    W,
    G,
    R1,
    R2,
    RZ,
    fin,
    xin,
    cin,
    xs,
    xr,
    vg,
    vec,
    VA,
    VB,
    VC,
    VD,
    VZ,
    xf,
    cf,
    neq,
    q,
    k,
    v,
    qT,
    kT,
    P,
    at,
    hid,
    n1,
    s1,
    hb,
    hT,
    act,
    dact,
    outf,
    r2g,
    dg,
    dgT,
    pg,
    fg,
    fgT,
    pgT,
    prg,
    dA,
    dAT,
    dT,
    tcross,
    ccross,
    tgp,
    tgr,
    osend,
    obuf,
    tsend,
    tbuf,
    send,
    recv,
):
    dp = lax.axis_index("dp")
    z = lax.axis_index("row")
    x = lax.axis_index("col")
    core = lax.rem(dp, 2)
    y = lax.div(dp, 2)
    mate = dp + 1 - 2 * core
    far = lax.rem(dp + 2, 4)
    matefar = lax.rem(mate + 2, 4)
    other = 1 - x
    counts = {"s": 0, "r": 0}
    pending = []

    def new(kind, n=1):
        base = counts[kind]
        counts[kind] = base + n
        assert counts[kind] <= SEMS
        return base

    def push(src, dst, ssem, rsem, **where):
        return pltpu.make_async_remote_copy(
            src_ref=src,
            dst_ref=dst,
            send_sem=send.at[ssem],
            recv_sem=recv.at[rsem],
            device_id=where,
            device_id_type=MESH_ID,
        )

    def start(pred, make):
        if pred is None:
            make().start()
        else:

            @pl.when(pred)
            def _():
                make().start()

        pending.append((pred, make))

    def arrived(dst, rsem, **where):
        push(dst, dst, 0, rsem, **where).wait_recv()

    def rows(b):
        return pl.ds(pl.multiple_of(b * ROWS, ROWS), ROWS)

    bar = pltpu.get_barrier_semaphore()
    for j in range(4):
        for h in range(2):

            @pl.when((z != j) | (x != h))
            def _(j=j, h=h):
                pl.semaphore_signal(bar, inc=1, device_id={"row": j, "col": h}, device_id_type=MESH_ID)

    pl.semaphore_signal(bar, inc=1, device_id={"dp": mate}, device_id_type=MESH_ID)
    pl.semaphore_signal(bar, inc=1, device_id={"dp": far}, device_id_type=MESH_ID)

    lsem = new("s", CHUNKS)
    mine = rows(z)

    def local_parts():
        parts = []
        for j, ref in enumerate((qw, kw, vw, ow)):
            parts.append((ref, W.at[j, mine]))
        for i in range(4):
            parts.append((uw.at[:, i * CHUNK : (i + 1) * CHUNK], W.at[4 + i, mine]))
        for i in range(4):
            parts.append((dw.at[:, i * CHUNK : (i + 1) * CHUNK], W.at[8 + i, mine]))
        return [pltpu.make_async_copy(a, b, send.at[lsem + n]) for n, (a, b) in enumerate(parts)]

    locals_ = local_parts()
    for c in locals_:
        c.start()
    own_vec[...] = jnp.zeros_like(own_vec)
    for n, ref in enumerate((ob, ag, ash, db, fgn, fsh)):
        own_vec[n : n + 1, 0:ROWS] = ref[...].reshape(1, ROWS)
    own_vec[...] = pltpu.roll(own_vec[...], z * ROWS, 1)
    vg[z] = own_vec[...]
    for i in range(4):
        upb[i] = ub[i * CHUNK : (i + 1) * CHUNK].reshape(1, CHUNK)
    seg = jnp.broadcast_to(ids[...].astype(F32), (SEQ, SEQ))
    neq[...] = jnp.abs(seg - seg.T)
    pl.semaphore_wait(bar, 9)

    def spread(ref, landing, cross):
        xs_, xr_, ssem, rsem = new("s", 2), new("r", 2), new("s", 8), new("r", 4)

        def half(s, h):
            return ref.at[:, pl.ds(pl.multiple_of(s * SEQ + h * HALF, HALF), HALF)]

        def out(j, src, mine_):
            n = ssem + j + (0 if mine_ else 4)
            here = (x == j // 2) if mine_ else (x != j // 2)
            start(here & (z != j), lambda: push(src, landing.at[x, mine], n, rsem + z, row=j))

            @pl.when(here & (z == j))
            def _():
                pltpu.make_async_copy(src, landing.at[x, mine], recv.at[rsem + z]).start()

        def begin():
            for s in range(2):
                start(None, lambda s=s: push(half(s, other), cross.at[s], xs_ + s, xr_ + s, col=other))
            for j in range(4):
                out(j, half(j % 2, x), True)

        def relay():
            for s in range(2):
                arrived(cross.at[s], xr_ + s, col=other)
            for j in range(4):
                out(j, cross.at[j % 2], False)

        def collect():
            for b in range(4):
                dst = landing.at[x, rows(b)]

                @pl.when(z == b)
                def _(dst=dst, b=b):
                    pltpu.make_async_copy(cross.at[0], dst, recv.at[rsem + b]).wait()

                @pl.when(z != b)
                def _(dst=dst, b=b):
                    arrived(dst, rsem + b, row=b)

        return begin, relay, collect

    def swap(landing):
        ssem, rsem = new("s"), new("r")
        start(None, lambda: push(landing.at[x], landing.at[x], ssem, rsem, col=other))

        def collect():
            arrived(landing.at[other], rsem, col=other)

        return collect

    def share_vec():
        ssem, rsem = new("s", 3), new("r", 4)
        for o in range(1, 4):
            to = lax.rem(z + o, 4)
            start(None, lambda o=o, to=to: push(own_vec, vg.at[z], ssem + o - 1, rsem + z, row=to))

        def collect():
            for o in range(1, 4):
                b = lax.rem(z + o, 4)
                arrived(vg.at[b], rsem + b, row=b)
            vec[...] = vg[0] + vg[1] + vg[2] + vg[3]

        return collect

    def gather(g):
        zs, ys, cs = new("s", 5), new("s", 4), new("s", 8)
        zr, yr, cr = new("r", 4), new("r", 4), new("r", 8)
        own, ychunk = 4 * g + dp, 4 * g + far

        def block(chunk, b):
            return W.at[chunk, rows(b)]

        def along(n, b, to, pred):
            start(pred, lambda: push(block(own, b), block(own, b), zs + n, zr + b, row=to))

        def first():
            along(0, z, z + 1, (z < 3) if g == 0 else (z < 2))
            along(1, z, z - 1, (z > 0) if g == 0 else (z > 1))

        def second():
            along(2, z, z + 2, z < 2)
            along(3, z, z - 2, z > 1)

        def late():
            along(0, z, z + 1, z == 2)
            along(1, z, z - 1, z == 1)

        def take(b, pred):
            @pl.when(pred)
            def _():
                arrived(block(own, b), zr + b, row=b)

            start(pred, lambda: push(block(own, b), block(own, b), ys + b, yr + b, dp=far))
            start(pred, lambda: push(block(own, b), block(own, b), cs + b, cr + b, dp=mate))

        def hop1():
            for b in range(4):
                take(b, (z == b - 1) | (z == b + 1))

        def hop2():
            for b, at_ in ((0, 2), (3, 1)):

                @pl.when(z == at_)
                def _(b=b):
                    arrived(block(own, b), zr + b, row=b)

                along(4, b, 3 - b, z == at_)
                start(z == at_, lambda b=b: push(block(own, b), block(own, b), ys + b, yr + b, dp=far))
                start(z == at_, lambda b=b: push(block(own, b), block(own, b), cs + b, cr + b, dp=mate))
            if g < 2:
                gathers[g + 1][1]()
            take(2, z == 0)
            take(1, z == 3)

        def hop3():
            take(3, z == 0)
            take(0, z == 3)

        def across():
            for b in range(4):
                there = z != b

                @pl.when(there)
                def _(b=b):
                    arrived(block(ychunk, b), yr + b, dp=far)

                start(
                    there,
                    lambda b=b: push(block(ychunk, b), block(ychunk, b), cs + 4 + b, cr + 4 + b, dp=mate),
                )

        def finish():
            for b in range(4):

                @pl.when(z != b)
                def _(b=b):
                    arrived(block(4 * g + mate, b), cr + b, dp=mate)
                    arrived(block(4 * g + matefar, b), cr + 4 + b, dp=mate)

        return (first, second), late, hop1, hop2, hop3, across, finish

    def exchange(n):
        ssem, rsem = new("s", 3), new("r", 3)

        def put(c, value):
            xs[n, c] = value.astype(BF)
            start(None, lambda: push(xs.at[n, c], xr.at[n, c], ssem + c, rsem + c, col=other))

        def collect():
            for c in range(3):
                arrived(xr.at[n, c], rsem + c, col=other)

        return put, collect

    def both(n, r):
        own = [xs[n, c, r, :].astype(F32) + xr[n, c, r, :].astype(F32) for c in range(3)]
        return jnp.concatenate(own, axis=1)

    def reduce(g):
        s1_, s2_, sz, sy, sc = new("s", 2), new("s", 4), new("s", 4), new("s"), new("s", 2)
        r1, r2, rz, ry, rc = new("r", 2), new("r", 4), new("r", 4), new("r"), new("r", 2)
        own, ychunk = 4 * g + dp, 4 * g + far

        def to_core():
            for j in range(2):
                src = G.at[4 * g + 2 * j + 1 - core]
                start(None, lambda src=src, j=j: push(src, R1.at[g, j], s1_ + j, r1 + j, dp=mate))

        def add(chunk, extra, base, count):
            def step(i):
                at_ = pl.ds(pl.multiple_of(base + i * 64, 64), 64)
                G[chunk, at_, :] = (G[chunk, at_, :].astype(F32) + extra[at_, :].astype(F32)).astype(BF)

            loop(count // 64, step)

        def piece(ref, b):
            return ref.at[pl.ds(b * ROWS, ROWS)]

        def to_y():
            arrived(R1.at[g, 1 - y], r1 + 1 - y, dp=mate)
            for b in ORDER:
                add(ychunk, R1.at[g, 1 - y], b * ROWS, ROWS)
                start(
                    None,
                    lambda b=b: push(piece(G.at[ychunk], b), piece(R2.at[g], b), s2_ + b, r2 + b, dp=far),
                )
            arrived(R1.at[g, y], r1 + y, dp=mate)
            add(own, R1.at[g, y], 0, WIDE)

        def take(b):
            arrived(piece(R2.at[g], b), r2 + b, dp=far)
            add(own, R2.at[g], b * ROWS, ROWS)
            start(z != b, lambda: push(piece(G.at[own], b), RZ.at[g, z], sz + b, rz + z, row=b))

        def settle():
            for o in range(1, 4):
                b = lax.rem(z + o, 4)
                arrived(RZ.at[g, b], rz + b, row=b)
            RZ[g, z] = G[own, mine, :]

            def step(i):
                at_ = pl.ds(pl.multiple_of(i * 32, 32), 32)
                part = [RZ[g, b, at_, :].astype(F32) for b in range(4)]
                fin[own, at_, :] = ((part[0] + part[1]) + (part[2] + part[3])).astype(BF)

            loop(ROWS // 32, step)
            start(None, lambda: push(fin.at[own], fin.at[own], sy, ry, dp=far))
            start(None, lambda: push(fin.at[own], fin.at[own], sc, rc, dp=mate))

        def across():
            arrived(fin.at[ychunk], ry, dp=far)
            start(None, lambda: push(fin.at[ychunk], fin.at[ychunk], sc + 1, rc + 1, dp=mate))

        def finish():
            arrived(fin.at[4 * g + mate], rc, dp=mate)
            arrived(fin.at[4 * g + matefar], rc + 1, dp=mate)

        return to_core, to_y, take, settle, across, finish

    def deliver(sent, landed, out):
        ssem, rsem = new("s", 4), new("r", 4)
        slot = 2 * lax.rem(z, 2) + x
        home = lax.div(z, 2) == x
        for b in range(4):
            self_ = home & (z == b)
            start(
                jnp.logical_not(self_),
                lambda b=b: push(
                    sent.at[rows(b)], landed.at[slot], ssem + b, rsem + slot, row=b, col=lax.div(z, 2)
                ),
            )

            @pl.when(self_)
            def _(b=b):
                pltpu.make_async_copy(sent.at[rows(b)], landed.at[slot], recv.at[rsem + slot]).start()

        def collect():
            osem = new("s", 4)
            copies = []
            for n in range(4):
                s, h = n // 2, n % 2
                local = (2 * x + s == z) & (h == x)

                @pl.when(local)
                def _(n=n):
                    pltpu.make_async_copy(sent.at[rows(z)], landed.at[n], recv.at[rsem + n]).wait()

                @pl.when(jnp.logical_not(local))
                def _(n=n):
                    arrived(landed.at[n], rsem + n, col=other)

                copies.append(
                    pltpu.make_async_copy(
                        landed.at[n], out.at[:, n * HALF : (n + 1) * HALF], send.at[osem + n]
                    )
                )
                copies[-1].start()
            return copies

        return collect

    tok_out, tok_relay, tok_in = spread(tok, xin, tcross)
    tok_out()
    gathers = [gather(g) for g in range(3)]
    for c in locals_:
        c.wait()
    gathers[0][0][0]()
    tok_relay()
    gathers[0][0][1]()
    vec_in = share_vec()
    for g in range(1, 3):
        gathers[g][0][0]()
        gathers[g][0][1]()
    cot_out, cot_relay, cot_in = spread(cot, cin, ccross)
    gathers[0][2]()
    gathers[0][3]()
    tok_in()
    tok_swap = swap(xin)
    gathers[0][4]()
    vec_in()
    tok_swap()
    for h in range(2):
        xf[h * HALF : (h + 1) * HALF, :] = xin[h].astype(F32).T
    gathers[0][5]()
    gathers[0][6]()

    xb = xf[...].astype(BF)
    for j, (dst, bias) in enumerate(((q, qb), (k, None), (v, vb))):
        r = mm(xb, W[j])
        if bias is not None:
            r = r + bias[...].reshape(1, CHUNK)
        for p in range(3):
            dst[p] = r[:, p * HALF : (p + 1) * HALF].astype(BF)

    lane = lax.broadcasted_iota(jnp.int32, (SEQ, HALF), 1) < HEAD
    scale = 1.0 / math.sqrt(HEAD)

    def only(values, hh):
        keep = lane if hh == 0 else jnp.logical_not(lane)
        return jnp.where(keep, values.astype(F32), 0.0).astype(BF)

    def attend(p):
        qv, kv, vv = q[p], k[p], v[p]
        outs = []
        for hh in range(2):
            s = mm_nt(only(qv, hh), kv) * scale
            s = jnp.where(neq[...] == 0.0, s, -1000000000.0)
            e = jnp.exp(s - jnp.max(s, axis=1, keepdims=True))
            pr = e / jnp.sum(e, axis=1, keepdims=True)
            P[2 * p + hh] = pr
            outs.append(mm(pr.astype(BF), vv))
        at[p] = jnp.where(lane, outs[0], outs[1]).astype(BF)

    gathers[1][2]()
    loop(3, attend)
    gathers[1][3]()
    cot_out()

    put0, get0 = exchange(0)
    att = jnp.concatenate([at[0], at[1], at[2]], axis=1)
    for c in range(3):
        put0(c, mm_nt(att, W[3, c * SEQ : (c + 1) * SEQ, :]))
    cot_relay()
    gathers[1][4]()
    for p in range(3):
        qT[p] = q[p].astype(F32).T.astype(BF)
        kT[p] = k[p].astype(F32).T.astype(BF)
    gathers[1][5]()
    gathers[2][2]()
    get0()

    def norm1(i):
        r = pl.ds(pl.multiple_of(i * 32, 32), 32)
        resid = xf[r, :] + (both(0, r) + vec[0:1, :])
        d = resid - row_mean(resid)
        s = lax.rsqrt(row_mean(d * d) + EPS)
        n = d * s
        h = n * vec[1:2, :] + vec[2:3, :]
        n1[r, :] = n
        s1[r, :] = jnp.broadcast_to(s, (32, HALF))
        hid[r, :] = h
        hb[r, :] = h.astype(BF)

    loop(8, norm1)
    gathers[2][3]()
    gathers[1][6]()

    hv = hb[...]
    c0 = math.sqrt(2.0 / math.pi)

    def up_step(i):
        u = mm(hv, W[4 + i]) + upb[i]
        u2 = u * u
        t = jnp.tanh(c0 * (u + 0.044715 * (u2 * u)))
        half = 0.5 * (1.0 + t)
        act[i] = (u * half).astype(BF)
        dact[i] = half + (0.5 * u) * (1.0 - t * t) * (c0 * (1.0 + (3 * 0.044715) * u2))

    loop(4, up_step)
    gathers[2][4]()
    cot_in()
    cot_swap = swap(cin)
    gathers[2][5]()
    hT[...] = hid[...].T.astype(BF)
    gathers[2][6]()
    put1, get1 = exchange(1)
    for c in range(3):
        acc = mm_nt(act[0], W[8, c * SEQ : (c + 1) * SEQ, :])
        for i in range(1, 4):
            acc = acc + mm_nt(act[i], W[8 + i, c * SEQ : (c + 1) * SEQ, :])
        put1(c, acc)
    cot_swap()
    for h in range(2):
        cf[h * HALF : (h + 1) * HALF, :] = cin[h].astype(F32).T
    get1()

    VA[...] = jnp.zeros_like(VA)

    def norm2(i, carry):
        gain_sum, shift_sum, bias_sum = carry
        r = pl.ds(pl.multiple_of(i * 32, 32), 32)
        resid = hid[r, :] + (both(1, r) + vec[3:4, :])
        d = resid - row_mean(resid)
        s = lax.rsqrt(row_mean(d * d) + EPS)
        n = d * s
        outf[r, :] = n * vec[4:5, :] + vec[5:6, :]
        up = cf[r, :]
        e = up * vec[4:5, :]
        grad = s * (e - row_mean(e) - n * row_mean(e * n))
        low = grad.astype(BF)
        r2g[r, :] = grad
        dg[r, :] = low
        return gain_sum + fold(up * n), shift_sum + fold(up), bias_sum + fold(low.astype(F32))

    zero = jnp.zeros((8, WIDE), F32)
    sums = lax.fori_loop(0, 8, norm2, (zero, zero, zero))

    def total(values):
        return jnp.sum(values, axis=0, keepdims=True)

    VA[7:8, :] = total(sums[0])
    VA[8:9, :] = total(sums[1])
    VA[6:7, :] = total(sums[2])
    dgT[...] = r2g[...].T.astype(BF)
    reduces = [reduce(g) for g in range(3)]

    def outer(dst, left, right):
        def step(b):
            r = pl.ds(pl.multiple_of(b * SEQ, SEQ), SEQ)
            G[dst, r, :] = mm(left[r, :], right).astype(BF)

        loop(3, step)

    loop(4, lambda i: outer(8 + i, dgT, act[i]))
    reduces[2][0]()

    ones = jnp.ones((8, SEQ), BF)
    dgv = dg[...]

    def pre_step(i):
        low = (mm(dgv, W[8 + i]) * dact[i]).astype(BF)
        prg[i] = low

    loop(4, pre_step)
    reduces[2][1]()
    put2, get2 = exchange(2)
    for c in range(3):
        acc = mm_nt(prg[0], W[4, c * SEQ : (c + 1) * SEQ, :])
        for i in range(1, 4):
            acc = acc + mm_nt(prg[i], W[4 + i, c * SEQ : (c + 1) * SEQ, :])
        put2(c, acc)
    for i in range(4):
        VA[1 + i // 2 : 2 + i // 2, (i % 2) * CHUNK : (i % 2 + 1) * CHUNK] = mm(ones, prg[i])[0:1, :]
    loop(4, lambda i: outer(4 + i, hT, prg[i]))
    reduces[1][0]()
    reduces[2][2](ORDER[0])

    mine_tokens = pl.ds(pl.multiple_of(x * HALF, HALF), HALF)
    osend[...] = outf[mine_tokens, :].T.astype(BF)
    out_in = deliver(osend, obuf, res_out)
    reduces[2][2](ORDER[1])
    reduces[1][1]()
    get2()

    def norm1_back(i, carry):
        gain_sum, shift_sum, bias_sum = carry
        r = pl.ds(pl.multiple_of(i * 32, 32), 32)
        up = r2g[r, :] + both(2, r)
        n = n1[r, :]
        s = s1[r, :][:, 0:1]
        e = up * vec[1:2, :]
        grad = s * (e - row_mean(e) - n * row_mean(e * n))
        low = grad.astype(BF)
        fg[r, :] = grad
        pg[r, :] = low
        return gain_sum + fold(up * n), shift_sum + fold(up), bias_sum + fold(low.astype(F32))

    sums = lax.fori_loop(0, 8, norm1_back, (zero, zero, zero))
    VA[4:5, :] = total(sums[0])
    VA[5:6, :] = total(sums[1])
    VA[3:4, :] = total(sums[2])
    for h in range(2):
        t = fg[h * HALF : (h + 1) * HALF, :].T
        fgT[h] = t
        pgT[:, h * HALF : (h + 1) * HALF] = t.astype(BF)

    reduces[2][2](ORDER[2])
    reduces[2][2](ORDER[3])
    r = mm(pg[...], W[3])
    for p in range(3):
        part = r[:, p * HALF : (p + 1) * HALF].astype(BF)
        dA[p] = part
        dAT[p] = part.astype(F32).T.astype(BF)
    outer(3, pgT, att)

    top = lax.broadcasted_iota(jnp.int32, (HALF, SEQ), 0) < HEAD

    def attend_back(p):
        dAv, vv = dA[p], v[p]
        dq, dk, dv = [], [], []
        for hh in range(2):
            pr = P[2 * p + hh]
            pgrad = mm_nt(only(dAv, hh), vv)
            ds = (pr * (pgrad - jnp.sum(pgrad * pr, axis=1, keepdims=True))).astype(BF)
            dq.append(mm_nt(kT[p], ds))
            dk.append(mm(qT[p], ds))
            dv.append(mm(dAT[p], pr.astype(BF)))
        dT[0, p] = (jnp.where(top, dq[0], dq[1]) * scale).astype(BF)
        dT[1, p] = (jnp.where(top, dk[0], dk[1]) * scale).astype(BF)
        dT[2, p] = jnp.where(top, dv[0], dv[1]).astype(BF)

    loop(3, attend_back)
    reduces[1][2](ORDER[0])

    for j in range(3):
        t = dT[j].reshape(CHUNK, SEQ)
        if j != 1:
            at_ = 0 if j == 0 else CHUNK
            VA[0:1, at_ : at_ + CHUNK] = mm_nt(ones, t)[0:1, :]

        def step(b, t=t, j=j):
            r = pl.ds(pl.multiple_of(b * SEQ, SEQ), SEQ)
            left = jnp.concatenate([xin[0, r, :], xin[1, r, :]], axis=1)
            G[j, r, :] = mm_nt(left, t).astype(BF)

        loop(3, step)
    reduces[0][0]()
    vs, vr = new("s", 5), new("r", 6)
    start(None, lambda: push(VA, VB, vs, vr, dp=mate))

    def back_step(b):
        r = pl.ds(pl.multiple_of(b * SEQ, SEQ), SEQ)
        acc = mm(W[0, r, :], dT[0].reshape(CHUNK, SEQ))
        acc = acc + mm(W[1, r, :], dT[1].reshape(CHUNK, SEQ))
        acc = acc + mm(W[2, r, :], dT[2].reshape(CHUNK, SEQ))
        tgp[0, r, :] = acc[:, :HALF].astype(BF)
        tgp[1, r, :] = acc[:, HALF:].astype(BF)

    loop(3, back_step)
    ts, tr = new("s"), new("r")
    start(None, lambda: push(tgp.at[other], tgr, ts, tr, col=other))
    reduces[1][2](ORDER[1])
    arrived(VB, vr, dp=mate)
    VD[...] = VA[...] + VB[...]
    start(None, lambda: push(VD, VC, vs + 1, vr + 1, dp=far))
    reduces[0][1]()
    reduces[1][2](ORDER[2])
    arrived(tgr, tr, col=other)
    tsend[...] = (tgp[x].astype(F32) + tgr[...].astype(F32) + fgT[x]).astype(BF)
    tg_in = deliver(tsend, tbuf, tg_out)
    reduces[1][2](ORDER[3])
    reduces[2][3]()
    arrived(VC, vr + 1, dp=far)
    VZ[z] = VD[...] + VC[...]
    for o in range(1, 4):
        to = lax.rem(z + o, 4)
        start(None, lambda o=o, to=to: push(VZ.at[z], VZ.at[z], vs + 1 + o, vr + 2 + z, row=to))
    reduces[0][2](ORDER[0])
    reduces[0][2](ORDER[1])
    reduces[1][3]()
    reduces[0][2](ORDER[2])
    reduces[0][2](ORDER[3])
    reduces[2][4]()
    reduces[1][4]()
    reduces[2][5]()
    reduces[1][5]()
    reduces[0][3]()
    copies = []
    fsem = new("s", CHUNKS)

    def flush(g):
        for i in range(4):
            if g == 0:
                dst = (q_out, k_out, v_out, o_out)[i]
            else:
                dst = (u_out, d_out)[g - 1].at[:, i * CHUNK : (i + 1) * CHUNK]
            c = pltpu.make_async_copy(fin.at[4 * g + i], dst, send.at[fsem + 4 * g + i])
            c.start()
            copies.append(c)

    flush(2)
    flush(1)
    for o in range(1, 4):
        b = lax.rem(z + o, 4)
        arrived(VZ.at[b], vr + 2 + b, row=b)
    sums = VZ[0] + VZ[1] + VZ[2] + VZ[3]
    bias_out[...] = sums[0:8, :]
    norm_out[...] = pltpu.roll(sums, WIDE - z * ROWS, 1)[:, 0:SEQ]
    copies += out_in()
    copies += tg_in()
    reduces[0][4]()
    reduces[0][5]()
    flush(0)
    for pred, make in pending:
        if pred is None:
            make().wait_send()
        else:

            @pl.when(pred)
            def _(make=make):
                make().wait_send()

    for c in copies:
        c.wait()


WIDTHS = (CHUNK,) * 4 + (4 * CHUNK,) * 2 + (2 * SEQ,)


def widen_kernel(*refs):
    count = len(WIDTHS)
    ins, passed, bias, norm = refs[:count], refs[count], refs[count + 1], refs[count + 2]
    refs = refs[count + 3 :]
    outs, passed_out, vectors = refs[:count], refs[count], refs[count + 1 : count + 10]
    refs = refs[count + 10 :]
    low, wide, held, sem_in, sem_out = refs[:count], refs[count : 2 * count], *refs[2 * count :]
    order = (4, 5, 6, 0, 1, 2, 3)
    reads = {n: pltpu.make_async_copy(ins[n], low[n], sem_in.at[n]) for n in order}
    through = pltpu.make_async_copy(passed, held, sem_in.at[count])
    for n in order:
        reads[n].start()
    through.start()
    vectors[0][...] = bias[0, 0:CHUNK]
    vectors[1][...] = bias[0, CHUNK:WIDE]
    for i in range(2):
        vectors[2][i * WIDE : (i + 1) * WIDE] = bias[1 + i, :]
    for n in range(6):
        vectors[3 + n][...] = norm[3 + n, 0:ROWS]
    writes = []
    for n in order:
        reads[n].wait()

        def step(i, n=n):
            r = pl.ds(pl.multiple_of(i * 32, 32), 32)
            wide[n][r, :] = low[n][r, :].astype(F32)

        loop(ROWS // 32, step)
        writes.append(pltpu.make_async_copy(wide[n], outs[n], sem_out.at[n]))
        writes[-1].start()
    through.wait()
    writes.append(pltpu.make_async_copy(held, passed_out, sem_out.at[count]))
    writes[-1].start()
    for c in writes:
        c.wait()


def fused_body(
    tokens,
    segment_ids,
    query_weight,
    key_weight,
    value_weight,
    query_bias,
    value_bias,
    out_weight,
    out_bias,
    attn_gain,
    attn_shift,
    up_weight,
    up_bias,
    down_weight,
    down_bias,
    ffn_gain,
    ffn_shift,
    cotangent,
):
    hbm = pl.BlockSpec(memory_space=pl.ANY)
    vmem = pl.BlockSpec(memory_space=pltpu.VMEM)
    gq, gk, gv, go, gu, gd, out, tgrad, bias, norm = pl.pallas_call(
        layer_kernel,
        out_shape=(
            *[jax.ShapeDtypeStruct((ROWS, CHUNK), BF)] * 4,
            *[jax.ShapeDtypeStruct((ROWS, 4 * CHUNK), BF)] * 2,
            *[jax.ShapeDtypeStruct((ROWS, 2 * SEQ), BF)] * 2,
            jax.ShapeDtypeStruct((8, WIDE), F32),
            jax.ShapeDtypeStruct((16, SEQ), F32),
        ),
        in_specs=[vmem] + [hbm] * 8 + [vmem] * 9,
        out_specs=(hbm,) * 8 + (vmem, vmem),
        scratch_shapes=[
            pltpu.VMEM((8, WIDE), F32),
            pltpu.VMEM((4, 1, CHUNK), F32),
            pltpu.VMEM((CHUNKS, WIDE, CHUNK), BF),
            pltpu.VMEM((CHUNKS, WIDE, CHUNK), BF),
            pltpu.VMEM((3, 2, WIDE, CHUNK), BF),
            pltpu.VMEM((3, WIDE, CHUNK), BF),
            pltpu.VMEM((3, 4, ROWS, CHUNK), BF),
            pltpu.VMEM((CHUNKS, ROWS, CHUNK), BF),
            pltpu.VMEM((2, WIDE, HALF), BF),
            pltpu.VMEM((2, WIDE, HALF), BF),
            pltpu.VMEM((3, 3, SEQ, SEQ), BF),
            pltpu.VMEM((3, 3, SEQ, SEQ), BF),
            pltpu.VMEM((4, 8, WIDE), F32),
            pltpu.VMEM((8, WIDE), F32),
            pltpu.VMEM((16, WIDE), F32),
            pltpu.VMEM((16, WIDE), F32),
            pltpu.VMEM((16, WIDE), F32),
            pltpu.VMEM((16, WIDE), F32),
            pltpu.VMEM((4, 16, WIDE), F32),
            pltpu.VMEM((SEQ, WIDE), F32),
            pltpu.VMEM((SEQ, WIDE), F32),
            pltpu.VMEM((SEQ, SEQ), F32),
            pltpu.VMEM((3, SEQ, HALF), BF),
            pltpu.VMEM((3, SEQ, HALF), BF),
            pltpu.VMEM((3, SEQ, HALF), BF),
            pltpu.VMEM((3, HALF, SEQ), BF),
            pltpu.VMEM((3, HALF, SEQ), BF),
            pltpu.VMEM((6, SEQ, SEQ), F32),
            pltpu.VMEM((3, SEQ, HALF), BF),
            pltpu.VMEM((SEQ, WIDE), F32),
            pltpu.VMEM((SEQ, WIDE), F32),
            pltpu.VMEM((SEQ, HALF), F32),
            pltpu.VMEM((SEQ, WIDE), BF),
            pltpu.VMEM((WIDE, SEQ), BF),
            pltpu.VMEM((4, SEQ, CHUNK), BF),
            pltpu.VMEM((4, SEQ, CHUNK), F32),
            pltpu.VMEM((SEQ, WIDE), F32),
            pltpu.VMEM((SEQ, WIDE), F32),
            pltpu.VMEM((SEQ, WIDE), BF),
            pltpu.VMEM((WIDE, SEQ), BF),
            pltpu.VMEM((SEQ, WIDE), BF),
            pltpu.VMEM((SEQ, WIDE), F32),
            pltpu.VMEM((2, WIDE, HALF), F32),
            pltpu.VMEM((WIDE, SEQ), BF),
            pltpu.VMEM((4, SEQ, CHUNK), BF),
            pltpu.VMEM((3, SEQ, HALF), BF),
            pltpu.VMEM((3, HALF, SEQ), BF),
            pltpu.VMEM((3, 3, HALF, SEQ), BF),
            pltpu.VMEM((2, ROWS, HALF), BF),
            pltpu.VMEM((2, ROWS, HALF), BF),
            pltpu.VMEM((2, WIDE, HALF), BF),
            pltpu.VMEM((WIDE, HALF), BF),
            pltpu.VMEM((WIDE, HALF), BF),
            pltpu.VMEM((4, ROWS, HALF), BF),
            pltpu.VMEM((WIDE, HALF), BF),
            pltpu.VMEM((4, ROWS, HALF), BF),
            pltpu.SemaphoreType.DMA((SEMS,)),
            pltpu.SemaphoreType.DMA((SEMS,)),
        ],
        compiler_params=pltpu.CompilerParams(
            collective_id=0, has_side_effects=True, vmem_limit_bytes=63 * 1024 * 1024
        ),
    )(
        segment_ids,
        tokens,
        cotangent,
        query_weight,
        key_weight,
        value_weight,
        out_weight.T,
        up_weight,
        down_weight.T,
        query_bias,
        value_bias,
        up_bias,
        out_bias,
        attn_gain,
        attn_shift,
        down_bias,
        ffn_gain,
        ffn_shift,
    )
    count = len(WIDTHS)
    sizes = (CHUNK, CHUNK, 4 * CHUNK) + (ROWS,) * 6
    gq, gk, gv, go, gu, gd, tgrad, out, *vectors = pl.pallas_call(
        widen_kernel,
        out_shape=(
            *[jax.ShapeDtypeStruct((ROWS, w), F32) for w in WIDTHS],
            jax.ShapeDtypeStruct((ROWS, 2 * SEQ), BF),
            *[jax.ShapeDtypeStruct((n,), F32) for n in sizes],
        ),
        in_specs=[hbm] * (count + 1) + [vmem] * 2,
        out_specs=(hbm,) * (count + 1) + (vmem,) * len(sizes),
        scratch_shapes=[
            *[pltpu.VMEM((ROWS, w), BF) for w in WIDTHS],
            *[pltpu.VMEM((ROWS, w), F32) for w in WIDTHS],
            pltpu.VMEM((ROWS, 2 * SEQ), BF),
            pltpu.SemaphoreType.DMA((count + 1,)),
            pltpu.SemaphoreType.DMA((count + 1,)),
        ],
    )(gq, gk, gv, go, gu, gd, tgrad, out, bias, norm)
    return (
        out,
        tgrad,
        gq,
        gk,
        gv,
        vectors[0],
        vectors[1],
        go.T,
        *vectors[3:6],
        gu,
        vectors[2],
        gd.T,
        *vectors[6:9],
    )


def solution(mesh):
    placed = (
        P("row", ("dp", "col")),
        P(("dp", "row"), None),
        P("row", "col"),
        P("row", "col"),
        P("row", "col"),
        P("col"),
        P("col"),
        P("col", "row"),
        P("row"),
        P("row"),
        P("row"),
        P("row", "col"),
        P("col"),
        P("col", "row"),
        P("row"),
        P("row"),
        P("row"),
        P("row", ("dp", "col")),
    )
    return jax.shard_map(
        fused_body if small_grid(mesh) else body,
        mesh=mesh,
        in_specs=placed,
        out_specs=(
            P("row", ("dp", "col")),
            P("row", ("dp", "col")),
            P("row", "col"),
            P("row", "col"),
            P("row", "col"),
            P("col"),
            P("col"),
            P("col", "row"),
            P("row"),
            P("row"),
            P("row"),
            P("row", "col"),
            P("col"),
            P("col", "row"),
            P("row"),
            P("row"),
            P("row"),
        ),
        check_vma=False,
    )
```

```python
import math

import jax
import jax.numpy as jnp
from jax import lax
from jax.experimental import pallas as pl
from jax.experimental.pallas import tpu as pltpu
from jax.sharding import PartitionSpec as P

HEADS = 12
HEAD = 64


EPS = 1e-05


def gather_over_col(values):
    return lax.all_gather(values, "col", axis=0, tiled=True)


def gather_over_row(values):
    return lax.all_gather(values, "row", axis=0, tiled=True)


def contract(left, weight, flipped):
    if flipped:
        return lax.dot_general(
            left, weight, (((1,), (1,)), ((), ())), preferred_element_type=jnp.float32
        )
    return jnp.dot(left, weight, preferred_element_type=jnp.float32)


def product_rows(gathered, weight, flipped):
    return contract(gathered, weight, flipped)


def heads_in(values):
    return lax.all_to_all(values, "col", split_axis=0, concat_axis=1, tiled=True)


def heads_out(values):
    return lax.all_to_all(values, "col", split_axis=1, concat_axis=0, tiled=True)


def sum_over_row(gathered, block, flipped):
    return lax.psum_scatter(
        product_rows(gathered, block, flipped), "row", scatter_dimension=0, tiled=True
    )


def sum_over_col(gathered, block, flipped):
    return lax.psum_scatter(
        product_rows(gathered, block, flipped), "col", scatter_dimension=0, tiled=True
    )


def row_totals(values):
    return lax.psum(values, "row")


def layer_norm(resid, gain, shift):
    feature_count = resid.shape[1] * lax.axis_size("row")
    centre = row_totals((jnp.sum(resid, 1, keepdims=True),))[0] / feature_count
    deviate = resid - centre
    spread = row_totals((jnp.sum(deviate * deviate, 1, keepdims=True),))[0] / feature_count
    scaling = lax.rsqrt(spread + EPS)
    normed = deviate * scaling
    return (normed * gain + shift, normed, scaling)


def norm_backward(upstream, normed, scaling, gain):
    feature_count = upstream.shape[1] * lax.axis_size("row")
    scaled_grad = upstream * gain
    first_sum, second_sum = row_totals(
        (jnp.sum(scaled_grad, 1, keepdims=True), jnp.sum(scaled_grad * normed, 1, keepdims=True))
    )
    return scaling * (
        scaled_grad - first_sum / feature_count - normed * (second_sum / feature_count)
    )


def gelu_tanh(values):
    return jax.nn.gelu(values, approximate=True)


def column_sums(values):
    return jnp.sum(values, 0, dtype=jnp.float32)


def head_scores(query_split, key_split, same_doc):
    scores = jnp.einsum("qhd,khd->hqk", query_split, key_split, preferred_element_type=jnp.float32)
    scores = scores * (1.0 / math.sqrt(HEAD))
    return jnp.where(same_doc[None], scores, -1000000000.0)


def body(
    tokens,
    segment_ids,
    query_weight,
    key_weight,
    value_weight,
    query_bias,
    value_bias,
    out_weight,
    out_bias,
    attn_gain,
    attn_shift,
    up_weight,
    up_bias,
    down_weight,
    down_bias,
    ffn_gain,
    ffn_shift,
    cotangent,
):
    token_major = tokens.T
    head_cols = query_weight.shape[1]
    score_scale = 1.0 / math.sqrt(HEAD)
    joined_weight = jnp.concatenate([query_weight, key_weight, value_weight], 1)
    token_rows = gather_over_col(token_major)
    joined = sum_over_row(token_rows, joined_weight, False)
    query_block = (joined[:, :head_cols] + query_bias).astype(jnp.bfloat16)
    key_block = joined[:, head_cols : 2 * head_cols].astype(jnp.bfloat16)
    value_block = (joined[:, 2 * head_cols :] + value_bias).astype(jnp.bfloat16)
    query_heads = heads_in(query_block)
    key_heads, value_heads = (
        lax.all_gather(key_block, "col", axis=1, tiled=True),
        lax.all_gather(value_block, "col", axis=1, tiled=True),
    )
    query_count = query_heads.shape[0]
    key_count = key_heads.shape[0]
    sequence_ids = segment_ids[0]
    query_ids = lax.dynamic_slice_in_dim(
        sequence_ids, lax.axis_index("col") * query_count, query_count, 0
    )
    same_doc = query_ids[:, None] == sequence_ids[None, :]
    query_split = query_heads.reshape(query_count, HEADS, HEAD)
    key_split = key_heads.reshape(key_count, HEADS, HEAD)
    value_split = value_heads.reshape(key_count, HEADS, HEAD)
    scores = head_scores(query_split, key_split, same_doc)
    highest = jnp.max(scores, -1, keepdims=True)
    exponent = jnp.exp(scores - highest)
    totals = jnp.sum(exponent, -1, keepdims=True)
    log_totals = highest + jnp.log(totals)
    attn_probs = (exponent / totals).astype(jnp.bfloat16)
    attended = jnp.einsum(
        "hqk,khd->qhd", attn_probs, value_split, preferred_element_type=jnp.float32
    )
    attended = attended.reshape(query_count, -1).astype(jnp.bfloat16)
    attended_block = heads_out(attended)
    attended_rows = gather_over_row(attended_block)
    projected = sum_over_col(attended_rows, out_weight, False) + out_bias
    hidden, hidden_normed, hidden_scaling = layer_norm(
        token_major.astype(jnp.float32) + projected, attn_gain, attn_shift
    )
    hidden_low = hidden.astype(jnp.bfloat16)
    hidden_rows = gather_over_col(hidden_low)
    pre_act = sum_over_row(hidden_rows, up_weight, False) + up_bias
    activated, gelu_pull = jax.vjp(gelu_tanh, pre_act)
    act_block = activated.astype(jnp.bfloat16)
    act_rows = gather_over_row(act_block)
    down_out = sum_over_col(act_rows, down_weight, False) + down_bias
    output, out_normed, out_scaling = layer_norm(hidden + down_out, ffn_gain, ffn_shift)
    upstream = cotangent.T.astype(jnp.float32)
    ffn_gain_grad = jnp.sum(upstream * out_normed, 0)
    ffn_shift_grad = jnp.sum(upstream, 0)
    resid_grad = norm_backward(upstream, out_normed, out_scaling, ffn_gain)
    down_grad_rows = gather_over_col(resid_grad.astype(jnp.bfloat16))
    down_weight_grad = jnp.einsum(
        "tf,td->fd", act_rows, down_grad_rows, preferred_element_type=jnp.float32
    )
    down_bias_grad = column_sums(down_grad_rows)
    act_grad = sum_over_row(down_grad_rows, down_weight, True)
    pre_grad = gelu_pull(act_grad)[0].astype(jnp.bfloat16)
    pre_grad_rows = gather_over_row(pre_grad)
    up_weight_grad = jnp.einsum(
        "td,tf->df", hidden_rows, pre_grad_rows, preferred_element_type=jnp.float32
    )
    up_bias_grad = column_sums(pre_grad_rows)
    hidden_grad = sum_over_col(pre_grad_rows, up_weight, True) + resid_grad
    attn_gain_grad = jnp.sum(hidden_grad * hidden_normed, 0)
    attn_shift_grad = jnp.sum(hidden_grad, 0)
    first_grad = norm_backward(hidden_grad, hidden_normed, hidden_scaling, attn_gain)
    proj_grad_rows = gather_over_col(first_grad.astype(jnp.bfloat16))
    out_weight_grad = jnp.einsum(
        "tc,td->cd", attended_rows, proj_grad_rows, preferred_element_type=jnp.float32
    )
    out_bias_grad = column_sums(proj_grad_rows)
    attended_grad = heads_in(sum_over_row(proj_grad_rows, out_weight, True).astype(jnp.bfloat16))
    scores = head_scores(query_split, key_split, same_doc)
    attn_exact = jnp.exp(scores - log_totals)
    grad_split = attended_grad.reshape(query_count, HEADS, HEAD)
    prob_grad = jnp.einsum(
        "qhd,khd->hqk", grad_split, value_split, preferred_element_type=jnp.float32
    )
    score_grad = attn_exact * (prob_grad - jnp.sum(prob_grad * attn_exact, -1, keepdims=True))
    score_grad = score_grad.astype(jnp.bfloat16)
    query_grad = (
        jnp.einsum("hqk,khd->qhd", score_grad, key_split, preferred_element_type=jnp.float32)
        * score_scale
    )
    query_grad = query_grad.reshape(query_count, -1).astype(jnp.bfloat16)
    key_grad = (
        jnp.einsum("hqk,qhd->khd", score_grad, query_split, preferred_element_type=jnp.float32)
        * score_scale
    )
    key_grad = key_grad.reshape(key_count, -1)
    value_grad = jnp.einsum(
        "hqk,qhd->khd",
        attn_exact.astype(jnp.bfloat16),
        grad_split,
        preferred_element_type=jnp.float32,
    ).reshape(key_count, -1)
    key_sum, value_sum = (
        lax.psum_scatter(
            key_grad.astype(jnp.bfloat16), "col", scatter_dimension=1, tiled=True
        ).astype(jnp.float32),
        lax.psum_scatter(
            value_grad.astype(jnp.bfloat16), "col", scatter_dimension=1, tiled=True
        ).astype(jnp.float32),
    )
    joined_grad = jnp.concatenate(
        [heads_out(query_grad), key_sum.astype(jnp.bfloat16), value_sum.astype(jnp.bfloat16)], 1
    )
    joined_rows = gather_over_row(joined_grad)
    joined_weight_grad = jnp.einsum(
        "td,tf->df", token_rows, joined_rows, preferred_element_type=jnp.float32
    )
    query_bias_grad = column_sums(joined_rows[:, :head_cols])
    value_bias_grad = column_sums(joined_rows[:, 2 * head_cols :])
    tokens_grad = sum_over_col(joined_rows, joined_weight, True) + first_grad
    summed = lax.psum(
        (
            joined_weight_grad,
            query_bias_grad,
            value_bias_grad,
            out_weight_grad,
            out_bias_grad,
            up_weight_grad,
            up_bias_grad,
            down_weight_grad,
            down_bias_grad,
        ),
        "dp",
    )
    norm_sums = lax.psum(
        (attn_gain_grad, attn_shift_grad, ffn_gain_grad, ffn_shift_grad), ("dp", "col")
    )
    return (
        output.T.astype(jnp.bfloat16),
        tokens_grad.T,
        summed[0][:, :head_cols],
        summed[0][:, head_cols : 2 * head_cols],
        summed[0][:, 2 * head_cols :],
        summed[1],
        summed[2],
        summed[3],
        summed[4],
        norm_sums[0],
        norm_sums[1],
        summed[5],
        summed[6],
        summed[7],
        summed[8],
        norm_sums[2],
        norm_sums[3],
    )


MESH_ID = pl.DeviceIdType.MESH
BF = jnp.bfloat16
F32 = jnp.float32
GRID = {"dp": 4, "row": 4, "col": 2}
SEQ = 256
WIDE = 768
HALF = 128
PART = 64
ROWS = 192
CHUNK = 384
CHUNKS = 12
SEMS = 256
ORDER = (0, 3, 1, 2)


def small_grid(mesh):
    return dict(mesh.shape) == GRID


def mm(a, b):
    return jnp.dot(a, b, preferred_element_type=F32)


def mm_nt(a, b):
    return lax.dot_general(a, b, (((1,), (1,)), ((), ())), preferred_element_type=F32)


def loop(count, step):
    def wrapped(i, carry):
        step(i)
        return carry

    lax.fori_loop(0, count, wrapped, 0)


def row_mean(values):
    return jnp.sum(values, axis=1, keepdims=True) * (1.0 / WIDE)


def fold(values):
    return jnp.sum(values.reshape(values.shape[0] // 8, 8, values.shape[1]), axis=0)


def layer_kernel(
    ids,
    tok,
    cot,
    qw,
    kw,
    vw,
    ow,
    uw,
    dw,
    qb,
    vb,
    ub,
    ob,
    ag,
    ash,
    db,
    fgn,
    fsh,
    q_out,
    k_out,
    v_out,
    o_out,
    u_out,
    d_out,
    res_out,
    tg_out,
    bias_out,
    norm_out,
    own_vec,
    upb,
    W,
    G,
    R1,
    R2,
    RZ,
    fin,
    xin,
    cin,
    xs,
    xr,
    RX,
    vg,
    vec,
    VA,
    VB,
    VC,
    VD,
    VZ,
    xf,
    cf,
    neq,
    q,
    k,
    v,
    qT,
    kT,
    P,
    at,
    hid,
    n1,
    s1,
    hb,
    hT,
    act,
    dact,
    outf,
    r2g,
    dg,
    dgT,
    pg,
    fg,
    fgT,
    pgT,
    prg,
    dA,
    dAT,
    dT,
    tcross,
    ccross,
    tgp,
    tgr,
    osend,
    obuf,
    tsend,
    tbuf,
    send,
    recv,
):
    dp = lax.axis_index("dp")
    z = lax.axis_index("row")
    x = lax.axis_index("col")
    core = lax.rem(dp, 2)
    y = lax.div(dp, 2)
    mate = dp + 1 - 2 * core
    far = lax.rem(dp + 2, 4)
    matefar = lax.rem(mate + 2, 4)
    other = 1 - x
    counts = {"s": 0, "r": 0}
    pending = []

    def new(kind, n=1):
        base = counts[kind]
        counts[kind] = base + n
        assert counts[kind] <= SEMS
        return base

    def push(src, dst, ssem, rsem, **where):
        return pltpu.make_async_remote_copy(
            src_ref=src,
            dst_ref=dst,
            send_sem=send.at[ssem],
            recv_sem=recv.at[rsem],
            device_id=where,
            device_id_type=MESH_ID,
        )

    def start(pred, make):
        if pred is None:
            make().start()
        else:

            @pl.when(pred)
            def _():
                make().start()

        pending.append((pred, make))

    def arrived(dst, rsem, **where):
        push(dst, dst, 0, rsem, **where).wait_recv()

    def rows(b):
        return pl.ds(pl.multiple_of(b * ROWS, ROWS), ROWS)

    bar = pltpu.get_barrier_semaphore()
    for j in range(4):
        for h in range(2):

            @pl.when((z != j) | (x != h))
            def _(j=j, h=h):
                pl.semaphore_signal(bar, inc=1, device_id={"row": j, "col": h}, device_id_type=MESH_ID)

    pl.semaphore_signal(bar, inc=1, device_id={"dp": mate}, device_id_type=MESH_ID)
    pl.semaphore_signal(bar, inc=1, device_id={"dp": far}, device_id_type=MESH_ID)

    lsem = new("s", CHUNKS)
    mine = rows(z)

    def local_parts():
        parts = []
        for j, ref in enumerate((qw, kw, vw, ow)):
            parts.append((ref, W.at[j, mine]))
        for i in range(4):
            parts.append((uw.at[:, i * CHUNK : (i + 1) * CHUNK], W.at[4 + i, mine]))
        for i in range(4):
            parts.append((dw.at[:, i * CHUNK : (i + 1) * CHUNK], W.at[8 + i, mine]))
        return [pltpu.make_async_copy(a, b, send.at[lsem + n]) for n, (a, b) in enumerate(parts)]

    locals_ = local_parts()
    for c in locals_:
        c.start()
    own_vec[...] = jnp.zeros_like(own_vec)
    for n, ref in enumerate((ob, ag, ash, db, fgn, fsh)):
        own_vec[n : n + 1, 0:ROWS] = ref[...].reshape(1, ROWS)
    own_vec[...] = pltpu.roll(own_vec[...], z * ROWS, 1)
    vg[z] = own_vec[...]
    for i in range(4):
        upb[i] = ub[i * CHUNK : (i + 1) * CHUNK].reshape(1, CHUNK)
    seg = jnp.broadcast_to(ids[...].astype(F32), (SEQ, SEQ))
    neq[...] = jnp.abs(seg - seg.T)
    pl.semaphore_wait(bar, 9)

    def spread(ref, landing, cross):
        xs_, xr_, ssem, rsem = new("s", 2), new("r", 2), new("s", 8), new("r", 4)

        def half(s, h):
            return ref.at[:, pl.ds(pl.multiple_of(s * SEQ + h * HALF, HALF), HALF)]

        def out(j, src, mine_):
            n = ssem + j + (0 if mine_ else 4)
            here = (x == j // 2) if mine_ else (x != j // 2)
            start(here & (z != j), lambda: push(src, landing.at[x, mine], n, rsem + z, row=j))

            @pl.when(here & (z == j))
            def _():
                pltpu.make_async_copy(src, landing.at[x, mine], recv.at[rsem + z]).start()

        def begin():
            for s in range(2):
                start(None, lambda s=s: push(half(s, other), cross.at[s], xs_ + s, xr_ + s, col=other))
            for j in range(4):
                out(j, half(j % 2, x), True)

        def relay():
            for s in range(2):
                arrived(cross.at[s], xr_ + s, col=other)
            for j in range(4):
                out(j, cross.at[j % 2], False)

        def collect():
            for b in range(4):
                dst = landing.at[x, rows(b)]

                @pl.when(z == b)
                def _(dst=dst, b=b):
                    pltpu.make_async_copy(cross.at[0], dst, recv.at[rsem + b]).wait()

                @pl.when(z != b)
                def _(dst=dst, b=b):
                    arrived(dst, rsem + b, row=b)

        return begin, relay, collect

    def swap(landing):
        ssem, rsem = new("s"), new("r")
        start(None, lambda: push(landing.at[x], landing.at[x], ssem, rsem, col=other))

        def collect():
            arrived(landing.at[other], rsem, col=other)

        return collect

    def share_vec():
        ssem, rsem = new("s", 3), new("r", 4)
        for o in range(1, 4):
            to = lax.rem(z + o, 4)
            start(None, lambda o=o, to=to: push(own_vec, vg.at[z], ssem + o - 1, rsem + z, row=to))

        def collect():
            for o in range(1, 4):
                b = lax.rem(z + o, 4)
                arrived(vg.at[b], rsem + b, row=b)
            vec[...] = vg[0] + vg[1] + vg[2] + vg[3]

        return collect

    def gather(g):
        zs, ys, cs = new("s", 5), new("s", 4), new("s", 8)
        zr, yr, cr = new("r", 4), new("r", 4), new("r", 8)
        own, ychunk = 4 * g + dp, 4 * g + far

        def block(chunk, b):
            return W.at[chunk, rows(b)]

        def along(n, b, to, pred):
            start(pred, lambda: push(block(own, b), block(own, b), zs + n, zr + b, row=to))

        def first():
            along(0, z, z + 1, (z < 3) if g == 0 else (z < 2))
            along(1, z, z - 1, (z > 0) if g == 0 else (z > 1))

        def second():
            along(2, z, z + 2, z < 2)
            along(3, z, z - 2, z > 1)

        def late():
            along(0, z, z + 1, z == 2)
            along(1, z, z - 1, z == 1)

        def take(b, pred):
            @pl.when(pred)
            def _():
                arrived(block(own, b), zr + b, row=b)

            start(pred, lambda: push(block(own, b), block(own, b), ys + b, yr + b, dp=far))
            start(pred, lambda: push(block(own, b), block(own, b), cs + b, cr + b, dp=mate))

        def hop1(ends=None):
            if ends is not False:
                take(1, z == 0)
                take(2, z == 3)
            if ends is not True:
                for b in range(4):
                    take(b, ((z == b - 1) | (z == b + 1)) & ((z == 1) | (z == 2)))

        def hop2():
            for b, at_ in ((0, 2), (3, 1)):

                @pl.when(z == at_)
                def _(b=b):
                    arrived(block(own, b), zr + b, row=b)

                along(4, b, 3 - b, z == at_)
                start(z == at_, lambda b=b: push(block(own, b), block(own, b), ys + b, yr + b, dp=far))
                start(z == at_, lambda b=b: push(block(own, b), block(own, b), cs + b, cr + b, dp=mate))
            if g < 2:
                gathers[g + 1][1]()

        def hop2_ends():
            take(2, z == 0)
            take(1, z == 3)

        def hop3():
            take(3, z == 0)
            take(0, z == 3)

        def across():
            for b in range(4):
                there = z != b

                @pl.when(there)
                def _(b=b):
                    arrived(block(ychunk, b), yr + b, dp=far)

                start(
                    there,
                    lambda b=b: push(block(ychunk, b), block(ychunk, b), cs + 4 + b, cr + 4 + b, dp=mate),
                )

        def finish():
            for b in range(4):

                @pl.when(z != b)
                def _(b=b):
                    arrived(block(4 * g + mate, b), cr + b, dp=mate)
                    arrived(block(4 * g + matefar, b), cr + 4 + b, dp=mate)

        return (first, second), late, hop1, hop2, hop3, across, finish, hop2_ends

    def exchange(n):
        ssem, rsem = new("s", 4), new("r", 4)

        def quarter(ref, i):
            return ref.at[n, pl.ds(pl.multiple_of(i * PART, PART), PART)]

        def put(h, value):
            xs[n, h * HALF : (h + 1) * HALF, :] = value.astype(BF)
            for i in (2 * h, 2 * h + 1):
                start(
                    None,
                    lambda i=i: push(quarter(xs, i), quarter(xr, i), ssem + i, rsem + i, col=other),
                )

        def get(i):
            arrived(quarter(xr, i), rsem + i, col=other)

        return put, get

    def both(n, r):
        return xs[n, r, :].astype(F32) + xr[n, r, :].astype(F32)

    def by_quarter(get, step, carry):
        def quarter(i, carry):
            get(i)
            return lax.fori_loop(0, 2, lambda j, c: step(2 * i + j, c), carry)

        return lax.fori_loop(0, 4, quarter, carry)

    def reduce(g):
        rx = new("r")
        s1_, s2_, sz, sy, sc = new("s", 2), new("s", 4), new("s", 4), new("s"), new("s", 2)
        r1, r2, rz, ry, rc = new("r", 2), new("r", 4), new("r", 4), new("r"), new("r", 2)
        own, ychunk = 4 * g + dp, 4 * g + far

        def to_core(j):
            src = G.at[4 * g + 2 * j + 1 - core]
            start(None, lambda: push(src, R1.at[g, j], s1_ + j, r1 + j, dp=mate))

        def add(chunk, extra, base, count):
            def step(i):
                at_ = pl.ds(pl.multiple_of(base + i * 64, 64), 64)
                G[chunk, at_, :] = (G[chunk, at_, :].astype(F32) + extra[at_, :].astype(F32)).astype(BF)

            loop(count // 64, step)

        def piece(ref, b):
            return ref.at[pl.ds(b * ROWS, ROWS)]

        def to_y():
            arrived(R1.at[g, 1 - y], r1 + 1 - y, dp=mate)
            for b in ORDER:
                add(ychunk, R1.at[g, 1 - y], b * ROWS, ROWS)
                start(
                    None,
                    lambda b=b: push(piece(G.at[ychunk], b), piece(R2.at[g], b), s2_ + b, r2 + b, dp=far),
                )
            arrived(R1.at[g, y], r1 + y, dp=mate)
            add(own, R1.at[g, y], 0, WIDE)

        def send(b, pred):
            start(pred, lambda: push(piece(G.at[own], b), RZ.at[g, z], sz + b, rz + z, row=b))

        def take(b):
            arrived(piece(R2.at[g], b), r2 + b, dp=far)
            add(own, R2.at[g], b * ROWS, ROWS)
            if b in (1, 2):
                send(b, z != b)
            else:
                send(b, z == (1 if b == 0 else 2))
                start(
                    z == 3 - b,
                    lambda: push(piece(G.at[own], b), RX.at[g], sz + b, rx, row=2 if b == 0 else 1),
                )

        def relay(b):
            here = z == (2 if b == 0 else 1)

            @pl.when(here)
            def _():
                arrived(RX.at[g], rx, row=3 - b)

                def step(i):
                    at_ = pl.ds(pl.multiple_of(b * ROWS + i * 64, 64), 64)
                    from_ = pl.ds(pl.multiple_of(i * 64, 64), 64)
                    G[own, at_, :] = (G[own, at_, :].astype(F32) + RX[g, from_, :].astype(F32)).astype(BF)

                loop(ROWS // 64, step)

            send(b, here)

        def settle():
            for b in range(4):
                if b in (0, 3):

                    @pl.when(z == 3 - b)
                    def _(b=b):
                        RZ[g, b] = jnp.zeros((ROWS, CHUNK), BF)

                there = (z != b) & (z != 3 - b) if b in (0, 3) else z != b

                @pl.when(there)
                def _(b=b):
                    arrived(RZ.at[g, b], rz + b, row=b)

            RZ[g, z] = G[own, mine, :]

            def step(i):
                at_ = pl.ds(pl.multiple_of(i * 32, 32), 32)
                part = [RZ[g, b, at_, :].astype(F32) for b in range(4)]
                fin[own, at_, :] = ((part[0] + part[1]) + (part[2] + part[3])).astype(BF)

            loop(ROWS // 32, step)
            start(None, lambda: push(fin.at[own], fin.at[own], sy, ry, dp=far))
            start(None, lambda: push(fin.at[own], fin.at[own], sc, rc, dp=mate))

        def across():
            arrived(fin.at[ychunk], ry, dp=far)
            start(None, lambda: push(fin.at[ychunk], fin.at[ychunk], sc + 1, rc + 1, dp=mate))

        def finish():
            arrived(fin.at[4 * g + mate], rc, dp=mate)
            arrived(fin.at[4 * g + matefar], rc + 1, dp=mate)

        return to_core, to_y, take, settle, across, finish, relay

    def deliver(sent, landed, out):
        ssem, rsem = new("s", 4), new("r", 4)
        slot = 2 * lax.rem(z, 2) + x
        home = lax.div(z, 2) == x
        for b in range(4):
            self_ = home & (z == b)
            start(
                jnp.logical_not(self_),
                lambda b=b: push(
                    sent.at[rows(b)], landed.at[slot], ssem + b, rsem + slot, row=b, col=lax.div(z, 2)
                ),
            )

            @pl.when(self_)
            def _(b=b):
                pltpu.make_async_copy(sent.at[rows(b)], landed.at[slot], recv.at[rsem + slot]).start()

        def collect():
            osem = new("s", 4)
            copies = []
            for n in range(4):
                s, h = n // 2, n % 2
                local = (2 * x + s == z) & (h == x)

                @pl.when(local)
                def _(n=n):
                    pltpu.make_async_copy(sent.at[rows(z)], landed.at[n], recv.at[rsem + n]).wait()

                @pl.when(jnp.logical_not(local))
                def _(n=n):
                    arrived(landed.at[n], rsem + n, col=other)

                copies.append(
                    pltpu.make_async_copy(
                        landed.at[n], out.at[:, n * HALF : (n + 1) * HALF], send.at[osem + n]
                    )
                )
                copies[-1].start()
            return copies

        return collect

    tok_out, tok_relay, tok_in = spread(tok, xin, tcross)
    tok_out()
    gathers = [gather(g) for g in range(3)]
    for c in locals_:
        c.wait()
    gathers[0][0][0]()
    tok_relay()
    gathers[0][0][1]()
    vec_in = share_vec()
    for g in range(1, 3):
        gathers[g][0][0]()
        gathers[g][0][1]()
    cot_out, cot_relay, cot_in = spread(cot, cin, ccross)
    gathers[0][2]()
    gathers[0][3]()
    gathers[0][7]()
    tok_in()
    tok_swap = swap(xin)
    gathers[0][4]()
    gathers[1][3]()
    gathers[1][2](True)
    vec_in()
    tok_swap()
    for h in range(2):
        xf[h * HALF : (h + 1) * HALF, :] = xin[h].astype(F32).T
    gathers[0][5]()
    gathers[0][6]()

    xb = xf[...].astype(BF)
    for j, (dst, bias) in enumerate(((q, qb), (k, None), (v, vb))):
        r = mm(xb, W[j])
        if bias is not None:
            r = r + bias[...].reshape(1, CHUNK)
        for p in range(3):
            dst[p] = r[:, p * HALF : (p + 1) * HALF].astype(BF)

    lane = lax.broadcasted_iota(jnp.int32, (SEQ, HALF), 1) < HEAD
    scale = 1.0 / math.sqrt(HEAD)

    def only(values, hh):
        keep = lane if hh == 0 else jnp.logical_not(lane)
        return jnp.where(keep, values.astype(F32), 0.0).astype(BF)

    def attend(p):
        qv, kv, vv = q[p], k[p], v[p]
        outs = []
        for hh in range(2):
            s = mm_nt(only(qv, hh), kv) * scale
            s = jnp.where(neq[...] == 0.0, s, -1000000000.0)
            e = jnp.exp(s - jnp.max(s, axis=1, keepdims=True))
            pr = e / jnp.sum(e, axis=1, keepdims=True)
            P[2 * p + hh] = pr
            outs.append(mm(pr.astype(BF), vv))
        at[p] = jnp.where(lane, outs[0], outs[1]).astype(BF)

    gathers[1][2](False)
    gathers[1][7]()
    loop(3, attend)
    gathers[2][3]()
    cot_out()
    gathers[1][4]()

    put0, get0 = exchange(0)
    att = jnp.concatenate([at[0], at[1], at[2]], axis=1)
    for h in range(2):
        put0(h, mm_nt(att[h * HALF : (h + 1) * HALF, :], W[3]))
    gathers[2][2](True)
    cot_relay()
    for p in range(3):
        qT[p] = q[p].astype(F32).T.astype(BF)
        kT[p] = k[p].astype(F32).T.astype(BF)
    gathers[1][5]()
    gathers[2][2](False)
    def norm1(i, carry):
        r = pl.ds(pl.multiple_of(i * 32, 32), 32)
        resid = xf[r, :] + (both(0, r) + vec[0:1, :])
        d = resid - row_mean(resid)
        s = lax.rsqrt(row_mean(d * d) + EPS)
        n = d * s
        h = n * vec[1:2, :] + vec[2:3, :]
        n1[r, :] = n
        s1[r, :] = jnp.broadcast_to(s, (32, HALF))
        hid[r, :] = h
        hb[r, :] = h.astype(BF)
        return carry

    gathers[2][7]()
    gathers[2][4]()
    by_quarter(get0, norm1, 0)
    gathers[1][6]()

    hv = hb[...]
    c0 = math.sqrt(2.0 / math.pi)

    def up_step(i):
        u = mm(hv, W[4 + i]) + upb[i]
        u2 = u * u
        t = jnp.tanh(c0 * (u + 0.044715 * (u2 * u)))
        half = 0.5 * (1.0 + t)
        act[i] = (u * half).astype(BF)
        dact[i] = half + (0.5 * u) * (1.0 - t * t) * (c0 * (1.0 + (3 * 0.044715) * u2))

    loop(4, up_step)
    cot_in()
    cot_swap = swap(cin)
    gathers[2][5]()
    hT[...] = hid[...].T.astype(BF)
    gathers[2][6]()
    put1, get1 = exchange(1)
    for h in range(2):
        half = slice(h * HALF, (h + 1) * HALF)
        acc = mm_nt(act[0, half, :], W[8])
        for i in range(1, 4):
            acc = acc + mm_nt(act[i, half, :], W[8 + i])
        put1(h, acc)
    cot_swap()
    for h in range(2):
        cf[h * HALF : (h + 1) * HALF, :] = cin[h].astype(F32).T

    VA[...] = jnp.zeros_like(VA)

    def norm2(i, carry):
        gain_sum, shift_sum, bias_sum = carry
        r = pl.ds(pl.multiple_of(i * 32, 32), 32)
        resid = hid[r, :] + (both(1, r) + vec[3:4, :])
        d = resid - row_mean(resid)
        s = lax.rsqrt(row_mean(d * d) + EPS)
        n = d * s
        outf[r, :] = n * vec[4:5, :] + vec[5:6, :]
        up = cf[r, :]
        e = up * vec[4:5, :]
        grad = s * (e - row_mean(e) - n * row_mean(e * n))
        low = grad.astype(BF)
        r2g[r, :] = grad
        dg[r, :] = low
        return gain_sum + fold(up * n), shift_sum + fold(up), bias_sum + fold(low.astype(F32))

    zero = jnp.zeros((8, WIDE), F32)
    sums = by_quarter(get1, norm2, (zero, zero, zero))

    def total(values):
        return jnp.sum(values, axis=0, keepdims=True)

    VA[7:8, :] = total(sums[0])
    VA[8:9, :] = total(sums[1])
    VA[6:7, :] = total(sums[2])
    dgT[...] = r2g[...].T.astype(BF)
    reduces = [reduce(g) for g in range(3)]

    def outer(dst, left, right):
        def step(b):
            r = pl.ds(pl.multiple_of(b * SEQ, SEQ), SEQ)
            G[dst, r, :] = mm(left[r, :], right).astype(BF)

        loop(3, step)

    def products(g, left, rights):
        for to in (1 - core, core):
            for j in (1 - y, y):
                i = 2 * j + to
                outer(4 * g + i, left, rights[i])
                if to is not core:
                    reduces[g][0](j)

    products(2, dgT, act)
    reduces[2][1]()

    ones = jnp.ones((8, SEQ), BF)
    dgv = dg[...]

    def pre_step(i):
        low = (mm(dgv, W[8 + i]) * dact[i]).astype(BF)
        prg[i] = low

    loop(4, pre_step)
    put2, get2 = exchange(2)
    for h in range(2):
        half = slice(h * HALF, (h + 1) * HALF)
        acc = mm_nt(prg[0, half, :], W[4])
        for i in range(1, 4):
            acc = acc + mm_nt(prg[i, half, :], W[4 + i])
        put2(h, acc)
    for i in range(4):
        VA[1 + i // 2 : 2 + i // 2, (i % 2) * CHUNK : (i % 2 + 1) * CHUNK] = mm(ones, prg[i])[0:1, :]
    products(1, hT, prg)
    reduces[2][2](ORDER[0])

    mine_tokens = pl.ds(pl.multiple_of(x * HALF, HALF), HALF)
    osend[...] = outf[mine_tokens, :].T.astype(BF)
    out_in = deliver(osend, obuf, res_out)
    reduces[2][2](ORDER[1])
    reduces[1][1]()

    def norm1_back(i, carry):
        gain_sum, shift_sum, bias_sum = carry
        r = pl.ds(pl.multiple_of(i * 32, 32), 32)
        up = r2g[r, :] + both(2, r)
        n = n1[r, :]
        s = s1[r, :][:, 0:1]
        e = up * vec[1:2, :]
        grad = s * (e - row_mean(e) - n * row_mean(e * n))
        low = grad.astype(BF)
        fg[r, :] = grad
        pg[r, :] = low
        return gain_sum + fold(up * n), shift_sum + fold(up), bias_sum + fold(low.astype(F32))

    sums = by_quarter(get2, norm1_back, (zero, zero, zero))
    VA[4:5, :] = total(sums[0])
    VA[5:6, :] = total(sums[1])
    VA[3:4, :] = total(sums[2])
    for h in range(2):
        t = fg[h * HALF : (h + 1) * HALF, :].T
        fgT[h] = t
        pgT[:, h * HALF : (h + 1) * HALF] = t.astype(BF)

    reduces[2][2](ORDER[2])
    reduces[2][6](ORDER[0])
    reduces[2][2](ORDER[3])
    r = mm(pg[...], W[3])
    for p in range(3):
        part = r[:, p * HALF : (p + 1) * HALF].astype(BF)
        dA[p] = part
        dAT[p] = part.astype(F32).T.astype(BF)
    outer(3, pgT, att)

    top = lax.broadcasted_iota(jnp.int32, (HALF, SEQ), 0) < HEAD

    def attend_back(p):
        dAv, vv = dA[p], v[p]
        dq, dk, dv = [], [], []
        for hh in range(2):
            pr = P[2 * p + hh]
            pgrad = mm_nt(only(dAv, hh), vv)
            ds = (pr * (pgrad - jnp.sum(pgrad * pr, axis=1, keepdims=True))).astype(BF)
            dq.append(mm_nt(kT[p], ds))
            dk.append(mm(qT[p], ds))
            dv.append(mm(dAT[p], pr.astype(BF)))
        dT[0, p] = (jnp.where(top, dq[0], dq[1]) * scale).astype(BF)
        dT[1, p] = (jnp.where(top, dk[0], dk[1]) * scale).astype(BF)
        dT[2, p] = jnp.where(top, dv[0], dv[1]).astype(BF)

    loop(3, attend_back)
    reduces[2][6](ORDER[1])
    reduces[1][2](ORDER[0])

    for j in range(3):
        t = dT[j].reshape(CHUNK, SEQ)
        if j != 1:
            at_ = 0 if j == 0 else CHUNK
            VA[0:1, at_ : at_ + CHUNK] = mm_nt(ones, t)[0:1, :]

        def step(b, t=t, j=j):
            r = pl.ds(pl.multiple_of(b * SEQ, SEQ), SEQ)
            left = jnp.concatenate([xin[0, r, :], xin[1, r, :]], axis=1)
            G[j, r, :] = mm_nt(left, t).astype(BF)

        loop(3, step)
    vs, vr = new("s", 5), new("r", 6)
    start(None, lambda: push(VA, VB, vs, vr, dp=mate))
    reduces[0][0](1 - y)
    reduces[0][0](y)

    def back_step(b):
        r = pl.ds(pl.multiple_of(b * SEQ, SEQ), SEQ)
        acc = mm(W[0, r, :], dT[0].reshape(CHUNK, SEQ))
        acc = acc + mm(W[1, r, :], dT[1].reshape(CHUNK, SEQ))
        acc = acc + mm(W[2, r, :], dT[2].reshape(CHUNK, SEQ))
        tgp[0, r, :] = acc[:, :HALF].astype(BF)
        tgp[1, r, :] = acc[:, HALF:].astype(BF)

    loop(3, back_step)
    ts, tr = new("s"), new("r")
    start(None, lambda: push(tgp.at[other], tgr, ts, tr, col=other))
    reduces[1][2](ORDER[1])
    arrived(VB, vr, dp=mate)
    VD[...] = VA[...] + VB[...]
    start(None, lambda: push(VD, VC, vs + 1, vr + 1, dp=far))
    reduces[0][1]()
    reduces[1][2](ORDER[2])
    reduces[1][6](ORDER[0])
    reduces[1][2](ORDER[3])
    reduces[1][6](ORDER[1])
    arrived(tgr, tr, col=other)
    tsend[...] = (tgp[x].astype(F32) + tgr[...].astype(F32) + fgT[x]).astype(BF)
    tg_in = deliver(tsend, tbuf, tg_out)
    reduces[2][3]()
    arrived(VC, vr + 1, dp=far)
    VZ[z] = VD[...] + VC[...]
    for o in range(1, 4):
        to = lax.rem(z + o, 4)
        start(None, lambda o=o, to=to: push(VZ.at[z], VZ.at[z], vs + 1 + o, vr + 2 + z, row=to))
    reduces[0][2](ORDER[0])
    reduces[0][2](ORDER[1])
    reduces[0][2](ORDER[2])
    reduces[0][6](ORDER[0])
    reduces[0][2](ORDER[3])
    reduces[0][6](ORDER[1])
    reduces[1][3]()
    reduces[2][4]()
    reduces[1][4]()
    reduces[2][5]()
    reduces[0][3]()
    reduces[1][5]()
    copies = []
    fsem = new("s", CHUNKS)

    def flush(g):
        for i in range(4):
            if g == 0:
                dst = (q_out, k_out, v_out, o_out)[i]
            else:
                dst = (u_out, d_out)[g - 1].at[:, i * CHUNK : (i + 1) * CHUNK]
            c = pltpu.make_async_copy(fin.at[4 * g + i], dst, send.at[fsem + 4 * g + i])
            c.start()
            copies.append(c)

    flush(2)
    flush(1)
    for o in range(1, 4):
        b = lax.rem(z + o, 4)
        arrived(VZ.at[b], vr + 2 + b, row=b)
    sums = VZ[0] + VZ[1] + VZ[2] + VZ[3]
    bias_out[...] = sums[0:8, :]
    norm_out[...] = pltpu.roll(sums, WIDE - z * ROWS, 1)[:, 0:SEQ]
    copies += out_in()
    copies += tg_in()
    reduces[0][4]()
    reduces[0][5]()
    flush(0)
    for pred, make in pending:
        if pred is None:
            make().wait_send()
        else:

            @pl.when(pred)
            def _(make=make):
                make().wait_send()

    for c in copies:
        c.wait()


WIDTHS = (CHUNK,) * 4 + (4 * CHUNK,) * 2 + (2 * SEQ,)


def widen_kernel(*refs):
    count = len(WIDTHS)
    ins, passed, bias, norm = refs[:count], refs[count], refs[count + 1], refs[count + 2]
    refs = refs[count + 3 :]
    outs, passed_out, vectors = refs[:count], refs[count], refs[count + 1 : count + 10]
    refs = refs[count + 10 :]
    low, wide, held, sem_in, sem_out = refs[:count], refs[count : 2 * count], *refs[2 * count :]
    order = (4, 5, 6, 0, 1, 2, 3)
    reads = {n: pltpu.make_async_copy(ins[n], low[n], sem_in.at[n]) for n in order}
    through = pltpu.make_async_copy(passed, held, sem_in.at[count])
    for n in order:
        reads[n].start()
    through.start()
    vectors[0][...] = bias[0, 0:CHUNK]
    vectors[1][...] = bias[0, CHUNK:WIDE]
    for i in range(2):
        vectors[2][i * WIDE : (i + 1) * WIDE] = bias[1 + i, :]
    for n in range(6):
        vectors[3 + n][...] = norm[3 + n, 0:ROWS]
    writes = []
    for n in order:
        reads[n].wait()

        def step(i, n=n):
            r = pl.ds(pl.multiple_of(i * 32, 32), 32)
            wide[n][r, :] = low[n][r, :].astype(F32)

        loop(ROWS // 32, step)
        writes.append(pltpu.make_async_copy(wide[n], outs[n], sem_out.at[n]))
        writes[-1].start()
    through.wait()
    writes.append(pltpu.make_async_copy(held, passed_out, sem_out.at[count]))
    writes[-1].start()
    for c in writes:
        c.wait()


def fused_body(
    tokens,
    segment_ids,
    query_weight,
    key_weight,
    value_weight,
    query_bias,
    value_bias,
    out_weight,
    out_bias,
    attn_gain,
    attn_shift,
    up_weight,
    up_bias,
    down_weight,
    down_bias,
    ffn_gain,
    ffn_shift,
    cotangent,
):
    hbm = pl.BlockSpec(memory_space=pl.ANY)
    vmem = pl.BlockSpec(memory_space=pltpu.VMEM)
    gq, gk, gv, go, gu, gd, out, tgrad, bias, norm = pl.pallas_call(
        layer_kernel,
        out_shape=(
            *[jax.ShapeDtypeStruct((ROWS, CHUNK), BF)] * 4,
            *[jax.ShapeDtypeStruct((ROWS, 4 * CHUNK), BF)] * 2,
            *[jax.ShapeDtypeStruct((ROWS, 2 * SEQ), BF)] * 2,
            jax.ShapeDtypeStruct((8, WIDE), F32),
            jax.ShapeDtypeStruct((16, SEQ), F32),
        ),
        in_specs=[vmem] + [hbm] * 8 + [vmem] * 9,
        out_specs=(hbm,) * 8 + (vmem, vmem),
        scratch_shapes=[
            pltpu.VMEM((8, WIDE), F32),
            pltpu.VMEM((4, 1, CHUNK), F32),
            pltpu.VMEM((CHUNKS, WIDE, CHUNK), BF),
            pltpu.VMEM((CHUNKS, WIDE, CHUNK), BF),
            pltpu.VMEM((3, 2, WIDE, CHUNK), BF),
            pltpu.VMEM((3, WIDE, CHUNK), BF),
            pltpu.VMEM((3, 4, ROWS, CHUNK), BF),
            pltpu.VMEM((CHUNKS, ROWS, CHUNK), BF),
            pltpu.VMEM((2, WIDE, HALF), BF),
            pltpu.VMEM((2, WIDE, HALF), BF),
            pltpu.VMEM((3, SEQ, WIDE), BF),
            pltpu.VMEM((3, SEQ, WIDE), BF),
            pltpu.VMEM((3, ROWS, CHUNK), BF),
            pltpu.VMEM((4, 8, WIDE), F32),
            pltpu.VMEM((8, WIDE), F32),
            pltpu.VMEM((16, WIDE), F32),
            pltpu.VMEM((16, WIDE), F32),
            pltpu.VMEM((16, WIDE), F32),
            pltpu.VMEM((16, WIDE), F32),
            pltpu.VMEM((4, 16, WIDE), F32),
            pltpu.VMEM((SEQ, WIDE), F32),
            pltpu.VMEM((SEQ, WIDE), F32),
            pltpu.VMEM((SEQ, SEQ), F32),
            pltpu.VMEM((3, SEQ, HALF), BF),
            pltpu.VMEM((3, SEQ, HALF), BF),
            pltpu.VMEM((3, SEQ, HALF), BF),
            pltpu.VMEM((3, HALF, SEQ), BF),
            pltpu.VMEM((3, HALF, SEQ), BF),
            pltpu.VMEM((6, SEQ, SEQ), F32),
            pltpu.VMEM((3, SEQ, HALF), BF),
            pltpu.VMEM((SEQ, WIDE), F32),
            pltpu.VMEM((SEQ, WIDE), F32),
            pltpu.VMEM((SEQ, HALF), F32),
            pltpu.VMEM((SEQ, WIDE), BF),
            pltpu.VMEM((WIDE, SEQ), BF),
            pltpu.VMEM((4, SEQ, CHUNK), BF),
            pltpu.VMEM((4, SEQ, CHUNK), F32),
            pltpu.VMEM((SEQ, WIDE), F32),
            pltpu.VMEM((SEQ, WIDE), F32),
            pltpu.VMEM((SEQ, WIDE), BF),
            pltpu.VMEM((WIDE, SEQ), BF),
            pltpu.VMEM((SEQ, WIDE), BF),
            pltpu.VMEM((SEQ, WIDE), F32),
            pltpu.VMEM((2, WIDE, HALF), F32),
            pltpu.VMEM((WIDE, SEQ), BF),
            pltpu.VMEM((4, SEQ, CHUNK), BF),
            pltpu.VMEM((3, SEQ, HALF), BF),
            pltpu.VMEM((3, HALF, SEQ), BF),
            pltpu.VMEM((3, 3, HALF, SEQ), BF),
            pltpu.VMEM((2, ROWS, HALF), BF),
            pltpu.VMEM((2, ROWS, HALF), BF),
            pltpu.VMEM((2, WIDE, HALF), BF),
            pltpu.VMEM((WIDE, HALF), BF),
            pltpu.VMEM((WIDE, HALF), BF),
            pltpu.VMEM((4, ROWS, HALF), BF),
            pltpu.VMEM((WIDE, HALF), BF),
            pltpu.VMEM((4, ROWS, HALF), BF),
            pltpu.SemaphoreType.DMA((SEMS,)),
            pltpu.SemaphoreType.DMA((SEMS,)),
        ],
        compiler_params=pltpu.CompilerParams(
            collective_id=0, has_side_effects=True, vmem_limit_bytes=63 * 1024 * 1024
        ),
    )(
        segment_ids,
        tokens,
        cotangent,
        query_weight,
        key_weight,
        value_weight,
        out_weight.T,
        up_weight,
        down_weight.T,
        query_bias,
        value_bias,
        up_bias,
        out_bias,
        attn_gain,
        attn_shift,
        down_bias,
        ffn_gain,
        ffn_shift,
    )
    count = len(WIDTHS)
    sizes = (CHUNK, CHUNK, 4 * CHUNK) + (ROWS,) * 6
    gq, gk, gv, go, gu, gd, tgrad, out, *vectors = pl.pallas_call(
        widen_kernel,
        out_shape=(
            *[jax.ShapeDtypeStruct((ROWS, w), F32) for w in WIDTHS],
            jax.ShapeDtypeStruct((ROWS, 2 * SEQ), BF),
            *[jax.ShapeDtypeStruct((n,), F32) for n in sizes],
        ),
        in_specs=[hbm] * (count + 1) + [vmem] * 2,
        out_specs=(hbm,) * (count + 1) + (vmem,) * len(sizes),
        scratch_shapes=[
            *[pltpu.VMEM((ROWS, w), BF) for w in WIDTHS],
            *[pltpu.VMEM((ROWS, w), F32) for w in WIDTHS],
            pltpu.VMEM((ROWS, 2 * SEQ), BF),
            pltpu.SemaphoreType.DMA((count + 1,)),
            pltpu.SemaphoreType.DMA((count + 1,)),
        ],
    )(gq, gk, gv, go, gu, gd, tgrad, out, bias, norm)
    return (
        out,
        tgrad,
        gq,
        gk,
        gv,
        vectors[0],
        vectors[1],
        go.T,
        *vectors[3:6],
        gu,
        vectors[2],
        gd.T,
        *vectors[6:9],
    )


def solution(mesh):
    placed = (
        P("row", ("dp", "col")),
        P(("dp", "row"), None),
        P("row", "col"),
        P("row", "col"),
        P("row", "col"),
        P("col"),
        P("col"),
        P("col", "row"),
        P("row"),
        P("row"),
        P("row"),
        P("row", "col"),
        P("col"),
        P("col", "row"),
        P("row"),
        P("row"),
        P("row"),
        P("row", ("dp", "col")),
    )
    return jax.shard_map(
        fused_body if small_grid(mesh) else body,
        mesh=mesh,
        in_specs=placed,
        out_specs=(
            P("row", ("dp", "col")),
            P("row", ("dp", "col")),
            P("row", "col"),
            P("row", "col"),
            P("row", "col"),
            P("col"),
            P("col"),
            P("col", "row"),
            P("row"),
            P("row"),
            P("row"),
            P("row", "col"),
            P("col"),
            P("col", "row"),
            P("row"),
            P("row"),
            P("row"),
        ),
        check_vma=False,
    )
```

```python
import math

import jax
import jax.numpy as jnp
from jax import lax
from jax.experimental import pallas as pl
from jax.experimental.pallas import tpu as pltpu
from jax.sharding import PartitionSpec as P

HEADS = 12
HEAD = 64


EPS = 1e-05


def gather_over_col(values):
    return lax.all_gather(values, "col", axis=0, tiled=True)


def gather_over_row(values):
    return lax.all_gather(values, "row", axis=0, tiled=True)


def contract(left, weight, flipped):
    if flipped:
        return lax.dot_general(
            left, weight, (((1,), (1,)), ((), ())), preferred_element_type=jnp.float32
        )
    return jnp.dot(left, weight, preferred_element_type=jnp.float32)


def product_rows(gathered, weight, flipped):
    return contract(gathered, weight, flipped)


def heads_in(values):
    return lax.all_to_all(values, "col", split_axis=0, concat_axis=1, tiled=True)


def heads_out(values):
    return lax.all_to_all(values, "col", split_axis=1, concat_axis=0, tiled=True)


def sum_over_row(gathered, block, flipped):
    return lax.psum_scatter(
        product_rows(gathered, block, flipped), "row", scatter_dimension=0, tiled=True
    )


def sum_over_col(gathered, block, flipped):
    return lax.psum_scatter(
        product_rows(gathered, block, flipped), "col", scatter_dimension=0, tiled=True
    )


def row_totals(values):
    return lax.psum(values, "row")


def layer_norm(resid, gain, shift):
    feature_count = resid.shape[1] * lax.axis_size("row")
    centre = row_totals((jnp.sum(resid, 1, keepdims=True),))[0] / feature_count
    deviate = resid - centre
    spread = row_totals((jnp.sum(deviate * deviate, 1, keepdims=True),))[0] / feature_count
    scaling = lax.rsqrt(spread + EPS)
    normed = deviate * scaling
    return (normed * gain + shift, normed, scaling)


def norm_backward(upstream, normed, scaling, gain):
    feature_count = upstream.shape[1] * lax.axis_size("row")
    scaled_grad = upstream * gain
    first_sum, second_sum = row_totals(
        (jnp.sum(scaled_grad, 1, keepdims=True), jnp.sum(scaled_grad * normed, 1, keepdims=True))
    )
    return scaling * (
        scaled_grad - first_sum / feature_count - normed * (second_sum / feature_count)
    )


def gelu_tanh(values):
    return jax.nn.gelu(values, approximate=True)


def column_sums(values):
    return jnp.sum(values, 0, dtype=jnp.float32)


def head_scores(query_split, key_split, same_doc):
    scores = jnp.einsum("qhd,khd->hqk", query_split, key_split, preferred_element_type=jnp.float32)
    scores = scores * (1.0 / math.sqrt(HEAD))
    return jnp.where(same_doc[None], scores, -1000000000.0)


def body(
    tokens,
    segment_ids,
    query_weight,
    key_weight,
    value_weight,
    query_bias,
    value_bias,
    out_weight,
    out_bias,
    attn_gain,
    attn_shift,
    up_weight,
    up_bias,
    down_weight,
    down_bias,
    ffn_gain,
    ffn_shift,
    cotangent,
):
    token_major = tokens.T
    head_cols = query_weight.shape[1]
    score_scale = 1.0 / math.sqrt(HEAD)
    joined_weight = jnp.concatenate([query_weight, key_weight, value_weight], 1)
    token_rows = gather_over_col(token_major)
    joined = sum_over_row(token_rows, joined_weight, False)
    query_block = (joined[:, :head_cols] + query_bias).astype(jnp.bfloat16)
    key_block = joined[:, head_cols : 2 * head_cols].astype(jnp.bfloat16)
    value_block = (joined[:, 2 * head_cols :] + value_bias).astype(jnp.bfloat16)
    query_heads = heads_in(query_block)
    key_heads, value_heads = (
        lax.all_gather(key_block, "col", axis=1, tiled=True),
        lax.all_gather(value_block, "col", axis=1, tiled=True),
    )
    query_count = query_heads.shape[0]
    key_count = key_heads.shape[0]
    sequence_ids = segment_ids[0]
    query_ids = lax.dynamic_slice_in_dim(
        sequence_ids, lax.axis_index("col") * query_count, query_count, 0
    )
    same_doc = query_ids[:, None] == sequence_ids[None, :]
    query_split = query_heads.reshape(query_count, HEADS, HEAD)
    key_split = key_heads.reshape(key_count, HEADS, HEAD)
    value_split = value_heads.reshape(key_count, HEADS, HEAD)
    scores = head_scores(query_split, key_split, same_doc)
    highest = jnp.max(scores, -1, keepdims=True)
    exponent = jnp.exp(scores - highest)
    totals = jnp.sum(exponent, -1, keepdims=True)
    log_totals = highest + jnp.log(totals)
    attn_probs = (exponent / totals).astype(jnp.bfloat16)
    attended = jnp.einsum(
        "hqk,khd->qhd", attn_probs, value_split, preferred_element_type=jnp.float32
    )
    attended = attended.reshape(query_count, -1).astype(jnp.bfloat16)
    attended_block = heads_out(attended)
    attended_rows = gather_over_row(attended_block)
    projected = sum_over_col(attended_rows, out_weight, False) + out_bias
    hidden, hidden_normed, hidden_scaling = layer_norm(
        token_major.astype(jnp.float32) + projected, attn_gain, attn_shift
    )
    hidden_low = hidden.astype(jnp.bfloat16)
    hidden_rows = gather_over_col(hidden_low)
    pre_act = sum_over_row(hidden_rows, up_weight, False) + up_bias
    activated, gelu_pull = jax.vjp(gelu_tanh, pre_act)
    act_block = activated.astype(jnp.bfloat16)
    act_rows = gather_over_row(act_block)
    down_out = sum_over_col(act_rows, down_weight, False) + down_bias
    output, out_normed, out_scaling = layer_norm(hidden + down_out, ffn_gain, ffn_shift)
    upstream = cotangent.T.astype(jnp.float32)
    ffn_gain_grad = jnp.sum(upstream * out_normed, 0)
    ffn_shift_grad = jnp.sum(upstream, 0)
    resid_grad = norm_backward(upstream, out_normed, out_scaling, ffn_gain)
    down_grad_rows = gather_over_col(resid_grad.astype(jnp.bfloat16))
    down_weight_grad = jnp.einsum(
        "tf,td->fd", act_rows, down_grad_rows, preferred_element_type=jnp.float32
    )
    down_bias_grad = column_sums(down_grad_rows)
    act_grad = sum_over_row(down_grad_rows, down_weight, True)
    pre_grad = gelu_pull(act_grad)[0].astype(jnp.bfloat16)
    pre_grad_rows = gather_over_row(pre_grad)
    up_weight_grad = jnp.einsum(
        "td,tf->df", hidden_rows, pre_grad_rows, preferred_element_type=jnp.float32
    )
    up_bias_grad = column_sums(pre_grad_rows)
    hidden_grad = sum_over_col(pre_grad_rows, up_weight, True) + resid_grad
    attn_gain_grad = jnp.sum(hidden_grad * hidden_normed, 0)
    attn_shift_grad = jnp.sum(hidden_grad, 0)
    first_grad = norm_backward(hidden_grad, hidden_normed, hidden_scaling, attn_gain)
    proj_grad_rows = gather_over_col(first_grad.astype(jnp.bfloat16))
    out_weight_grad = jnp.einsum(
        "tc,td->cd", attended_rows, proj_grad_rows, preferred_element_type=jnp.float32
    )
    out_bias_grad = column_sums(proj_grad_rows)
    attended_grad = heads_in(sum_over_row(proj_grad_rows, out_weight, True).astype(jnp.bfloat16))
    scores = head_scores(query_split, key_split, same_doc)
    attn_exact = jnp.exp(scores - log_totals)
    grad_split = attended_grad.reshape(query_count, HEADS, HEAD)
    prob_grad = jnp.einsum(
        "qhd,khd->hqk", grad_split, value_split, preferred_element_type=jnp.float32
    )
    score_grad = attn_exact * (prob_grad - jnp.sum(prob_grad * attn_exact, -1, keepdims=True))
    score_grad = score_grad.astype(jnp.bfloat16)
    query_grad = (
        jnp.einsum("hqk,khd->qhd", score_grad, key_split, preferred_element_type=jnp.float32)
        * score_scale
    )
    query_grad = query_grad.reshape(query_count, -1).astype(jnp.bfloat16)
    key_grad = (
        jnp.einsum("hqk,qhd->khd", score_grad, query_split, preferred_element_type=jnp.float32)
        * score_scale
    )
    key_grad = key_grad.reshape(key_count, -1)
    value_grad = jnp.einsum(
        "hqk,qhd->khd",
        attn_exact.astype(jnp.bfloat16),
        grad_split,
        preferred_element_type=jnp.float32,
    ).reshape(key_count, -1)
    key_sum, value_sum = (
        lax.psum_scatter(
            key_grad.astype(jnp.bfloat16), "col", scatter_dimension=1, tiled=True
        ).astype(jnp.float32),
        lax.psum_scatter(
            value_grad.astype(jnp.bfloat16), "col", scatter_dimension=1, tiled=True
        ).astype(jnp.float32),
    )
    joined_grad = jnp.concatenate(
        [heads_out(query_grad), key_sum.astype(jnp.bfloat16), value_sum.astype(jnp.bfloat16)], 1
    )
    joined_rows = gather_over_row(joined_grad)
    joined_weight_grad = jnp.einsum(
        "td,tf->df", token_rows, joined_rows, preferred_element_type=jnp.float32
    )
    query_bias_grad = column_sums(joined_rows[:, :head_cols])
    value_bias_grad = column_sums(joined_rows[:, 2 * head_cols :])
    tokens_grad = sum_over_col(joined_rows, joined_weight, True) + first_grad
    summed = lax.psum(
        (
            joined_weight_grad,
            query_bias_grad,
            value_bias_grad,
            out_weight_grad,
            out_bias_grad,
            up_weight_grad,
            up_bias_grad,
            down_weight_grad,
            down_bias_grad,
        ),
        "dp",
    )
    norm_sums = lax.psum(
        (attn_gain_grad, attn_shift_grad, ffn_gain_grad, ffn_shift_grad), ("dp", "col")
    )
    return (
        output.T.astype(jnp.bfloat16),
        tokens_grad.T,
        summed[0][:, :head_cols],
        summed[0][:, head_cols : 2 * head_cols],
        summed[0][:, 2 * head_cols :],
        summed[1],
        summed[2],
        summed[3],
        summed[4],
        norm_sums[0],
        norm_sums[1],
        summed[5],
        summed[6],
        summed[7],
        summed[8],
        norm_sums[2],
        norm_sums[3],
    )


MESH_ID = pl.DeviceIdType.MESH
BF = jnp.bfloat16
F32 = jnp.float32
GRID = {"dp": 4, "row": 4, "col": 2}
SEQ = 256
WIDE = 768
HALF = 128
PART = 64
ROWS = 192
CHUNK = 384
CHUNKS = 12
SEMS = 256
ORDER = (0, 3, 1, 2)


def small_grid(mesh):
    return dict(mesh.shape) == GRID


def mm(a, b):
    return jnp.dot(a, b, preferred_element_type=F32)


def mm_nt(a, b):
    return lax.dot_general(a, b, (((1,), (1,)), ((), ())), preferred_element_type=F32)


def loop(count, step):
    def wrapped(i, carry):
        step(i)
        return carry

    lax.fori_loop(0, count, wrapped, 0)


def row_mean(values):
    return jnp.sum(values, axis=1, keepdims=True) * (1.0 / WIDE)


def fold(values):
    return jnp.sum(values.reshape(values.shape[0] // 8, 8, values.shape[1]), axis=0)


def layer_kernel(
    ids,
    tok,
    cot,
    qw,
    kw,
    vw,
    ow,
    uw,
    dw,
    qb,
    vb,
    ub,
    ob,
    ag,
    ash,
    db,
    fgn,
    fsh,
    q_out,
    k_out,
    v_out,
    o_out,
    u_out,
    d_out,
    res_out,
    tg_out,
    bias_out,
    norm_out,
    own_vec,
    upb,
    W,
    G,
    R1,
    R2,
    RZ,
    fin,
    xin,
    cin,
    xs,
    xr,
    RX,
    vg,
    vec,
    VA,
    VB,
    VC,
    VD,
    VZ,
    xf,
    cf,
    neq,
    q,
    k,
    v,
    qT,
    kT,
    P,
    at,
    hid,
    n1,
    s1,
    hb,
    hT,
    act,
    dact,
    outf,
    r2g,
    dg,
    dgT,
    pg,
    fg,
    fgT,
    pgT,
    prg,
    dA,
    dAT,
    dT,
    tcross,
    ccross,
    tgp,
    tgr,
    osend,
    obuf,
    tsend,
    tbuf,
    send,
    recv,
):
    dp = lax.axis_index("dp")
    z = lax.axis_index("row")
    x = lax.axis_index("col")
    core = lax.rem(dp, 2)
    y = lax.div(dp, 2)
    mate = dp + 1 - 2 * core
    far = lax.rem(dp + 2, 4)
    matefar = lax.rem(mate + 2, 4)
    other = 1 - x
    counts = {"s": 0, "r": 0}
    pending = []

    def new(kind, n=1):
        base = counts[kind]
        counts[kind] = base + n
        assert counts[kind] <= SEMS
        return base

    def push(src, dst, ssem, rsem, **where):
        return pltpu.make_async_remote_copy(
            src_ref=src,
            dst_ref=dst,
            send_sem=send.at[ssem],
            recv_sem=recv.at[rsem],
            device_id=where,
            device_id_type=MESH_ID,
        )

    def start(pred, make):
        if pred is None:
            make().start()
        else:

            @pl.when(pred)
            def _():
                make().start()

        pending.append((pred, make))

    def arrived(dst, rsem, **where):
        push(dst, dst, 0, rsem, **where).wait_recv()

    def rows(b):
        return pl.ds(pl.multiple_of(b * ROWS, ROWS), ROWS)

    bar = pltpu.get_barrier_semaphore()
    for j in range(4):
        for h in range(2):

            @pl.when((z != j) | (x != h))
            def _(j=j, h=h):
                pl.semaphore_signal(bar, inc=1, device_id={"row": j, "col": h}, device_id_type=MESH_ID)

    pl.semaphore_signal(bar, inc=1, device_id={"dp": mate}, device_id_type=MESH_ID)
    pl.semaphore_signal(bar, inc=1, device_id={"dp": far}, device_id_type=MESH_ID)

    lsem = new("s", CHUNKS)
    mine = rows(z)

    def local_parts():
        parts = []
        for j, ref in enumerate((qw, kw, vw, ow)):
            parts.append((ref, W.at[j, mine]))
        for i in range(4):
            parts.append((uw.at[:, i * CHUNK : (i + 1) * CHUNK], W.at[4 + i, mine]))
        for i in range(4):
            parts.append((dw.at[:, i * CHUNK : (i + 1) * CHUNK], W.at[8 + i, mine]))
        return [pltpu.make_async_copy(a, b, send.at[lsem + n]) for n, (a, b) in enumerate(parts)]

    locals_ = local_parts()
    for c in locals_:
        c.start()
    own_vec[...] = jnp.zeros_like(own_vec)
    for n, ref in enumerate((ob, ag, ash, db, fgn, fsh)):
        own_vec[n : n + 1, 0:ROWS] = ref[...].reshape(1, ROWS)
    own_vec[...] = pltpu.roll(own_vec[...], z * ROWS, 1)
    vg[z] = own_vec[...]
    for i in range(4):
        upb[i] = ub[i * CHUNK : (i + 1) * CHUNK].reshape(1, CHUNK)
    seg = jnp.broadcast_to(ids[...].astype(F32), (SEQ, SEQ))
    neq[...] = jnp.abs(seg - seg.T)
    pl.semaphore_wait(bar, 9)

    def spread(ref, landing, cross):
        xs_, xr_, ssem, rsem = new("s", 2), new("r", 2), new("s", 8), new("r", 4)

        def half(s, h):
            return ref.at[:, pl.ds(pl.multiple_of(s * SEQ + h * HALF, HALF), HALF)]

        def out(j, src, mine_):
            n = ssem + j + (0 if mine_ else 4)
            here = (x == j // 2) if mine_ else (x != j // 2)
            start(here & (z != j), lambda: push(src, landing.at[x, mine], n, rsem + z, row=j))

            @pl.when(here & (z == j))
            def _():
                pltpu.make_async_copy(src, landing.at[x, mine], recv.at[rsem + z]).start()

        def begin():
            for s in range(2):
                start(None, lambda s=s: push(half(s, other), cross.at[s], xs_ + s, xr_ + s, col=other))

        def along():
            for j in range(4):
                out(j, half(j % 2, x), True)

        def relay():
            for s in range(2):
                arrived(cross.at[s], xr_ + s, col=other)
            for j in range(4):
                out(j, cross.at[j % 2], False)

        def collect():
            for b in range(4):
                dst = landing.at[x, rows(b)]

                @pl.when(z == b)
                def _(dst=dst, b=b):
                    pltpu.make_async_copy(cross.at[0], dst, recv.at[rsem + b]).wait()

                @pl.when(z != b)
                def _(dst=dst, b=b):
                    arrived(dst, rsem + b, row=b)

        return begin, along, relay, collect

    def swap(landing):
        ssem, rsem = new("s"), new("r")
        start(None, lambda: push(landing.at[x], landing.at[x], ssem, rsem, col=other))

        def collect():
            arrived(landing.at[other], rsem, col=other)

        return collect

    def share_vec():
        ssem, rsem = new("s", 3), new("r", 4)
        for o in range(1, 4):
            to = lax.rem(z + o, 4)
            start(None, lambda o=o, to=to: push(own_vec, vg.at[z], ssem + o - 1, rsem + z, row=to))

        def collect():
            for o in range(1, 4):
                b = lax.rem(z + o, 4)
                arrived(vg.at[b], rsem + b, row=b)
            vec[...] = vg[0] + vg[1] + vg[2] + vg[3]

        return collect

    def gather(g):
        zs, ys, cs = new("s", 5), new("s", 4), new("s", 8)
        zr, yr, cr = new("r", 4), new("r", 4), new("r", 8)
        own, ychunk = 4 * g + dp, 4 * g + far

        def block(chunk, b):
            return W.at[chunk, rows(b)]

        def along(n, b, to, pred):
            start(pred, lambda: push(block(own, b), block(own, b), zs + n, zr + b, row=to))

        def first():
            along(0, z, z + 1, (z < 3) if g == 0 else (z < 2))
            along(1, z, z - 1, (z > 0) if g == 0 else (z > 1))

        def second():
            along(2, z, z + 2, z < 2)
            along(3, z, z - 2, z > 1)

        def late():
            along(0, z, z + 1, z == 2)
            along(1, z, z - 1, z == 1)

        def take(b, pred):
            @pl.when(pred)
            def _():
                arrived(block(own, b), zr + b, row=b)

            start(pred, lambda: push(block(own, b), block(own, b), ys + b, yr + b, dp=far))
            start(pred, lambda: push(block(own, b), block(own, b), cs + b, cr + b, dp=mate))

        def hop1(ends=None):
            if ends is not False:
                take(1, z == 0)
                take(2, z == 3)
            if ends is not True:
                for b in range(4):
                    take(b, ((z == b - 1) | (z == b + 1)) & ((z == 1) | (z == 2)))

        def hop2():
            for b, at_ in ((0, 2), (3, 1)):

                @pl.when(z == at_)
                def _(b=b):
                    arrived(block(own, b), zr + b, row=b)

                along(4, b, 3 - b, z == at_)
                start(z == at_, lambda b=b: push(block(own, b), block(own, b), ys + b, yr + b, dp=far))
                start(z == at_, lambda b=b: push(block(own, b), block(own, b), cs + b, cr + b, dp=mate))
            if g < 2:
                gathers[g + 1][1]()

        def hop2_ends():
            take(2, z == 0)
            take(1, z == 3)

        def hop3():
            take(3, z == 0)
            take(0, z == 3)

        def across():
            for b in range(4):
                there = z != b

                @pl.when(there)
                def _(b=b):
                    arrived(block(ychunk, b), yr + b, dp=far)

                start(
                    there,
                    lambda b=b: push(block(ychunk, b), block(ychunk, b), cs + 4 + b, cr + 4 + b, dp=mate),
                )

        def finish():
            for b in range(4):

                @pl.when(z != b)
                def _(b=b):
                    arrived(block(4 * g + mate, b), cr + b, dp=mate)
                    arrived(block(4 * g + matefar, b), cr + 4 + b, dp=mate)

        return (first, second), late, hop1, hop2, hop3, across, finish, hop2_ends

    def exchange(n):
        ssem, rsem = new("s", 4), new("r", 4)

        def quarter(ref, i):
            return ref.at[n, pl.ds(pl.multiple_of(i * PART, PART), PART)]

        def put(h, value):
            xs[n, h * HALF : (h + 1) * HALF, :] = value.astype(BF)
            for i in (2 * h, 2 * h + 1):
                start(
                    None,
                    lambda i=i: push(quarter(xs, i), quarter(xr, i), ssem + i, rsem + i, col=other),
                )

        def get(i):
            arrived(quarter(xr, i), rsem + i, col=other)

        return put, get

    def both(n, r):
        return xs[n, r, :].astype(F32) + xr[n, r, :].astype(F32)

    def by_quarter(get, step, carry):
        def quarter(i, carry):
            get(i)
            return lax.fori_loop(0, 2, lambda j, c: step(2 * i + j, c), carry)

        return lax.fori_loop(0, 4, quarter, carry)

    def reduce(g):
        rx = new("r")
        s1_, s2_, sz, sy, sc = new("s", 2), new("s", 4), new("s", 4), new("s"), new("s", 2)
        r1, r2, rz, ry, rc = new("r", 2), new("r", 4), new("r", 4), new("r"), new("r", 2)
        own, ychunk = 4 * g + dp, 4 * g + far

        def to_core(j):
            src = G.at[4 * g + 2 * j + 1 - core]
            start(None, lambda: push(src, R1.at[g, j], s1_ + j, r1 + j, dp=mate))

        def add(chunk, extra, base, count):
            def step(i):
                at_ = pl.ds(pl.multiple_of(base + i * 64, 64), 64)
                G[chunk, at_, :] = (G[chunk, at_, :].astype(F32) + extra[at_, :].astype(F32)).astype(BF)

            loop(count // 64, step)

        def piece(ref, b):
            return ref.at[pl.ds(b * ROWS, ROWS)]

        def to_y():
            arrived(R1.at[g, 1 - y], r1 + 1 - y, dp=mate)
            for b in ORDER:
                add(ychunk, R1.at[g, 1 - y], b * ROWS, ROWS)
                start(
                    None,
                    lambda b=b: push(piece(G.at[ychunk], b), piece(R2.at[g], b), s2_ + b, r2 + b, dp=far),
                )
            arrived(R1.at[g, y], r1 + y, dp=mate)
            add(own, R1.at[g, y], 0, WIDE)

        def send(b, pred):
            start(pred, lambda: push(piece(G.at[own], b), RZ.at[g, z], sz + b, rz + z, row=b))

        def take(b):
            arrived(piece(R2.at[g], b), r2 + b, dp=far)
            add(own, R2.at[g], b * ROWS, ROWS)
            if b in (1, 2):
                send(b, z != b)
            else:
                send(b, z == (1 if b == 0 else 2))
                start(
                    z == 3 - b,
                    lambda: push(piece(G.at[own], b), RX.at[g], sz + b, rx, row=2 if b == 0 else 1),
                )

        def relay(b):
            here = z == (2 if b == 0 else 1)

            @pl.when(here)
            def _():
                arrived(RX.at[g], rx, row=3 - b)

                def step(i):
                    at_ = pl.ds(pl.multiple_of(b * ROWS + i * 64, 64), 64)
                    from_ = pl.ds(pl.multiple_of(i * 64, 64), 64)
                    G[own, at_, :] = (G[own, at_, :].astype(F32) + RX[g, from_, :].astype(F32)).astype(BF)

                loop(ROWS // 64, step)

            send(b, here)

        def settle():
            for b in range(4):
                if b in (0, 3):

                    @pl.when(z == 3 - b)
                    def _(b=b):
                        RZ[g, b] = jnp.zeros((ROWS, CHUNK), BF)

                there = (z != b) & (z != 3 - b) if b in (0, 3) else z != b

                @pl.when(there)
                def _(b=b):
                    arrived(RZ.at[g, b], rz + b, row=b)

            RZ[g, z] = G[own, mine, :]

            def step(i):
                at_ = pl.ds(pl.multiple_of(i * 32, 32), 32)
                part = [RZ[g, b, at_, :].astype(F32) for b in range(4)]
                fin[own, at_, :] = ((part[0] + part[1]) + (part[2] + part[3])).astype(BF)

            loop(ROWS // 32, step)
            start(None, lambda: push(fin.at[own], fin.at[own], sy, ry, dp=far))
            start(None, lambda: push(fin.at[own], fin.at[own], sc, rc, dp=mate))

        def across():
            arrived(fin.at[ychunk], ry, dp=far)
            start(None, lambda: push(fin.at[ychunk], fin.at[ychunk], sc + 1, rc + 1, dp=mate))

        def finish():
            arrived(fin.at[4 * g + mate], rc, dp=mate)
            arrived(fin.at[4 * g + matefar], rc + 1, dp=mate)

        return to_core, to_y, take, settle, across, finish, relay

    def deliver(sent, landed, out):
        ssem, rsem = new("s", 4), new("r", 4)
        slot = 2 * lax.rem(z, 2) + x
        home = lax.div(z, 2) == x
        for b in range(4):
            self_ = home & (z == b)
            start(
                jnp.logical_not(self_),
                lambda b=b: push(
                    sent.at[rows(b)], landed.at[slot], ssem + b, rsem + slot, row=b, col=lax.div(z, 2)
                ),
            )

            @pl.when(self_)
            def _(b=b):
                pltpu.make_async_copy(sent.at[rows(b)], landed.at[slot], recv.at[rsem + slot]).start()

        def collect():
            osem = new("s", 4)
            copies = []
            for n in range(4):
                s, h = n // 2, n % 2
                local = (2 * x + s == z) & (h == x)

                @pl.when(local)
                def _(n=n):
                    pltpu.make_async_copy(sent.at[rows(z)], landed.at[n], recv.at[rsem + n]).wait()

                @pl.when(jnp.logical_not(local))
                def _(n=n):
                    arrived(landed.at[n], rsem + n, col=other)

                copies.append(
                    pltpu.make_async_copy(
                        landed.at[n], out.at[:, n * HALF : (n + 1) * HALF], send.at[osem + n]
                    )
                )
                copies[-1].start()
            return copies

        return collect

    tok_out, tok_along, tok_relay, tok_in = spread(tok, xin, tcross)
    tok_out()
    tok_along()
    gathers = [gather(g) for g in range(3)]
    for c in locals_:
        c.wait()
    gathers[0][0][0]()
    tok_relay()
    gathers[0][0][1]()
    vec_in = share_vec()
    for g in range(1, 3):
        gathers[g][0][0]()
        gathers[g][0][1]()
    cot_out, cot_along, cot_relay, cot_in = spread(cot, cin, ccross)
    gathers[0][2]()
    gathers[0][3]()
    tok_in()
    tok_swap = swap(xin)
    cot_out()
    gathers[0][7]()
    gathers[0][4]()
    gathers[1][3]()
    tok_swap()
    for h in range(2):
        xf[h * HALF : (h + 1) * HALF, :] = xin[h].astype(F32).T
    gathers[0][5]()
    gathers[1][2](True)
    gathers[0][6]()

    xb = xf[...].astype(BF)
    for j, (dst, bias) in enumerate(((q, qb), (k, None), (v, vb))):
        r = mm(xb, W[j])
        if bias is not None:
            r = r + bias[...].reshape(1, CHUNK)
        for p in range(3):
            dst[p] = r[:, p * HALF : (p + 1) * HALF].astype(BF)

    lane = lax.broadcasted_iota(jnp.int32, (SEQ, HALF), 1) < HEAD
    scale = 1.0 / math.sqrt(HEAD)

    def only(values, hh):
        keep = lane if hh == 0 else jnp.logical_not(lane)
        return jnp.where(keep, values.astype(F32), 0.0).astype(BF)

    def attend(p):
        qv, kv, vv = q[p], k[p], v[p]
        outs = []
        for hh in range(2):
            s = mm_nt(only(qv, hh), kv) * scale
            s = jnp.where(neq[...] == 0.0, s, -1000000000.0)
            e = jnp.exp(s - jnp.max(s, axis=1, keepdims=True))
            pr = e / jnp.sum(e, axis=1, keepdims=True)
            P[2 * p + hh] = pr
            outs.append(mm(pr.astype(BF), vv))
        at[p] = jnp.where(lane, outs[0], outs[1]).astype(BF)

    gathers[1][2](False)
    gathers[1][7]()
    loop(3, attend)
    gathers[2][3]()
    gathers[1][4]()

    put0, get0 = exchange(0)
    att = jnp.concatenate([at[0], at[1], at[2]], axis=1)
    for h in range(2):
        put0(h, mm_nt(att[h * HALF : (h + 1) * HALF, :], W[3]))
    gathers[2][2](True)
    cot_along()
    cot_relay()
    for p in range(3):
        qT[p] = q[p].astype(F32).T.astype(BF)
        kT[p] = k[p].astype(F32).T.astype(BF)
    gathers[1][5]()
    gathers[2][2](False)
    def norm1(i, carry):
        r = pl.ds(pl.multiple_of(i * 32, 32), 32)
        resid = xf[r, :] + (both(0, r) + vec[0:1, :])
        d = resid - row_mean(resid)
        s = lax.rsqrt(row_mean(d * d) + EPS)
        n = d * s
        h = n * vec[1:2, :] + vec[2:3, :]
        n1[r, :] = n
        s1[r, :] = jnp.broadcast_to(s, (32, HALF))
        hid[r, :] = h
        hb[r, :] = h.astype(BF)
        return carry

    gathers[2][7]()
    gathers[2][4]()
    vec_in()
    by_quarter(get0, norm1, 0)
    cot_in()
    cot_swap = swap(cin)
    gathers[1][6]()

    hv = hb[...]
    c0 = math.sqrt(2.0 / math.pi)

    def up_step(i):
        u = mm(hv, W[4 + i]) + upb[i]
        u2 = u * u
        t = jnp.tanh(c0 * (u + 0.044715 * (u2 * u)))
        half = 0.5 * (1.0 + t)
        act[i] = (u * half).astype(BF)
        dact[i] = half + (0.5 * u) * (1.0 - t * t) * (c0 * (1.0 + (3 * 0.044715) * u2))

    loop(4, up_step)
    gathers[2][5]()
    hT[...] = hid[...].T.astype(BF)
    gathers[2][6]()
    put1, get1 = exchange(1)
    for h in range(2):
        half = slice(h * HALF, (h + 1) * HALF)
        acc = mm_nt(act[0, half, :], W[8])
        for i in range(1, 4):
            acc = acc + mm_nt(act[i, half, :], W[8 + i])
        put1(h, acc)
    cot_swap()
    for h in range(2):
        cf[h * HALF : (h + 1) * HALF, :] = cin[h].astype(F32).T

    VA[...] = jnp.zeros_like(VA)

    def norm2(i, carry):
        gain_sum, shift_sum, bias_sum = carry
        r = pl.ds(pl.multiple_of(i * 32, 32), 32)
        resid = hid[r, :] + (both(1, r) + vec[3:4, :])
        d = resid - row_mean(resid)
        s = lax.rsqrt(row_mean(d * d) + EPS)
        n = d * s
        outf[r, :] = n * vec[4:5, :] + vec[5:6, :]
        up = cf[r, :]
        e = up * vec[4:5, :]
        grad = s * (e - row_mean(e) - n * row_mean(e * n))
        low = grad.astype(BF)
        r2g[r, :] = grad
        dg[r, :] = low
        return gain_sum + fold(up * n), shift_sum + fold(up), bias_sum + fold(low.astype(F32))

    zero = jnp.zeros((8, WIDE), F32)
    sums = by_quarter(get1, norm2, (zero, zero, zero))

    def total(values):
        return jnp.sum(values, axis=0, keepdims=True)

    VA[7:8, :] = total(sums[0])
    VA[8:9, :] = total(sums[1])
    VA[6:7, :] = total(sums[2])
    dgT[...] = r2g[...].T.astype(BF)
    reduces = [reduce(g) for g in range(3)]

    def outer(dst, left, right):
        def step(b):
            r = pl.ds(pl.multiple_of(b * SEQ, SEQ), SEQ)
            G[dst, r, :] = mm(left[r, :], right).astype(BF)

        loop(3, step)

    def products(g, left, rights):
        for to in (1 - core, core):
            for j in (1 - y, y):
                i = 2 * j + to
                outer(4 * g + i, left, rights[i])
                if to is not core:
                    reduces[g][0](j)

    products(2, dgT, act)
    reduces[2][1]()

    ones = jnp.ones((8, SEQ), BF)
    dgv = dg[...]

    def pre_step(i):
        low = (mm(dgv, W[8 + i]) * dact[i]).astype(BF)
        prg[i] = low

    loop(4, pre_step)
    put2, get2 = exchange(2)
    for h in range(2):
        half = slice(h * HALF, (h + 1) * HALF)
        acc = mm_nt(prg[0, half, :], W[4])
        for i in range(1, 4):
            acc = acc + mm_nt(prg[i, half, :], W[4 + i])
        put2(h, acc)
    for i in range(4):
        VA[1 + i // 2 : 2 + i // 2, (i % 2) * CHUNK : (i % 2 + 1) * CHUNK] = mm(ones, prg[i])[0:1, :]
    products(1, hT, prg)
    reduces[2][2](ORDER[0])

    mine_tokens = pl.ds(pl.multiple_of(x * HALF, HALF), HALF)
    osend[...] = outf[mine_tokens, :].T.astype(BF)
    out_in = deliver(osend, obuf, res_out)
    reduces[2][2](ORDER[1])
    reduces[1][1]()

    def norm1_back(i, carry):
        gain_sum, shift_sum, bias_sum = carry
        r = pl.ds(pl.multiple_of(i * 32, 32), 32)
        up = r2g[r, :] + both(2, r)
        n = n1[r, :]
        s = s1[r, :][:, 0:1]
        e = up * vec[1:2, :]
        grad = s * (e - row_mean(e) - n * row_mean(e * n))
        low = grad.astype(BF)
        fg[r, :] = grad
        pg[r, :] = low
        return gain_sum + fold(up * n), shift_sum + fold(up), bias_sum + fold(low.astype(F32))

    sums = by_quarter(get2, norm1_back, (zero, zero, zero))
    VA[4:5, :] = total(sums[0])
    VA[5:6, :] = total(sums[1])
    VA[3:4, :] = total(sums[2])
    for h in range(2):
        t = fg[h * HALF : (h + 1) * HALF, :].T
        fgT[h] = t
        pgT[:, h * HALF : (h + 1) * HALF] = t.astype(BF)

    reduces[2][2](ORDER[2])
    reduces[2][6](ORDER[0])
    reduces[2][2](ORDER[3])
    r = mm(pg[...], W[3])
    for p in range(3):
        part = r[:, p * HALF : (p + 1) * HALF].astype(BF)
        dA[p] = part
        dAT[p] = part.astype(F32).T.astype(BF)
    outer(3, pgT, att)

    top = lax.broadcasted_iota(jnp.int32, (HALF, SEQ), 0) < HEAD

    def attend_back(p):
        dAv, vv = dA[p], v[p]
        dq, dk, dv = [], [], []
        for hh in range(2):
            pr = P[2 * p + hh]
            pgrad = mm_nt(only(dAv, hh), vv)
            ds = (pr * (pgrad - jnp.sum(pgrad * pr, axis=1, keepdims=True))).astype(BF)
            dq.append(mm_nt(kT[p], ds))
            dk.append(mm(qT[p], ds))
            dv.append(mm(dAT[p], pr.astype(BF)))
        dT[0, p] = (jnp.where(top, dq[0], dq[1]) * scale).astype(BF)
        dT[1, p] = (jnp.where(top, dk[0], dk[1]) * scale).astype(BF)
        dT[2, p] = jnp.where(top, dv[0], dv[1]).astype(BF)

    loop(3, attend_back)
    reduces[2][6](ORDER[1])
    reduces[1][2](ORDER[0])

    for j in range(3):
        t = dT[j].reshape(CHUNK, SEQ)
        if j != 1:
            at_ = 0 if j == 0 else CHUNK
            VA[0:1, at_ : at_ + CHUNK] = mm_nt(ones, t)[0:1, :]

        def step(b, t=t, j=j):
            r = pl.ds(pl.multiple_of(b * SEQ, SEQ), SEQ)
            left = jnp.concatenate([xin[0, r, :], xin[1, r, :]], axis=1)
            G[j, r, :] = mm_nt(left, t).astype(BF)

        loop(3, step)
    vs, vr = new("s", 5), new("r", 6)
    start(None, lambda: push(VA, VB, vs, vr, dp=mate))
    reduces[0][0](1 - y)
    reduces[0][0](y)

    def back_step(b):
        r = pl.ds(pl.multiple_of(b * SEQ, SEQ), SEQ)
        acc = mm(W[0, r, :], dT[0].reshape(CHUNK, SEQ))
        acc = acc + mm(W[1, r, :], dT[1].reshape(CHUNK, SEQ))
        acc = acc + mm(W[2, r, :], dT[2].reshape(CHUNK, SEQ))
        tgp[0, r, :] = acc[:, :HALF].astype(BF)
        tgp[1, r, :] = acc[:, HALF:].astype(BF)

    loop(3, back_step)
    ts, tr = new("s"), new("r")
    start(None, lambda: push(tgp.at[other], tgr, ts, tr, col=other))
    reduces[1][2](ORDER[1])
    arrived(VB, vr, dp=mate)
    VD[...] = VA[...] + VB[...]
    start(None, lambda: push(VD, VC, vs + 1, vr + 1, dp=far))
    reduces[0][1]()
    reduces[1][2](ORDER[2])
    reduces[1][6](ORDER[0])
    reduces[1][2](ORDER[3])
    reduces[1][6](ORDER[1])
    reduces[2][3]()
    reduces[0][2](ORDER[0])
    reduces[0][2](ORDER[1])
    reduces[0][2](ORDER[2])
    reduces[0][6](ORDER[0])
    reduces[0][2](ORDER[3])
    reduces[0][6](ORDER[1])
    arrived(tgr, tr, col=other)
    tsend[...] = (tgp[x].astype(F32) + tgr[...].astype(F32) + fgT[x]).astype(BF)
    tg_in = deliver(tsend, tbuf, tg_out)
    arrived(VC, vr + 1, dp=far)
    VZ[z] = VD[...] + VC[...]
    for o in range(1, 4):
        to = lax.rem(z + o, 4)
        start(None, lambda o=o, to=to: push(VZ.at[z], VZ.at[z], vs + 1 + o, vr + 2 + z, row=to))
    reduces[1][3]()
    reduces[2][4]()
    reduces[1][4]()
    reduces[2][5]()
    reduces[0][3]()
    reduces[1][5]()
    copies = []
    fsem = new("s", CHUNKS)

    def flush(g):
        for i in range(4):
            if g == 0:
                dst = (q_out, k_out, v_out, o_out)[i]
            else:
                dst = (u_out, d_out)[g - 1].at[:, i * CHUNK : (i + 1) * CHUNK]
            c = pltpu.make_async_copy(fin.at[4 * g + i], dst, send.at[fsem + 4 * g + i])
            c.start()
            copies.append(c)

    flush(2)
    flush(1)
    for o in range(1, 4):
        b = lax.rem(z + o, 4)
        arrived(VZ.at[b], vr + 2 + b, row=b)
    sums = VZ[0] + VZ[1] + VZ[2] + VZ[3]
    bias_out[...] = sums[0:8, :]
    norm_out[...] = pltpu.roll(sums, WIDE - z * ROWS, 1)[:, 0:SEQ]
    copies += out_in()
    copies += tg_in()
    reduces[0][4]()
    reduces[0][5]()
    flush(0)
    for pred, make in pending:
        if pred is None:
            make().wait_send()
        else:

            @pl.when(pred)
            def _(make=make):
                make().wait_send()

    for c in copies:
        c.wait()


WIDTHS = (CHUNK,) * 4 + (4 * CHUNK,) * 2 + (2 * SEQ,)


def widen_kernel(*refs):
    count = len(WIDTHS)
    ins, passed, bias, norm = refs[:count], refs[count], refs[count + 1], refs[count + 2]
    refs = refs[count + 3 :]
    outs, passed_out, vectors = refs[:count], refs[count], refs[count + 1 : count + 10]
    refs = refs[count + 10 :]
    low, wide, held, sem_in, sem_out = refs[:count], refs[count : 2 * count], *refs[2 * count :]
    order = (4, 5, 6, 0, 1, 2, 3)
    reads = {n: pltpu.make_async_copy(ins[n], low[n], sem_in.at[n]) for n in order}
    through = pltpu.make_async_copy(passed, held, sem_in.at[count])
    for n in order:
        reads[n].start()
    through.start()
    vectors[0][...] = bias[0, 0:CHUNK]
    vectors[1][...] = bias[0, CHUNK:WIDE]
    for i in range(2):
        vectors[2][i * WIDE : (i + 1) * WIDE] = bias[1 + i, :]
    for n in range(6):
        vectors[3 + n][...] = norm[3 + n, 0:ROWS]
    writes = []
    for n in order:
        reads[n].wait()

        def step(i, n=n):
            r = pl.ds(pl.multiple_of(i * 32, 32), 32)
            wide[n][r, :] = low[n][r, :].astype(F32)

        loop(ROWS // 32, step)
        writes.append(pltpu.make_async_copy(wide[n], outs[n], sem_out.at[n]))
        writes[-1].start()
    through.wait()
    writes.append(pltpu.make_async_copy(held, passed_out, sem_out.at[count]))
    writes[-1].start()
    for c in writes:
        c.wait()


def fused_body(
    tokens,
    segment_ids,
    query_weight,
    key_weight,
    value_weight,
    query_bias,
    value_bias,
    out_weight,
    out_bias,
    attn_gain,
    attn_shift,
    up_weight,
    up_bias,
    down_weight,
    down_bias,
    ffn_gain,
    ffn_shift,
    cotangent,
):
    hbm = pl.BlockSpec(memory_space=pl.ANY)
    vmem = pl.BlockSpec(memory_space=pltpu.VMEM)
    gq, gk, gv, go, gu, gd, out, tgrad, bias, norm = pl.pallas_call(
        layer_kernel,
        out_shape=(
            *[jax.ShapeDtypeStruct((ROWS, CHUNK), BF)] * 4,
            *[jax.ShapeDtypeStruct((ROWS, 4 * CHUNK), BF)] * 2,
            *[jax.ShapeDtypeStruct((ROWS, 2 * SEQ), BF)] * 2,
            jax.ShapeDtypeStruct((8, WIDE), F32),
            jax.ShapeDtypeStruct((16, SEQ), F32),
        ),
        in_specs=[vmem] + [hbm] * 8 + [vmem] * 9,
        out_specs=(hbm,) * 8 + (vmem, vmem),
        scratch_shapes=[
            pltpu.VMEM((8, WIDE), F32),
            pltpu.VMEM((4, 1, CHUNK), F32),
            pltpu.VMEM((CHUNKS, WIDE, CHUNK), BF),
            pltpu.VMEM((CHUNKS, WIDE, CHUNK), BF),
            pltpu.VMEM((3, 2, WIDE, CHUNK), BF),
            pltpu.VMEM((3, WIDE, CHUNK), BF),
            pltpu.VMEM((3, 4, ROWS, CHUNK), BF),
            pltpu.VMEM((CHUNKS, ROWS, CHUNK), BF),
            pltpu.VMEM((2, WIDE, HALF), BF),
            pltpu.VMEM((2, WIDE, HALF), BF),
            pltpu.VMEM((3, SEQ, WIDE), BF),
            pltpu.VMEM((3, SEQ, WIDE), BF),
            pltpu.VMEM((3, ROWS, CHUNK), BF),
            pltpu.VMEM((4, 8, WIDE), F32),
            pltpu.VMEM((8, WIDE), F32),
            pltpu.VMEM((16, WIDE), F32),
            pltpu.VMEM((16, WIDE), F32),
            pltpu.VMEM((16, WIDE), F32),
            pltpu.VMEM((16, WIDE), F32),
            pltpu.VMEM((4, 16, WIDE), F32),
            pltpu.VMEM((SEQ, WIDE), F32),
            pltpu.VMEM((SEQ, WIDE), F32),
            pltpu.VMEM((SEQ, SEQ), F32),
            pltpu.VMEM((3, SEQ, HALF), BF),
            pltpu.VMEM((3, SEQ, HALF), BF),
            pltpu.VMEM((3, SEQ, HALF), BF),
            pltpu.VMEM((3, HALF, SEQ), BF),
            pltpu.VMEM((3, HALF, SEQ), BF),
            pltpu.VMEM((6, SEQ, SEQ), F32),
            pltpu.VMEM((3, SEQ, HALF), BF),
            pltpu.VMEM((SEQ, WIDE), F32),
            pltpu.VMEM((SEQ, WIDE), F32),
            pltpu.VMEM((SEQ, HALF), F32),
            pltpu.VMEM((SEQ, WIDE), BF),
            pltpu.VMEM((WIDE, SEQ), BF),
            pltpu.VMEM((4, SEQ, CHUNK), BF),
            pltpu.VMEM((4, SEQ, CHUNK), F32),
            pltpu.VMEM((SEQ, WIDE), F32),
            pltpu.VMEM((SEQ, WIDE), F32),
            pltpu.VMEM((SEQ, WIDE), BF),
            pltpu.VMEM((WIDE, SEQ), BF),
            pltpu.VMEM((SEQ, WIDE), BF),
            pltpu.VMEM((SEQ, WIDE), F32),
            pltpu.VMEM((2, WIDE, HALF), F32),
            pltpu.VMEM((WIDE, SEQ), BF),
            pltpu.VMEM((4, SEQ, CHUNK), BF),
            pltpu.VMEM((3, SEQ, HALF), BF),
            pltpu.VMEM((3, HALF, SEQ), BF),
            pltpu.VMEM((3, 3, HALF, SEQ), BF),
            pltpu.VMEM((2, ROWS, HALF), BF),
            pltpu.VMEM((2, ROWS, HALF), BF),
            pltpu.VMEM((2, WIDE, HALF), BF),
            pltpu.VMEM((WIDE, HALF), BF),
            pltpu.VMEM((WIDE, HALF), BF),
            pltpu.VMEM((4, ROWS, HALF), BF),
            pltpu.VMEM((WIDE, HALF), BF),
            pltpu.VMEM((4, ROWS, HALF), BF),
            pltpu.SemaphoreType.DMA((SEMS,)),
            pltpu.SemaphoreType.DMA((SEMS,)),
        ],
        compiler_params=pltpu.CompilerParams(
            collective_id=0, has_side_effects=True, vmem_limit_bytes=63 * 1024 * 1024
        ),
    )(
        segment_ids,
        tokens,
        cotangent,
        query_weight,
        key_weight,
        value_weight,
        out_weight.T,
        up_weight,
        down_weight.T,
        query_bias,
        value_bias,
        up_bias,
        out_bias,
        attn_gain,
        attn_shift,
        down_bias,
        ffn_gain,
        ffn_shift,
    )
    count = len(WIDTHS)
    sizes = (CHUNK, CHUNK, 4 * CHUNK) + (ROWS,) * 6
    gq, gk, gv, go, gu, gd, tgrad, out, *vectors = pl.pallas_call(
        widen_kernel,
        out_shape=(
            *[jax.ShapeDtypeStruct((ROWS, w), F32) for w in WIDTHS],
            jax.ShapeDtypeStruct((ROWS, 2 * SEQ), BF),
            *[jax.ShapeDtypeStruct((n,), F32) for n in sizes],
        ),
        in_specs=[hbm] * (count + 1) + [vmem] * 2,
        out_specs=(hbm,) * (count + 1) + (vmem,) * len(sizes),
        scratch_shapes=[
            *[pltpu.VMEM((ROWS, w), BF) for w in WIDTHS],
            *[pltpu.VMEM((ROWS, w), F32) for w in WIDTHS],
            pltpu.VMEM((ROWS, 2 * SEQ), BF),
            pltpu.SemaphoreType.DMA((count + 1,)),
            pltpu.SemaphoreType.DMA((count + 1,)),
        ],
    )(gq, gk, gv, go, gu, gd, tgrad, out, bias, norm)
    return (
        out,
        tgrad,
        gq,
        gk,
        gv,
        vectors[0],
        vectors[1],
        go.T,
        *vectors[3:6],
        gu,
        vectors[2],
        gd.T,
        *vectors[6:9],
    )


def solution(mesh):
    placed = (
        P("row", ("dp", "col")),
        P(("dp", "row"), None),
        P("row", "col"),
        P("row", "col"),
        P("row", "col"),
        P("col"),
        P("col"),
        P("col", "row"),
        P("row"),
        P("row"),
        P("row"),
        P("row", "col"),
        P("col"),
        P("col", "row"),
        P("row"),
        P("row"),
        P("row"),
        P("row", ("dp", "col")),
    )
    return jax.shard_map(
        fused_body if small_grid(mesh) else body,
        mesh=mesh,
        in_specs=placed,
        out_specs=(
            P("row", ("dp", "col")),
            P("row", ("dp", "col")),
            P("row", "col"),
            P("row", "col"),
            P("row", "col"),
            P("col"),
            P("col"),
            P("col", "row"),
            P("row"),
            P("row"),
            P("row"),
            P("row", "col"),
            P("col"),
            P("col", "row"),
            P("row"),
            P("row"),
            P("row"),
        ),
        check_vma=False,
    )
```
